256 devices in a mesh: job: 8 (over y, core), seq: 32 (over z, x).
Axes of the slice: x: 4, y: 4, z: 8, core: 2. Of those that a mesh axis runs over, the one named last changes fastest.
Arguments:
- video: bfloat16 [8, 4096, 3072], P('job', 'seq'), may hold values from -6 to 6
- text_cache: bfloat16 [8, 256, 4096], P('job', 'seq'), may hold values from -6 to 6
- text_count: int32 [8], replicated, may hold values from 129 to 256, as said below
- holder: int32 [8], replicated, may hold values from 0 to 7, each once
- text_splits: int32 [8, 32], replicated, may hold values from 0 to 16, as said below
- mod_shift: float32 [8, 3072], replicated, may hold values from -3 to 3
- mod_scale: float32 [8, 3072], replicated, may hold values from -2 to 2
- mod_gate: float32 [8, 3072], replicated, may hold values from -4 to 4
- text_gain: float32 [4096], replicated, may hold values from 0.25 to 1.75
- refine_w: bfloat16 [4096, 3072], P(None, 'job'), may hold values from -0.09375 to 0.09375
- refine_bias: float32 [3072], P('job'), may hold values from -3 to 3
- w_qkv: bfloat16 [3072, 16, 3, 128], P(None, 'job'), may hold values from -0.109375 to 0.109375
- q_gain: float32 [16, 128], P('job'), may hold values from 0.85 to 9.2
- k_gain: float32 [16, 128], P('job'), may hold values from 0.85 to 9.2
- w_out: bfloat16 [16, 128, 3072], P('job'), may hold values from -0.125 to 0.125
Outputs:
- video_out: bfloat16 [8, 4096, 3072], P('job', 'seq')
- text_out: bfloat16 [8, 512, 3072], P('job', 'seq')
The draws below stay inside these ranges and needn't reach their ends.
Inputs may be any that keep to these rules, and one draw needn't show every extreme that they name: `text_count`: 256 is reached by some job in every draw. `text_splits`: for each job the entries over the 32 shards add up to text_count of that job; some shard holds exactly 16 rows in every draw.
All inputs are finite; a program needn't handle non-finite values.
Results may differ from the reference program's by a relative error of at most 0.012.
The reference program's roundings to bfloat16 on the way count: a program that leaves them out, or rounds other values in their place, can miss the bound.
Values may be sent and summed in bfloat16 or wider, within the bound.
A program may use at most 64 MiB of HBM per device.

```python
import math
import jax
import jax.numpy as jnp
from jax import lax

D = 3072
DT = 4096
HD = 128
HEADS = 16
TXT = 256
VID_DEV = 128
JOBS = 8
SHARDS = 32
VIDEO = 4096
TCAP = 16
N_JOB = 8
N_SEQ = 32


def text_plan(key):
    base_key = jax.random.fold_in(key, 7)
    key_count, key_long, key_caps, key_lead = jax.random.split(base_key, 4)
    counts = jax.random.randint(key_count, (JOBS,), TXT // 2 + 1, TXT + 1)
    longest = jax.random.randint(key_long, (), 0, JOBS)
    counts = jnp.where(jnp.arange(JOBS) == longest, TXT, counts)
    capacity = jax.random.randint(key_caps, (JOBS, SHARDS), TCAP // 2, TCAP + 1)
    leading = jax.random.randint(key_lead, (JOBS,), 0, SHARDS)
    fill_order = (jnp.arange(SHARDS)[None, :] + leading[:, None]) % SHARDS
    ordered = jnp.take_along_axis(capacity, fill_order, axis=1)
    ordered = ordered.at[:, 0].set(TCAP)
    before = jnp.cumsum(ordered, axis=1) - ordered
    filled = jnp.clip(counts[:, None] - before, 0, ordered)
    position = (jnp.arange(SHARDS)[None, :] - leading[:, None]) % SHARDS
    splits = jnp.take_along_axis(filled, position, axis=1)
    return (counts.astype(jnp.int32), splits.astype(jnp.int32))


def draw_text_count(key, part):
    return text_plan(key)[0]


def draw_text_splits(key, part):
    return text_plan(key)[1]


def head_gains(key, salt_value):
    head_key, entry_key = jax.random.split(jax.random.fold_in(key, salt_value))
    lower_end = 1.2
    upper_end = 2.0
    head_level = jnp.exp(jax.random.uniform(head_key, (HEADS, 1), jnp.float32, math.log(lower_end), math.log(upper_end)))
    jitter = 1.0 + 0.15 * jax.random.uniform(entry_key, (HEADS, HD), jnp.float32, -1.0, 1.0)
    return (head_level * jitter).astype(jnp.float32)


def draw_q_gain(key, part):
    return head_gains(key, 11)


def draw_k_gain(key, part):
    return head_gains(key, 13)


def level_of(own_key, shape, shards, low, largest):
    level, own = 1.0, jax.random.fold_in(own_key, 6)
    for dim, blocks in shards:
        draws = jnp.exp(jax.random.uniform(jax.random.fold_in(own, dim), (blocks,), jnp.float32, low / len(shards), largest / len(shards)))
        level = level * jnp.repeat(draws, shape[dim] // blocks).reshape([-1 if axis == dim else 1 for axis in range(len(shape))])
    return level


def scatter_about(rng, extent, deviation, most, cuts=(), kind=jnp.bfloat16):
    loudness = level_of(rng, extent, cuts, -0.22, 0.18) if cuts else 1.0
    values = jax.random.normal(rng, extent, jnp.float32) * deviation * loudness
    return jnp.minimum(jnp.maximum(values, -most), most).astype(kind)


def setup_inputs(seed: int = 0) -> dict:
    seeds = jax.random.split(jax.random.key(seed), 16)
    video = scatter_about(seeds[0], (JOBS, VIDEO, D), 1.0, 6.0, ((0, 8), (1, 32)))
    text_cache = scatter_about(seeds[1], (JOBS, TXT, DT), 1.0, 6.0, ((0, 8), (1, 32)))
    text_count = draw_text_count(jax.random.fold_in(seeds[15], 71), 0)
    holder = jax.random.permutation(seeds[3], JOBS).astype(jnp.int32)
    text_splits = draw_text_splits(jax.random.fold_in(seeds[15], 71), 0)
    mod_shift = scatter_about(seeds[5], (JOBS, D), 0.5, 3.0, (), jnp.float32)
    mod_scale = scatter_about(seeds[6], (JOBS, D), 0.3, 2.0, (), jnp.float32)
    mod_gate = scatter_about(seeds[7], (JOBS, D), 1.0, 4.0, (), jnp.float32)
    text_gain = jnp.clip(1.0 + 0.15 * jax.random.normal(seeds[8], (DT,), jnp.float32), 0.25, 1.75)
    refine_w = scatter_about(seeds[9], (DT, D), DT ** -0.5, 0.09375, ((1, 8),))
    refine_bias = scatter_about(seeds[10], (D,), 0.5, 3.0, ((0, 8),), jnp.float32)
    w_qkv = scatter_about(seeds[11], (D, HEADS, 3, HD), D ** -0.5, 0.109375, ((1, 8),))
    q_gain = draw_q_gain(jax.random.fold_in(seeds[15], 71), 0)
    k_gain = draw_k_gain(jax.random.fold_in(seeds[15], 71), 0)
    w_out = scatter_about(seeds[14], (HEADS, HD, D), (HEADS * HD) ** -0.5, 0.125, ((0, 8),))
    return dict(video=video, text_cache=text_cache, text_count=text_count, holder=holder, text_splits=text_splits, mod_shift=mod_shift, mod_scale=mod_scale, mod_gate=mod_gate, text_gain=text_gain, refine_w=refine_w, refine_bias=refine_bias, w_qkv=w_qkv, q_gain=q_gain, k_gain=k_gain, w_out=w_out)


epsilon = 1e-06

def rms_scale(values, gains):
    mean_square = lax.optimization_barrier(jnp.mean(values * values, axis=-1, keepdims=True))
    return values * lax.rsqrt(mean_square + epsilon) * gains

def modulate(tokens, shift_part, scale_part):
    widened = tokens.astype(jnp.float32)
    centre = lax.optimization_barrier(jnp.mean(widened, axis=-1, keepdims=True))
    spread_sq = lax.optimization_barrier(jnp.mean((widened - centre) ** 2, axis=-1, keepdims=True))
    normed = (widened - centre) * lax.rsqrt(spread_sq + epsilon)
    return (normed * (1.0 + scale_part) + shift_part).astype(jnp.bfloat16)

def refine_rows(raw_text, text_gain, refine_w, refine_bias):
    normed = rms_scale(raw_text.astype(jnp.float32), text_gain).astype(jnp.bfloat16)
    lifted = jnp.dot(normed, refine_w, preferred_element_type=jnp.float32)
    return (lifted + refine_bias).astype(jnp.bfloat16)

def attend(queries, key_rows, values, key_ok):
    scores = jnp.dot(queries, key_rows.T, preferred_element_type=jnp.float32) * HD ** (-0.5)
    scores = jnp.where(key_ok[None, :], scores, -1e+30)
    highest = lax.optimization_barrier(jnp.max(scores, axis=-1, keepdims=True))
    weights = jnp.exp(scores - highest)
    summed = lax.optimization_barrier(jnp.sum(weights, axis=-1, keepdims=True))
    weights = (weights / summed).astype(jnp.bfloat16)
    return jnp.dot(weights, values, preferred_element_type=jnp.float32).astype(jnp.bfloat16)

def reference(video, text_cache, text_count, holder, text_splits, mod_shift, mod_scale, mod_gate, text_gain, refine_w, refine_bias, w_qkv, q_gain, k_gain, w_out):
    row_count = VID_DEV + TCAP
    group_size = HEADS // N_JOB
    offsets = (jnp.cumsum(text_splits, axis=1) - text_splits).astype(jnp.int32)
    slot_ids = jnp.arange(TCAP, dtype=jnp.int32)
    head_weights = jnp.moveaxis(w_qkv, 1, 0)
    video_outs = []
    text_outs = []
    for job_index in range(JOBS):
        raw_text = text_cache[holder[job_index]]
        refined = refine_rows(raw_text, text_gain, refine_w, refine_bias)
        padded = jnp.concatenate([refined, jnp.zeros((TCAP, D), jnp.bfloat16)], axis=0)
        position = (offsets[job_index][:, None] + slot_ids[None, :]).astype(jnp.int32)
        slot_valid = (slot_ids[None, :] < text_splits[job_index][:, None]) & (position < text_count[job_index])
        gathered = padded[position]
        text_rows = jnp.where(slot_valid[:, :, None], gathered, jnp.zeros_like(gathered))
        video_part = video[job_index].reshape(N_SEQ, VID_DEV, D)
        sequence = jnp.concatenate([video_part, text_rows], axis=1).reshape(N_SEQ * row_count, D)
        key_ok = jnp.concatenate([jnp.ones((N_SEQ, VID_DEV), jnp.bool_), slot_valid], axis=1).reshape(-1)
        modded = modulate(sequence, mod_shift[job_index], mod_scale[job_index])

        def one_head(operands):
            head_w, head_q, head_k = operands
            projections = jnp.dot(modded, head_w.reshape(D, 3 * HD), preferred_element_type=jnp.float32).reshape(-1, 3, HD)
            queries = rms_scale(projections[:, 0], head_q).astype(jnp.bfloat16)
            key_rows = rms_scale(projections[:, 1], head_k).astype(jnp.bfloat16)
            values = projections[:, 2].astype(jnp.bfloat16)
            return attend(queries, key_rows, values, key_ok)
        attended = lax.map(one_head, (head_weights, q_gain, k_gain))
        projected = jnp.zeros((N_SEQ * row_count, D), jnp.float32)
        for group_index in range(N_JOB):
            chosen = attended[group_index * group_size:(group_index + 1) * group_size]
            flat_heads = jnp.transpose(chosen, (1, 0, 2)).reshape(-1, group_size * HD)
            group_w = w_out[group_index * group_size:(group_index + 1) * group_size].reshape(group_size * HD, D)
            part_sum = jnp.dot(flat_heads, group_w, preferred_element_type=jnp.float32)
            rounded = lax.optimization_barrier(part_sum.astype(jnp.bfloat16))
            projected = projected + rounded.astype(jnp.float32)
        result = (sequence.astype(jnp.float32) + mod_gate[job_index] * projected).astype(jnp.bfloat16)
        result = result.reshape(N_SEQ, row_count, D)
        video_outs.append(result[:, :VID_DEV].reshape(N_SEQ * VID_DEV, D))
        text_part = result[:, VID_DEV:]
        text_outs.append(jnp.where(slot_valid[:, :, None], text_part, jnp.zeros_like(text_part)).reshape(N_SEQ * TCAP, D))
    return (jnp.stack(video_outs), jnp.stack(text_outs))
```

```python
import functools

import jax
import jax.numpy as jnp
from jax import lax
from jax.experimental import pallas as pl
from jax.experimental.pallas import tpu as pltpu
from jax.sharding import PartitionSpec as P

HD = 128
NY, NC, NZ, NX = 4, 2, 8, 4
N_JOB = NY * NC
N_SEQ = NZ * NX
MESH = pl.DeviceIdType.MESH
epsilon = 1e-06
ANY = pl.BlockSpec(memory_space=pl.ANY)
DMA = pltpu.SemaphoreType.DMA


def rms_scale(values, gains):
    mean_square = jnp.mean(values * values, axis=-1, keepdims=True)
    return values * lax.rsqrt(mean_square + epsilon) * gains


def modulate(tokens, shift_part, scale_part):
    widened = tokens.astype(jnp.float32)
    centre = jnp.mean(widened, axis=-1, keepdims=True)
    spread_sq = jnp.mean((widened - centre) ** 2, axis=-1, keepdims=True)
    normed = (widened - centre) * lax.rsqrt(spread_sq + epsilon)
    return (normed * (1.0 + scale_part) + shift_part).astype(jnp.bfloat16)


def place():
    job = lax.axis_index("job")
    seq = lax.axis_index("seq")
    return job // NC, job % NC, seq // NX, seq % NX


def signal(job, seq):
    pl.semaphore_signal(
        pltpu.get_barrier_semaphore(), inc=1, device_id=(job, seq), device_id_type=MESH
    )


def near():
    y, c, z, x = place()
    seq = z * NX + x
    up = (((y + 1) % NY) * NC + c, seq)
    down = (((y + NY - 1) % NY) * NC + c, seq)
    other = (y * NC + 1 - c, seq)
    return up, down, other


class JobGather:
    def __init__(self, src, dst, buf, send, recv, local, rows, chunks):
        self.src, self.dst, self.buf = src, dst, buf
        self.send, self.recv, self.local = send, recv, local
        self.step, self.chunks = rows // chunks, chunks

    def piece(self, k):
        return pl.ds(pl.multiple_of(k * self.step, self.step), self.step)

    def copy(self, source, block, role, k, device):
        return pltpu.make_async_remote_copy(
            src_ref=source.at[self.piece(k)],
            dst_ref=self.dst.at[block, self.piece(k)],
            send_sem=self.send.at[role, k],
            recv_sem=self.recv.at[role, k],
            device_id=device,
            device_id_type=MESH,
        )

    def block(self, role):
        y, c, _, _ = place()
        return {
            0: ((y + NY - 1) % NY) * NC + c,
            1: ((y + 1) % NY) * NC + c,
            2: ((y + 2) % NY) * NC + c,
            3: y * NC + 1 - c,
            4: ((y + NY - 1) % NY) * NC + 1 - c,
            5: ((y + 1) % NY) * NC + 1 - c,
            6: ((y + 2) % NY) * NC + 1 - c,
        }[role]

    def own(self):
        y, c, _, _ = place()
        return y * NC + c

    def start(self):
        up, down, other = near()
        own = self.own()
        pltpu.make_async_copy(self.src, self.buf, self.local.at[0]).start()

        def go(k, carry):
            self.copy(self.src, own, 0, k, up).start()
            self.copy(self.src, own, 1, k, down).start()
            self.copy(self.src, own, 3, k, other).start()
            return carry

        lax.fori_loop(0, self.chunks, go, 0)
        pltpu.make_async_copy(self.src, self.buf, self.local.at[0]).wait()
        pltpu.make_async_copy(self.buf, self.dst.at[own], self.local.at[1]).start()

    def arrived(self, role, k):
        block = self.block(role)
        self.copy(self.dst.at[block], block, role, k, near()[2]).wait_recv()

    def handon(self, role, k):
        block = self.block(role)
        self.copy(self.dst.at[block], block, role + 4, k, near()[2]).start()

    def middle(self, k):
        y, c, _, _ = place()
        up, down, other = near()
        self.arrived(0, k)

        @pl.when(c == 0)
        def _():
            self.copy(self.dst.at[self.block(0)], self.block(0), 2, k, up).start()

        self.handon(0, k)
        self.arrived(1, k)

        @pl.when(c == 1)
        def _():
            self.copy(self.dst.at[self.block(1)], self.block(1), 2, k, down).start()

        self.handon(1, k)

    def last(self, k):
        self.arrived(2, k)
        self.handon(2, k)

    def finish(self):
        own = self.own()
        other = near()[2]

        def go(k, carry):
            for role in (3, 4, 5, 6):
                self.arrived(role, k)
            for role in range(7):
                self.copy(self.src, own, role, k, other).wait_send()
            return carry

        lax.fori_loop(0, self.chunks, go, 0)
        pltpu.make_async_copy(self.buf, self.dst.at[own], self.local.at[1]).wait()


def gather_scratch(shapes, chunks):
    out = []
    for shape, n in zip(shapes, chunks):
        out += [
            pltpu.VMEM(shape, jnp.bfloat16),
            DMA((7, n)),
            DMA((7, n)),
            DMA((2,)),
        ]
    return out


def gather_kernel(shapes, chunks, *refs):
    n = len(shapes)
    sources, targets, scratch = refs[:n], refs[n : 2 * n], refs[2 * n :]
    for device in near():
        signal(*device)
    pl.semaphore_wait(pltpu.get_barrier_semaphore(), 3)
    gathers = []
    for i in range(n):
        buf, send, recv, local = scratch[4 * i : 4 * i + 4]
        gathers.append(
            JobGather(sources[i], targets[i], buf, send, recv, local, shapes[i][0], chunks[i])
        )
    for one in gathers:
        one.start()
    for one in gathers:
        lax.fori_loop(0, one.chunks, lambda k, carry: (one.middle(k), carry)[1], 0)
        lax.fori_loop(0, one.chunks, lambda k, carry: (one.last(k), carry)[1], 0)
    for one in gathers:
        one.finish()


def gather_job(arrays, chunks, collective_id):
    shapes = [a.shape for a in arrays]
    return pl.pallas_call(
        functools.partial(gather_kernel, shapes, chunks),
        out_shape=[jax.ShapeDtypeStruct((N_JOB, *s), jnp.bfloat16) for s in shapes],
        in_specs=[ANY] * len(arrays),
        out_specs=[ANY] * len(arrays),
        scratch_shapes=gather_scratch(shapes, chunks),
        compiler_params=pltpu.CompilerParams(collective_id=collective_id, has_side_effects=True),
        name=f"gather_job_{collective_id}",
    )(*arrays)


def far_first(n):
    return 4 + ((n + 1) // 2) * (1 - 2 * (n % 2))


W_CHUNKS = 8


def exchange_kernel(
    vid, txt, w_out, rvid, rtxt, w_all, vsend, vrecv, tsend, trecv, buf, wsend, wrecv, wlocal
):
    y, c, z, x = place()
    seq = z * NX + x
    up, down, other = near()
    here = (x // 2 == c).astype(jnp.int32)
    peer_job = y * NC + x // 2

    def greet(n, carry):
        for hl in range(2):
            to = n * NX + 2 * c + hl

            @pl.when(jnp.logical_or(to != seq, here == 0))
            def _():
                signal(peer_job, to)

        return carry

    lax.fori_loop(0, NZ, greet, 0)
    for device in near():
        signal(*device)
    pl.semaphore_wait(pltpu.get_barrier_semaphore(), 19 - here)

    def vrows(shard):
        return rvid.at[:, pl.ds(pl.multiple_of(shard * 128, 128), 128), :]

    def trows(shard):
        return rtxt.at[:, pl.ds(pl.multiple_of(shard * 8, 8), 8), :]

    def pair_of(n, hl):
        zd = (z + far_first(n)) % NZ
        j = (zd + NZ - 2 * y) % NZ
        return 2 * j + hl, zd * NX + 2 * c + hl

    slot = 2 * z + x % 2

    def sends(n, hl):
        pair, to = pair_of(n, hl)
        device = (peer_job, to)
        step = 2 * n + hl
        return to, (
            pltpu.make_async_remote_copy(
                vid.at[pair], vrows(seq), vsend.at[step], vrecv.at[slot], device, MESH
            ),
            pltpu.make_async_remote_copy(
                txt.at[pair], trows(seq), tsend.at[step], trecv.at[slot], device, MESH
            ),
        )

    def locals_(n, hl):
        pair, _ = pair_of(n, hl)
        return (
            pltpu.make_async_copy(vid.at[pair], vrows(seq), vrecv.at[slot]),
            pltpu.make_async_copy(txt.at[pair], trows(seq), trecv.at[slot]),
        )

    def start(n, carry):
        for hl in range(2):
            to, copies = sends(n, hl)
            away = jnp.logical_or(to != seq, here == 0)

            @pl.when(away)
            def _():
                for one in copies:
                    one.start()

            @pl.when(jnp.logical_not(away))
            def _():
                for one in locals_(n, hl):
                    one.start()

        return carry

    lax.fori_loop(0, NZ, start, 0)
    weights = JobGather(w_out, w_all, buf, wsend, wrecv, wlocal, w_out.shape[0], W_CHUNKS)
    weights.start()

    def handed(shard, index, base):
        return (
            pltpu.make_async_remote_copy(
                vrows(shard), vrows(shard), vsend.at[base], vrecv.at[index], other, MESH
            ),
            pltpu.make_async_remote_copy(
                trows(shard), trows(shard), tsend.at[base], trecv.at[index], other, MESH
            ),
        )

    def arrive(n, carry):
        zs = (z + NZ - far_first(n)) % NZ
        for b in range(2):
            shard = zs * NX + 2 * c + b
            index = 2 * zs + b
            for one in handed(shard, index, 0):
                one.wait_recv()
            for one in handed(shard, index + 16, index + 16):
                one.start()
        weights.middle(n)
        return carry

    lax.fori_loop(0, NZ, arrive, 0)
    lax.fori_loop(0, W_CHUNKS, lambda k, carry: (weights.last(k), carry)[1], 0)

    def finish(n, carry):
        for b in range(2):
            shard = n * NX + 2 * (1 - c) + b
            index = 2 * n + b
            for one in handed(shard, index + 16, index + 16):
                one.wait_recv()
            for one in handed(shard, index + 16, index + 16):
                one.wait_send()
        for hl in range(2):
            to, copies = sends(n, hl)

            @pl.when(jnp.logical_or(to != seq, here == 0))
            def _():
                for one in copies:
                    one.wait_send()

        return carry

    lax.fori_loop(0, NZ, finish, 0)
    weights.finish()


def exchange(vid, txt, w_out):
    bf = jnp.bfloat16
    return pl.pallas_call(
        exchange_kernel,
        out_shape=[
            jax.ShapeDtypeStruct((3, N_SEQ * 128, HD), bf),
            jax.ShapeDtypeStruct((5, N_SEQ * 8, HD), bf),
            jax.ShapeDtypeStruct((N_JOB, *w_out.shape), bf),
        ],
        in_specs=[ANY] * 3,
        out_specs=[ANY] * 3,
        scratch_shapes=[DMA((32,)), DMA((32,)), DMA((32,)), DMA((32,))]
        + gather_scratch([w_out.shape], [W_CHUNKS]),
        compiler_params=pltpu.CompilerParams(collective_id=5, has_side_effects=True),
        name="exchange",
    )(vid, txt, w_out)


def attend_kernel(counts, vid, txt, slots, ov, ot, vext, text_out):
    y, c, z, x = place()
    job = (z + NZ - 2 * y) % NZ
    count = counts[job]
    vext[0:4096, 0:HD] = vid[2]
    vext[4096:4352, 0:HD] = txt[2]
    vext[:, HD:] = jnp.ones((4352, HD), jnp.bfloat16)
    factor = (HD**-0.5) * 1.4426950408889634
    contract = (((1,), (1,)), ((), ()))

    def block(q):
        sv = lax.dot_general(q, vid[1], contract, preferred_element_type=jnp.float32)
        st = lax.dot_general(q, txt[1], contract, preferred_element_type=jnp.float32)
        st = jnp.where(lax.broadcasted_iota(jnp.int32, st.shape, 1) < count, st, -1e30)
        top = jnp.maximum(
            jnp.max(sv, axis=-1, keepdims=True), jnp.max(st, axis=-1, keepdims=True)
        )
        pv = jnp.exp2((sv - top) * factor).astype(jnp.bfloat16)
        pt = jnp.exp2((st - top) * factor).astype(jnp.bfloat16)
        both = jnp.dot(pv, vext[0:4096], preferred_element_type=jnp.float32)
        both += jnp.dot(pt, vext[4096:4352], preferred_element_type=jnp.float32)
        return (both[:, 0:HD] / both[:, HD:]).astype(jnp.bfloat16)

    def step(n, carry):
        q = vid[0, pl.ds(pl.multiple_of(n * 512 + c * 256, 256), 256), :]
        ov[pl.ds(2 * n, 2)] = block(q).reshape(2, 128, HD)
        return carry

    lax.fori_loop(0, NZ, step, 0)
    text_out[...] = block(txt[0])
    pick = (slots[...] == lax.broadcasted_iota(jnp.int32, (256, 256), 1)).astype(jnp.bfloat16)
    for part in range(3):
        rows = text_out[...] if part == 0 else txt[part + 2]
        moved = jnp.dot(pick, rows, preferred_element_type=jnp.float32).astype(jnp.bfloat16)
        ot[:, part] = moved.reshape(16, 16, HD)


def attend(counts, vid, txt, slots):
    bf = jnp.bfloat16
    vm = pl.BlockSpec(memory_space=pltpu.VMEM)
    return pl.pallas_call(
        attend_kernel,
        out_shape=[
            jax.ShapeDtypeStruct((16, 128, HD), bf),
            jax.ShapeDtypeStruct((16, 3, 16, HD), bf),
        ],
        in_specs=[pl.BlockSpec(memory_space=pltpu.SMEM), vm, vm, vm],
        out_specs=[vm, vm],
        scratch_shapes=[pltpu.VMEM((4352, 2 * HD), bf), pltpu.VMEM((256, HD), bf)],
        compiler_params=pltpu.CompilerParams(vmem_limit_bytes=48 << 20),
        name="attend",
    )(counts, vid, txt, slots)


def back_kernel(ov, ot, rv, rt, vsend, vrecv, tsend, trecv):
    y, c, z, x = place()
    seq = z * NX + x
    mine = y * NC + c
    job = (z + NZ - 2 * y) % NZ
    head = 4 * y + x

    def greet(n, carry):
        for b in range(NX):
            from_job = n * NC + x // 2
            from_seq = ((mine + 2 * n) % NZ) * NX + b

            @pl.when(jnp.logical_or(from_job != mine, from_seq != seq))
            def _():
                signal(from_job, from_seq)

        return carry

    lax.fori_loop(0, NY, greet, 0)
    inside = jnp.logical_and(job == mine, x // 2 == c).astype(jnp.int32)
    pl.semaphore_wait(pltpu.get_barrier_semaphore(), 16 - inside)

    def copies(n, b):
        zd = (z + far_first(n)) % NZ
        part = 2 * zd + b
        to = zd * NX + 2 * c + b
        away = jnp.logical_or(to != seq, job != mine)
        remote = (
            pltpu.make_async_remote_copy(
                ov.at[part], rv.at[head], vsend.at[part], vrecv.at[head], (job, to), MESH
            ),
            pltpu.make_async_remote_copy(
                ot.at[part], rt.at[head], tsend.at[part], trecv.at[head], (job, to), MESH
            ),
        )
        local = (
            pltpu.make_async_copy(ov.at[part], rv.at[head], vrecv.at[head]),
            pltpu.make_async_copy(ot.at[part], rt.at[head], trecv.at[head]),
        )
        return away, remote, local

    def start(n, carry):
        for b in range(2):
            away, remote, local = copies(n, b)

            @pl.when(away)
            def _():
                for one in remote:
                    one.start()

            @pl.when(jnp.logical_not(away))
            def _():
                for one in local:
                    one.start()

        return carry

    lax.fori_loop(0, NZ, start, 0)

    def finish(n, carry):
        pltpu.make_async_copy(ov.at[n], rv.at[n], vrecv.at[n]).wait()
        pltpu.make_async_copy(ot.at[n], rt.at[n], trecv.at[n]).wait()
        return carry

    lax.fori_loop(0, 16, finish, 0)

    def sent(n, carry):
        for b in range(2):
            away, remote, _ = copies(n, b)

            @pl.when(away)
            def _():
                for one in remote:
                    one.wait_send()

        return carry

    lax.fori_loop(0, NZ, sent, 0)


def send_back(ov, ot):
    bf = jnp.bfloat16
    return pl.pallas_call(
        back_kernel,
        out_shape=[
            jax.ShapeDtypeStruct((16, 128, HD), bf),
            jax.ShapeDtypeStruct((16, 3, 16, HD), bf),
        ],
        in_specs=[ANY] * 2,
        out_specs=[ANY] * 2,
        scratch_shapes=[DMA((16,)), DMA((16,)), DMA((16,)), DMA((16,))],
        compiler_params=pltpu.CompilerParams(collective_id=6, has_side_effects=True),
        name="send_back",
    )(ov, ot)


def body(
    video,
    text_cache,
    text_count,
    holder,
    text_splits,
    mod_shift,
    mod_scale,
    mod_gate,
    text_gain,
    refine_w,
    refine_bias,
    w_qkv,
    q_gain,
    k_gain,
    w_out,
):
    y, c, z, x = place()
    my_job = lax.axis_index("job")
    my_shard = lax.axis_index("seq")
    bf = jnp.bfloat16
    own_video = video[0]
    (raw,) = gather_job([text_cache[0]], [1], 1)
    chosen = jnp.take(raw, holder, axis=0).reshape(64, -1)
    normed = rms_scale(chosen.astype(jnp.float32), text_gain).astype(bf)
    refined = (
        jnp.dot(normed, refine_w, preferred_element_type=jnp.float32) + refine_bias
    ).astype(bf)
    video_all, refined_all = gather_job([own_video, refined], [4, 1], 2)
    text_full = jnp.transpose(refined_all, (1, 0, 2)).reshape(8, 8, -1)
    rows = jnp.concatenate([video_all, text_full], axis=1)
    modded = modulate(rows, mod_shift[:, None, :], mod_scale[:, None, :])
    projections = jnp.einsum("jrd,dhce->jrhce", modded, w_qkv, preferred_element_type=jnp.float32)
    queries = rms_scale(projections[:, :, :, 0], q_gain).astype(bf)
    keys = rms_scale(projections[:, :, :, 1], k_gain).astype(bf)
    values = projections[:, :, :, 2].astype(bf)
    heads = jnp.stack([queries, keys, values], axis=3)
    heads = jnp.transpose(heads, (0, 2, 3, 1, 4))
    vid = heads[:, :, :, :128].reshape(16, 3, 128, HD)
    carried = jnp.pad(refined.reshape(8, 8, 3, HD), ((0, 0), (0, 0), (0, 1), (0, 0)))
    carried = jnp.transpose(carried.reshape(8, 8, 2, 2, HD), (0, 2, 3, 1, 4))
    txt = jnp.concatenate([heads[:, :, :, 128:], carried], axis=2).reshape(16, 5, 8, HD)
    rvid, rtxt, w_all = exchange(vid, txt, w_out.reshape(2 * HD, -1))

    offsets = jnp.cumsum(text_splits, axis=1) - text_splits
    ids = jnp.arange(16, dtype=jnp.int32)
    where_to = offsets[:, :, None] + ids
    valid = (ids < text_splits[:, :, None]) & (where_to < text_count[:, None, None])
    where_to = jnp.where(valid, where_to, -1).reshape(8, NZ, NC, 2, 16)
    job_here = (z + NZ - 2 * y) % NZ
    slots = lax.dynamic_slice(where_to, (job_here, 0, c, 0, 0), (1, NZ, 1, 2, 16))
    ov, ot = attend(text_count, rvid, rtxt, slots.reshape(256, 1))
    rv, rt = send_back(ov, ot)

    attended = jnp.concatenate([rv, rt[:, 0]], axis=1)
    attended = jnp.transpose(attended, (1, 0, 2)).reshape(144, 2048)
    projected = jnp.dot(attended, w_all.reshape(2048, -1), preferred_element_type=jnp.float32)
    kept = rt[:, 1:].reshape(8, 4, 16, HD)[:, :3]
    kept = jnp.transpose(kept, (2, 0, 1, 3)).reshape(16, -1)
    own_rows = jnp.concatenate([own_video, kept], axis=0).astype(jnp.float32)
    gate = lax.dynamic_index_in_dim(mod_gate, my_job, 0, keepdims=True)
    result = (own_rows + gate * projected).astype(bf)
    ok = lax.dynamic_slice(valid, (my_job, my_shard, 0), (1, 1, 16)).reshape(16, 1)
    text_result = jnp.where(ok, result[128:], jnp.zeros_like(result[128:]))
    return (result[:128][None], text_result[None])


def solution(mesh):
    placed = (
        P("job", "seq", None),
        P("job", "seq", None),
        P(),
        P(),
        P(),
        P(),
        P(),
        P(),
        P(),
        P(None, "job"),
        P("job"),
        P(None, "job", None, None),
        P("job", None),
        P("job", None),
        P("job", None, None),
    )
    return jax.shard_map(
        body,
        mesh=mesh,
        in_specs=placed,
        out_specs=(P("job", "seq", None), P("job", "seq", None)),
        check_vma=False,
    )
```

```python
import functools

import jax
import jax.numpy as jnp
from jax import lax
from jax.experimental import pallas as pl
from jax.experimental.pallas import tpu as pltpu
from jax.sharding import PartitionSpec as P

HD = 128
NY, NC, NZ, NX = 4, 2, 8, 4
N_JOB = NY * NC
N_SEQ = NZ * NX
MESH = pl.DeviceIdType.MESH
epsilon = 1e-06
ANY = pl.BlockSpec(memory_space=pl.ANY)
DMA = pltpu.SemaphoreType.DMA


def rms_scale(values, gains):
    mean_square = jnp.mean(values * values, axis=-1, keepdims=True)
    return values * lax.rsqrt(mean_square + epsilon) * gains


def modulate(tokens, shift_part, scale_part):
    widened = tokens.astype(jnp.float32)
    centre = jnp.mean(widened, axis=-1, keepdims=True)
    spread_sq = jnp.mean((widened - centre) ** 2, axis=-1, keepdims=True)
    normed = (widened - centre) * lax.rsqrt(spread_sq + epsilon)
    return (normed * (1.0 + scale_part) + shift_part).astype(jnp.bfloat16)


def place():
    job = lax.axis_index("job")
    seq = lax.axis_index("seq")
    return job // NC, job % NC, seq // NX, seq % NX


def signal(job, seq):
    pl.semaphore_signal(
        pltpu.get_barrier_semaphore(), inc=1, device_id=(job, seq), device_id_type=MESH
    )


def near():
    y, c, z, x = place()
    seq = z * NX + x
    up = (((y + 1) % NY) * NC + c, seq)
    down = (((y + NY - 1) % NY) * NC + c, seq)
    other = (y * NC + 1 - c, seq)
    return up, down, other


class JobGather:
    def __init__(self, src, dst, buf, send, recv, local, rows, chunks):
        self.src, self.dst, self.buf = src, dst, buf
        self.send, self.recv, self.local = send, recv, local
        self.step, self.chunks = rows // chunks, chunks

    def piece(self, k):
        return pl.ds(pl.multiple_of(k * self.step, self.step), self.step)

    def copy(self, source, block, role, k, device):
        return pltpu.make_async_remote_copy(
            src_ref=source.at[self.piece(k)],
            dst_ref=self.dst.at[block, self.piece(k)],
            send_sem=self.send.at[role, k],
            recv_sem=self.recv.at[role, k],
            device_id=device,
            device_id_type=MESH,
        )

    def block(self, role):
        y, c, _, _ = place()
        return {
            0: ((y + NY - 1) % NY) * NC + c,
            1: ((y + 1) % NY) * NC + c,
            2: ((y + 2) % NY) * NC + c,
            3: y * NC + 1 - c,
            4: ((y + NY - 1) % NY) * NC + 1 - c,
            5: ((y + 1) % NY) * NC + 1 - c,
            6: ((y + 2) % NY) * NC + 1 - c,
        }[role]

    def own(self):
        y, c, _, _ = place()
        return y * NC + c

    def start(self):
        up, down, other = near()
        own = self.own()
        pltpu.make_async_copy(self.src, self.buf, self.local.at[0]).start()

        def go(k, carry):
            self.copy(self.src, own, 0, k, up).start()
            self.copy(self.src, own, 1, k, down).start()
            self.copy(self.src, own, 3, k, other).start()
            return carry

        lax.fori_loop(0, self.chunks, go, 0)
        pltpu.make_async_copy(self.src, self.buf, self.local.at[0]).wait()
        pltpu.make_async_copy(self.buf, self.dst.at[own], self.local.at[1]).start()

    def arrived(self, role, k):
        block = self.block(role)
        self.copy(self.dst.at[block], block, role, k, near()[2]).wait_recv()

    def handon(self, role, k):
        block = self.block(role)
        self.copy(self.dst.at[block], block, role + 4, k, near()[2]).start()

    def middle(self, k):
        y, c, _, _ = place()
        up, down, other = near()
        self.arrived(0, k)

        @pl.when(c == 0)
        def _():
            self.copy(self.dst.at[self.block(0)], self.block(0), 2, k, up).start()

        self.handon(0, k)
        self.arrived(1, k)

        @pl.when(c == 1)
        def _():
            self.copy(self.dst.at[self.block(1)], self.block(1), 2, k, down).start()

        self.handon(1, k)

    def last(self, k):
        self.arrived(2, k)
        self.handon(2, k)

    def finish(self):
        own = self.own()
        other = near()[2]

        def go(k, carry):
            for role in (3, 4, 5, 6):
                self.arrived(role, k)
            for role in range(7):
                self.copy(self.src, own, role, k, other).wait_send()
            return carry

        lax.fori_loop(0, self.chunks, go, 0)
        pltpu.make_async_copy(self.buf, self.dst.at[own], self.local.at[1]).wait()


def gather_scratch(shapes, chunks):
    out = []
    for shape, n in zip(shapes, chunks):
        out += [
            pltpu.VMEM(shape, jnp.bfloat16),
            DMA((7, n)),
            DMA((7, n)),
            DMA((2,)),
        ]
    return out


def gather_kernel(shapes, chunks, *refs):
    n = len(shapes)
    sources, targets, scratch = refs[:n], refs[n : 2 * n], refs[2 * n :]
    for device in near():
        signal(*device)
    pl.semaphore_wait(pltpu.get_barrier_semaphore(), 3)
    gathers = []
    for i in range(n):
        buf, send, recv, local = scratch[4 * i : 4 * i + 4]
        gathers.append(
            JobGather(sources[i], targets[i], buf, send, recv, local, shapes[i][0], chunks[i])
        )
    for one in gathers:
        one.start()
    for one in gathers:
        lax.fori_loop(0, one.chunks, lambda k, carry: (one.middle(k), carry)[1], 0)
        lax.fori_loop(0, one.chunks, lambda k, carry: (one.last(k), carry)[1], 0)
    for one in gathers:
        one.finish()


def gather_job(arrays, chunks, collective_id):
    shapes = [a.shape for a in arrays]
    return pl.pallas_call(
        functools.partial(gather_kernel, shapes, chunks),
        out_shape=[jax.ShapeDtypeStruct((N_JOB, *s), jnp.bfloat16) for s in shapes],
        in_specs=[ANY] * len(arrays),
        out_specs=[ANY] * len(arrays),
        scratch_shapes=gather_scratch(shapes, chunks),
        compiler_params=pltpu.CompilerParams(collective_id=collective_id, has_side_effects=True),
        name=f"gather_job_{collective_id}",
    )(*arrays)


def far_first(n):
    return 4 + ((n + 1) // 2) * (1 - 2 * (n % 2))


W_CHUNKS = 8


def exchange_kernel(
    vid, txt, w_out, rvid, rtxt, w_all, vsend, vrecv, tsend, trecv, buf, wsend, wrecv, wlocal
):
    y, c, z, x = place()
    seq = z * NX + x
    up, down, other = near()
    here = (x // 2 == c).astype(jnp.int32)
    peer_job = y * NC + x // 2

    def greet(n, carry):
        for hl in range(2):
            to = n * NX + 2 * c + hl

            @pl.when(jnp.logical_or(to != seq, here == 0))
            def _():
                signal(peer_job, to)

        return carry

    lax.fori_loop(0, NZ, greet, 0)
    for device in near():
        signal(*device)
    pl.semaphore_wait(pltpu.get_barrier_semaphore(), 19 - here)

    def vrows(shard):
        return rvid.at[:, pl.ds(pl.multiple_of(shard * 128, 128), 128), :]

    def trows(shard):
        return rtxt.at[:, pl.ds(pl.multiple_of(shard * 8, 8), 8), :]

    def pair_of(n, hl):
        zd = (z + far_first(n)) % NZ
        j = (zd + NZ - 2 * y) % NZ
        return 2 * j + hl, zd * NX + 2 * c + hl

    slot = 2 * z + x % 2

    def sends(n, hl):
        pair, to = pair_of(n, hl)
        device = (peer_job, to)
        step = 2 * n + hl
        return to, (
            pltpu.make_async_remote_copy(
                vid.at[pair], vrows(seq), vsend.at[step], vrecv.at[slot], device, MESH
            ),
            pltpu.make_async_remote_copy(
                txt.at[pair], trows(seq), tsend.at[step], trecv.at[slot], device, MESH
            ),
        )

    def locals_(n, hl):
        pair, _ = pair_of(n, hl)
        return (
            pltpu.make_async_copy(vid.at[pair], vrows(seq), vrecv.at[slot]),
            pltpu.make_async_copy(txt.at[pair], trows(seq), trecv.at[slot]),
        )

    def start(n, carry):
        for hl in range(2):
            to, copies = sends(n, hl)
            away = jnp.logical_or(to != seq, here == 0)

            @pl.when(away)
            def _():
                for one in copies:
                    one.start()

            @pl.when(jnp.logical_not(away))
            def _():
                for one in locals_(n, hl):
                    one.start()

        return carry

    lax.fori_loop(0, NZ, start, 0)
    weights = JobGather(w_out.at[0], w_all, buf, wsend, wrecv, wlocal, HD, W_CHUNKS)
    weights.start()

    def handed(shard, index, base):
        return (
            pltpu.make_async_remote_copy(
                vrows(shard), vrows(shard), vsend.at[base], vrecv.at[index], other, MESH
            ),
            pltpu.make_async_remote_copy(
                trows(shard), trows(shard), tsend.at[base], trecv.at[index], other, MESH
            ),
        )

    def arrive(n, carry):
        zs = (z + NZ - far_first(n)) % NZ
        for b in range(2):
            shard = zs * NX + 2 * c + b
            index = 2 * zs + b
            for one in handed(shard, index, 0):
                one.wait_recv()
            for one in handed(shard, index + 16, index + 16):
                one.start()
        weights.middle(n)
        return carry

    lax.fori_loop(0, NZ, arrive, 0)
    lax.fori_loop(0, W_CHUNKS, lambda k, carry: (weights.last(k), carry)[1], 0)

    def finish(n, carry):
        for b in range(2):
            shard = n * NX + 2 * (1 - c) + b
            index = 2 * n + b
            for one in handed(shard, index + 16, index + 16):
                one.wait_recv()
            for one in handed(shard, index + 16, index + 16):
                one.wait_send()
        for hl in range(2):
            to, copies = sends(n, hl)

            @pl.when(jnp.logical_or(to != seq, here == 0))
            def _():
                for one in copies:
                    one.wait_send()

        return carry

    lax.fori_loop(0, NZ, finish, 0)
    weights.finish()


def exchange(vid, txt, w_out):
    bf = jnp.bfloat16
    return pl.pallas_call(
        exchange_kernel,
        out_shape=[
            jax.ShapeDtypeStruct((3, N_SEQ * 128, HD), bf),
            jax.ShapeDtypeStruct((5, N_SEQ * 8, HD), bf),
            jax.ShapeDtypeStruct((N_JOB, *w_out.shape[1:]), bf),
        ],
        in_specs=[ANY] * 3,
        out_specs=[ANY] * 3,
        scratch_shapes=[DMA((32,)), DMA((32,)), DMA((32,)), DMA((32,))]
        + gather_scratch([w_out.shape[1:]], [W_CHUNKS]),
        compiler_params=pltpu.CompilerParams(collective_id=5, has_side_effects=True),
        name="exchange",
    )(vid, txt, w_out)


def attend_kernel(
    counts, vid, txt, slots, w_out, rv, rt, w_all,
    q, k, tx, vext, text_out, ov, ot, loads, vsend, vrecv, tsend, trecv, buf, wsend, wrecv, wlocal,
):
    y, c, z, x = place()
    seq = z * NX + x
    mine = y * NC + c
    job = (z + NZ - 2 * y) % NZ
    head = (x % 2) * 8 + 2 * y + x // 2
    incoming = [
        pltpu.make_async_copy(vid.at[0], q, loads.at[0]),
        pltpu.make_async_copy(vid.at[1], k, loads.at[1]),
        pltpu.make_async_copy(vid.at[2], vext.at[pl.ds(0, 4096), pl.ds(0, HD)], loads.at[2]),
        pltpu.make_async_copy(txt.at[2], vext.at[pl.ds(4096, 256), pl.ds(0, HD)], loads.at[3]),
        pltpu.make_async_copy(txt, tx, loads.at[4]),
    ]
    for one in incoming:
        one.start()

    def greet(n, carry):
        for b in range(NX):
            from_job = n * NC + x // 2
            from_seq = ((mine + 2 * n) % NZ) * NX + b

            @pl.when(jnp.logical_or(from_job != mine, from_seq != seq))
            def _():
                signal(from_job, from_seq)

        return carry

    lax.fori_loop(0, NY, greet, 0)
    for device in near():
        signal(*device)
    inside = jnp.logical_and(job == mine, x // 2 == c).astype(jnp.int32)
    pl.semaphore_wait(pltpu.get_barrier_semaphore(), 19 - inside)
    weights = JobGather(w_out.at[1], w_all, buf, wsend, wrecv, wlocal, HD, W_CHUNKS)
    weights.start()

    count = counts[job]
    vext[:, HD:] = jnp.ones((4352, HD), jnp.bfloat16)
    for one in incoming:
        one.wait()
    factor = (HD**-0.5) * 1.4426950408889634
    contract = (((1,), (1,)), ((), ()))

    def block(part):
        sv = lax.dot_general(part, k[...], contract, preferred_element_type=jnp.float32)
        st = lax.dot_general(part, tx[1], contract, preferred_element_type=jnp.float32)
        st = jnp.where(lax.broadcasted_iota(jnp.int32, st.shape, 1) < count, st, -1e30)
        top = jnp.maximum(
            jnp.max(sv, axis=-1, keepdims=True), jnp.max(st, axis=-1, keepdims=True)
        )
        pv = jnp.exp2((sv - top) * factor).astype(jnp.bfloat16)
        pt = jnp.exp2((st - top) * factor).astype(jnp.bfloat16)
        both = jnp.dot(pv, vext[0:4096], preferred_element_type=jnp.float32)
        both += jnp.dot(pt, vext[4096:4352], preferred_element_type=jnp.float32)
        return (both[:, 0:HD] / both[:, HD:]).astype(jnp.bfloat16)

    text_out[...] = block(tx[0])
    pick = (slots[...] == lax.broadcasted_iota(jnp.int32, (256, 256), 1)).astype(jnp.bfloat16)
    for part in range(3):
        rows = text_out[...] if part == 0 else tx[part + 2]
        moved = jnp.dot(pick, rows, preferred_element_type=jnp.float32).astype(jnp.bfloat16)
        ot[:, part] = moved.reshape(16, 16, HD)

    def copies(n, b):
        zd = (z + far_first(n)) % NZ
        part = 2 * zd + b
        to = zd * NX + 2 * c + b
        away = jnp.logical_or(to != seq, job != mine)
        remote = (
            pltpu.make_async_remote_copy(
                ov.at[part], rv.at[head], vsend.at[part], vrecv.at[head], (job, to), MESH
            ),
            pltpu.make_async_remote_copy(
                ot.at[part], rt.at[head], tsend.at[part], trecv.at[head], (job, to), MESH
            ),
        )
        local = (
            pltpu.make_async_copy(ov.at[part], rv.at[head], vrecv.at[head]),
            pltpu.make_async_copy(ot.at[part], rt.at[head], trecv.at[head]),
        )
        return away, remote, local

    def start(n):
        for b in range(2):
            away, remote, local = copies(n, b)

            @pl.when(away)
            def _():
                for one in remote:
                    one.start()

            @pl.when(jnp.logical_not(away))
            def _():
                for one in local:
                    one.start()

    def step(n, carry):
        zd = (z + far_first(n)) % NZ
        rows = pl.ds(pl.multiple_of(zd * 512 + c * 256, 256), 256)
        ov[pl.ds(2 * zd, 2)] = block(q[rows, :]).reshape(2, 128, HD)

        @pl.when(n > 0)
        def _():
            start(n - 1)

        weights.middle(n)
        return carry

    lax.fori_loop(0, NZ, step, 0)
    lax.fori_loop(0, W_CHUNKS, lambda n, carry: (weights.last(n), carry)[1], 0)
    start(NZ - 1)

    def finish(n, carry):
        pltpu.make_async_copy(ov.at[n], rv.at[n], vrecv.at[n]).wait()
        pltpu.make_async_copy(ot.at[n], rt.at[n], trecv.at[n]).wait()
        return carry

    lax.fori_loop(0, 16, finish, 0)

    def sent(n, carry):
        for b in range(2):
            away, remote, _ = copies(n, b)

            @pl.when(away)
            def _():
                for one in remote:
                    one.wait_send()

        return carry

    lax.fori_loop(0, NZ, sent, 0)
    weights.finish()


def attend(counts, vid, txt, slots, w_out):
    bf = jnp.bfloat16
    vm = pl.BlockSpec(memory_space=pltpu.VMEM)
    half = (HD, w_out.shape[2])
    return pl.pallas_call(
        attend_kernel,
        out_shape=[
            jax.ShapeDtypeStruct((16, 128, HD), bf),
            jax.ShapeDtypeStruct((16, 3, 16, HD), bf),
            jax.ShapeDtypeStruct((N_JOB, *half), bf),
        ],
        in_specs=[pl.BlockSpec(memory_space=pltpu.SMEM), ANY, ANY, vm, ANY],
        out_specs=[ANY] * 3,
        scratch_shapes=[
            pltpu.VMEM((4096, HD), bf),
            pltpu.VMEM((4096, HD), bf),
            pltpu.VMEM((5, 256, HD), bf),
            pltpu.VMEM((4352, 2 * HD), bf),
            pltpu.VMEM((256, HD), bf),
            pltpu.VMEM((16, 128, HD), bf),
            pltpu.VMEM((16, 3, 16, HD), bf),
            DMA((5,)),
            DMA((16,)),
            DMA((16,)),
            DMA((16,)),
            DMA((16,)),
        ]
        + gather_scratch([half], [W_CHUNKS]),
        compiler_params=pltpu.CompilerParams(
            collective_id=6, has_side_effects=True, vmem_limit_bytes=56 << 20
        ),
        name="attend",
    )(counts, vid, txt, slots, w_out)


def body(
    video,
    text_cache,
    text_count,
    holder,
    text_splits,
    mod_shift,
    mod_scale,
    mod_gate,
    text_gain,
    refine_w,
    refine_bias,
    w_qkv,
    q_gain,
    k_gain,
    w_out,
):
    y, c, z, x = place()
    my_job = lax.axis_index("job")
    my_shard = lax.axis_index("seq")
    bf = jnp.bfloat16
    own_video = video[0]
    (raw,) = gather_job([text_cache[0]], [1], 1)
    chosen = jnp.take(raw, holder, axis=0).reshape(64, -1)
    normed = rms_scale(chosen.astype(jnp.float32), text_gain).astype(bf)
    refined = (
        jnp.dot(normed, refine_w, preferred_element_type=jnp.float32) + refine_bias
    ).astype(bf)
    video_all, refined_all = gather_job([own_video, refined], [4, 1], 2)
    text_full = jnp.transpose(refined_all, (1, 0, 2)).reshape(8, 8, -1)
    rows = jnp.concatenate([video_all, text_full], axis=1)
    modded = modulate(rows, mod_shift[:, None, :], mod_scale[:, None, :])
    projections = jnp.einsum("jrd,dhce->jrhce", modded, w_qkv, preferred_element_type=jnp.float32)
    queries = rms_scale(projections[:, :, :, 0], q_gain).astype(bf)
    keys = rms_scale(projections[:, :, :, 1], k_gain).astype(bf)
    values = projections[:, :, :, 2].astype(bf)
    heads = jnp.stack([queries, keys, values], axis=3)
    heads = jnp.transpose(heads, (0, 2, 3, 1, 4))
    vid = heads[:, :, :, :128].reshape(16, 3, 128, HD)
    carried = jnp.pad(refined.reshape(8, 8, 3, HD), ((0, 0), (0, 0), (0, 1), (0, 0)))
    carried = jnp.transpose(carried.reshape(8, 8, 2, 2, HD), (0, 2, 3, 1, 4))
    txt = jnp.concatenate([heads[:, :, :, 128:], carried], axis=2).reshape(16, 5, 8, HD)
    rvid, rtxt, w_even = exchange(vid, txt, w_out)

    offsets = jnp.cumsum(text_splits, axis=1) - text_splits
    ids = jnp.arange(16, dtype=jnp.int32)
    where_to = offsets[:, :, None] + ids
    valid = (ids < text_splits[:, :, None]) & (where_to < text_count[:, None, None])
    where_to = jnp.where(valid, where_to, -1).reshape(8, NZ, NC, 2, 16)
    job_here = (z + NZ - 2 * y) % NZ
    slots = lax.dynamic_slice(where_to, (job_here, 0, c, 0, 0), (1, NZ, 1, 2, 16))
    rv, rt, w_odd = attend(text_count, rvid, rtxt, slots.reshape(256, 1), w_out)

    attended = jnp.concatenate([rv, rt[:, 0]], axis=1)
    attended = jnp.transpose(attended, (1, 0, 2)).reshape(144, 2048)
    f32 = jnp.float32
    projected = jnp.dot(
        attended[:, :1024], w_even.reshape(1024, -1), preferred_element_type=f32
    ) + jnp.dot(attended[:, 1024:], w_odd.reshape(1024, -1), preferred_element_type=f32)
    kept = jnp.concatenate([rt[:8, 1:], rt[8:, 1:2]], axis=1)
    kept = jnp.transpose(kept, (2, 0, 1, 3)).reshape(16, -1)
    own_rows = jnp.concatenate([own_video, kept], axis=0).astype(jnp.float32)
    gate = lax.dynamic_index_in_dim(mod_gate, my_job, 0, keepdims=True)
    result = (own_rows + gate * projected).astype(bf)
    ok = lax.dynamic_slice(valid, (my_job, my_shard, 0), (1, 1, 16)).reshape(16, 1)
    text_result = jnp.where(ok, result[128:], jnp.zeros_like(result[128:]))
    return (result[:128][None], text_result[None])


def solution(mesh):
    placed = (
        P("job", "seq", None),
        P("job", "seq", None),
        P(),
        P(),
        P(),
        P(),
        P(),
        P(),
        P(),
        P(None, "job"),
        P("job"),
        P(None, "job", None, None),
        P("job", None),
        P("job", None),
        P("job", None, None),
    )
    return jax.shard_map(
        body,
        mesh=mesh,
        in_specs=placed,
        out_specs=(P("job", "seq", None), P("job", "seq", None)),
        check_vma=False,
    )
```

```python
import functools

import jax
import jax.numpy as jnp
from jax import lax
from jax.experimental import pallas as pl
from jax.experimental.pallas import tpu as pltpu
from jax.sharding import PartitionSpec as P

HD = 128
NY, NC, NZ, NX = 4, 2, 8, 4
N_JOB = NY * NC
N_SEQ = NZ * NX
MESH = pl.DeviceIdType.MESH
epsilon = 1e-06
ANY = pl.BlockSpec(memory_space=pl.ANY)
DMA = pltpu.SemaphoreType.DMA


def rms_scale(values, gains):
    mean_square = jnp.mean(values * values, axis=-1, keepdims=True)
    return values * lax.rsqrt(mean_square + epsilon) * gains


def modulate(tokens, shift_part, scale_part):
    widened = tokens.astype(jnp.float32)
    centre = jnp.mean(widened, axis=-1, keepdims=True)
    spread_sq = jnp.mean((widened - centre) ** 2, axis=-1, keepdims=True)
    normed = (widened - centre) * lax.rsqrt(spread_sq + epsilon)
    return (normed * (1.0 + scale_part) + shift_part).astype(jnp.bfloat16)


def place():
    job = lax.axis_index("job")
    seq = lax.axis_index("seq")
    return job // NC, job % NC, seq // NX, seq % NX


def signal(job, seq):
    pl.semaphore_signal(
        pltpu.get_barrier_semaphore(), inc=1, device_id=(job, seq), device_id_type=MESH
    )


def near():
    y, c, z, x = place()
    seq = z * NX + x
    up = (((y + 1) % NY) * NC + c, seq)
    down = (((y + NY - 1) % NY) * NC + c, seq)
    other = (y * NC + 1 - c, seq)
    return up, down, other


def span(k, step):
    if isinstance(k, int):
        return pl.ds(k * step, step)
    return pl.ds(pl.multiple_of(k * step, step), step)


class JobGather:
    def __init__(self, src, dst, send, recv, local, rows, chunks, buf=None):
        self.src, self.dst, self.buf = src, dst, buf
        self.send, self.recv, self.local = send, recv, local
        self.step, self.chunks = rows // chunks, chunks

    def piece(self, k):
        return span(k, self.step)

    def copy(self, source, block, role, k, device):
        return pltpu.make_async_remote_copy(
            src_ref=source.at[self.piece(k)],
            dst_ref=self.dst.at[block, self.piece(k)],
            send_sem=self.send.at[role, k],
            recv_sem=self.recv.at[role, k],
            device_id=device,
            device_id_type=MESH,
        )

    def block(self, role):
        y, c, _, _ = place()
        return {
            0: ((y + NY - 1) % NY) * NC + c,
            1: ((y + 1) % NY) * NC + c,
            2: ((y + 2) % NY) * NC + c,
            3: y * NC + 1 - c,
            4: ((y + NY - 1) % NY) * NC + 1 - c,
            5: ((y + 1) % NY) * NC + 1 - c,
            6: ((y + 2) % NY) * NC + 1 - c,
        }[role]

    def own(self):
        y, c, _, _ = place()
        return y * NC + c

    def load(self):
        into = self.dst.at[self.own()] if self.buf is None else self.buf
        pltpu.make_async_copy(self.src, into, self.local.at[0]).start()

    def loaded(self):
        into = self.dst.at[self.own()] if self.buf is None else self.buf
        pltpu.make_async_copy(self.src, into, self.local.at[0]).wait()
        if self.buf is not None:
            pltpu.make_async_copy(self.buf, self.dst.at[self.own()], self.local.at[1]).start()

    def send_own(self, k):
        up, down, other = near()
        own = self.own()
        self.copy(self.src, own, 0, k, up).start()
        self.copy(self.src, own, 1, k, down).start()
        self.copy(self.src, own, 3, k, other).start()

    def arrived(self, role, k):
        block = self.block(role)
        self.copy(self.dst.at[block], block, role, k, near()[2]).wait_recv()

    def handon(self, role, k):
        block = self.block(role)
        self.copy(self.dst.at[block], block, role + 4, k, near()[2]).start()

    def middle(self, k):
        y, c, _, _ = place()
        up, down, other = near()
        self.arrived(0, k)

        @pl.when(c == 0)
        def _():
            self.copy(self.dst.at[self.block(0)], self.block(0), 2, k, up).start()

        self.handon(0, k)
        self.arrived(1, k)

        @pl.when(c == 1)
        def _():
            self.copy(self.dst.at[self.block(1)], self.block(1), 2, k, down).start()

        self.handon(1, k)

    def last(self, k):
        self.arrived(2, k)
        self.handon(2, k)

    def side(self, k):
        for role in (3, 4, 5, 6):
            self.arrived(role, k)

    def finish(self):
        own = self.own()
        other = near()[2]

        def go(k, carry):
            for role in range(7):
                self.copy(self.src, own, role, k, other).wait_send()
            return carry

        lax.fori_loop(0, self.chunks, go, 0)
        if self.buf is not None:
            pltpu.make_async_copy(self.buf, self.dst.at[own], self.local.at[1]).wait()


def gather_sems(chunks):
    return [DMA((7, chunks)), DMA((7, chunks)), DMA((2,))]


def far_first(n):
    return 4 + ((n + 1) // 2) * (1 - 2 * (n % 2))


W_CHUNKS = 8
AHEAD = 4
V_CHUNKS = 4
V_ROWS = 128 // V_CHUNKS


def project_kernel(
    holder, raw, video, refine_w, w_qkv, w_out, gain, bias, scale, shift, q_gain, k_gain,
    rvid, rtxt, w_all,
    raw_all, video_all, refined, refined_all, wr, wq, normed, modded, text_rows, svid, stxt, buf,
    loads, rsend, rrecv, rlocal, fsend, frecv, flocal, isend, irecv, ilocal,
    wsend, wrecv, wlocal, vsend, vrecv, tsend, trecv,
):
    y, c, z, x = place()
    seq = z * NX + x
    f32, bf = jnp.float32, jnp.bfloat16
    other = near()[2]
    here = (x // 2 == c).astype(jnp.int32)
    peer_job = y * NC + x // 2
    text = JobGather(raw, raw_all, rsend, rrecv, rlocal, 8, 1)
    frames = JobGather(video, video_all, fsend, frecv, flocal, 128, V_CHUNKS)
    inner = JobGather(refined, refined_all, isend, irecv, ilocal, 64, 1)
    weights = JobGather(w_out.at[0], w_all, wsend, wrecv, wlocal, HD, W_CHUNKS, buf)
    text.load()
    frames.load()
    load_r = pltpu.make_async_copy(refine_w, wr, loads.at[0])
    load_q = pltpu.make_async_copy(w_qkv, wq, loads.at[1])
    load_r.start()
    load_q.start()

    def greet(n, carry):
        for hl in range(2):
            to = n * NX + 2 * c + hl

            @pl.when(jnp.logical_or(to != seq, here == 0))
            def _():
                signal(peer_job, to)

        return carry

    lax.fori_loop(0, NZ, greet, 0)
    for device in near():
        signal(*device)
    pl.semaphore_wait(pltpu.get_barrier_semaphore(), 19 - here)

    text.send_own(0)
    frames.send_own(0)
    frames.send_own(1)
    text.middle(0)
    text.last(0)
    text.side(0)
    text.loaded()
    for j in range(N_JOB):
        rows = raw_all[holder[j]].astype(f32)
        normed[pl.ds(8 * j, 8)] = rms_scale(rows, gain[...])
    load_r.wait()
    lifted = jnp.dot(normed[...].astype(bf), wr[...], preferred_element_type=f32)
    refined[...] = (lifted + bias[...]).astype(bf)
    inner_own = pltpu.make_async_copy(refined, refined_all.at[inner.own()], ilocal.at[0])

    def vrows(shard, k):
        first = pl.multiple_of(shard * 128 + k * V_ROWS, V_ROWS)
        return rvid.at[:, pl.ds(first, V_ROWS), :]

    def trows(shard):
        return rtxt.at[:, pl.ds(pl.multiple_of(shard * 8, 8), 8), :]

    slot = 2 * z + x % 2

    def target(n, hl):
        zd = (z + far_first(n)) % NZ
        j = (zd + NZ - 2 * y) % NZ
        to = zd * NX + 2 * c + hl
        return 2 * j + hl, to, jnp.logical_or(to != seq, here == 0)

    def vcopy(n, hl, k):
        pair, to, away = target(n, hl)
        source = svid.at[pair, :, span(k, V_ROWS), :]
        remote = pltpu.make_async_remote_copy(
            source, vrows(seq, k), vsend.at[2 * n + hl, k], vrecv.at[slot, k],
            (peer_job, to), MESH,
        )
        return away, remote, pltpu.make_async_copy(source, vrows(seq, k), vrecv.at[slot, k])

    def tcopy(n, hl):
        pair, to, away = target(n, hl)
        remote = pltpu.make_async_remote_copy(
            stxt.at[pair], trows(seq), tsend.at[2 * n + hl], trecv.at[slot], (peer_job, to), MESH
        )
        return away, remote, pltpu.make_async_copy(stxt.at[pair], trows(seq), trecv.at[slot])

    def launch(make):
        def go(n, carry):
            for hl in range(2):
                away, remote, local = make(n, hl)

                @pl.when(away)
                def _():
                    remote.start()

                @pl.when(jnp.logical_not(away))
                def _():
                    local.start()

            return carry

        lax.fori_loop(0, NZ, go, 0)

    def drained(make):
        def go(n, carry):
            for hl in range(2):
                away, remote, _ = make(n, hl)

                @pl.when(away)
                def _():
                    remote.wait_send()

            return carry

        lax.fori_loop(0, NZ, go, 0)

    def vhand(shard, index, k):
        return pltpu.make_async_remote_copy(
            vrows(shard, k), vrows(shard, k), vsend.at[index, k], vrecv.at[index, k], other, MESH
        )

    def thand(shard, index):
        return pltpu.make_async_remote_copy(
            trows(shard), trows(shard), tsend.at[index], trecv.at[index], other, MESH
        )

    def sources(n):
        zs = (z + NZ - far_first(n)) % NZ
        return [(zs * NX + 2 * c + b, 2 * zs + b) for b in range(2)]

    def take(k):
        def go(n, carry):
            for shard, index in sources(n):
                vhand(shard, index, k).wait_recv()
                vhand(shard, index + 16, k).start()
            return carry

        lax.fori_loop(0, NZ, go, 0)

    def normalise(rows, j):
        centre = jnp.mean(rows, axis=-1, keepdims=True)
        moved = rows - centre
        spread_sq = jnp.mean(moved * moved, axis=-1, keepdims=True)
        out = moved * lax.rsqrt(spread_sq + epsilon)
        return (out * (1.0 + scale[pl.ds(j, 1), :]) + shift[pl.ds(j, 1), :]).astype(bf)

    def project(rows):
        got = jnp.dot(rows, wq[...], preferred_element_type=f32)
        out = []
        for hl in range(2):
            for part in range(3):
                piece = got[:, (hl * 3 + part) * HD : (hl * 3 + part + 1) * HD]
                if part == 0:
                    piece = rms_scale(piece, q_gain[pl.ds(hl, 1), :])
                if part == 1:
                    piece = rms_scale(piece, k_gain[pl.ds(hl, 1), :])
                out.append(piece.astype(bf))
        return out

    frames.loaded()

    def round_(k, carry):
        frames.middle(k)

        @pl.when(k + 2 < V_CHUNKS)
        def _():
            frames.send_own(k + 2)

        @pl.when(k == 0)
        def _():
            inner_own.start()
            inner.send_own(0)
            load_q.wait()

        @pl.when(k == 1)
        def _():
            inner.middle(0)
            inner.last(0)

        frames.last(k)
        frames.side(k)

        @pl.when(k > 0)
        def _():
            launch(lambda n, hl: vcopy(n, hl, k - 1))

        rows_k = span(k, V_ROWS)
        for j in range(N_JOB):
            modded[pl.ds(V_ROWS * j, V_ROWS)] = normalise(video_all[j, rows_k, :].astype(f32), j)
        for i, piece in enumerate(project(modded[...])):
            for j in range(N_JOB):
                svid[2 * j + i // 3, i % 3, rows_k, :] = piece[V_ROWS * j : V_ROWS * (j + 1)]

        @pl.when(k >= 2)
        def _():
            take(k - 2)

        return carry

    lax.fori_loop(0, V_CHUNKS, round_, 0)
    weights.load()
    weights.send_own(0)
    weights.send_own(1)
    inner.side(0)
    inner_own.wait()
    for g in range(N_JOB):
        text_rows[:, 384 * g : 384 * (g + 1)] = refined_all[g].astype(f32)
    for j in range(N_JOB):
        normed[pl.ds(8 * j, 8), 0:3072] = normalise(text_rows[pl.ds(8 * j, 8)], j).astype(f32)
    launch(lambda n, hl: vcopy(n, hl, V_CHUNKS - 1))
    for i, piece in enumerate(project(normed[:, 0:3072].astype(bf))):
        for j in range(N_JOB):
            stxt[2 * j + i // 3, i % 3] = piece[8 * j : 8 * (j + 1)]
    for j in range(N_JOB):
        for group in range(4):
            at = min(group, 2) * HD
            stxt[2 * j + group // 2, 3 + group % 2] = refined[8 * j : 8 * (j + 1), at : at + HD]
    weights.loaded()
    take(V_CHUNKS - 2)
    launch(tcopy)

    def rest(n, carry):
        weights.middle(n)

        @pl.when(n + 2 < W_CHUNKS)
        def _():
            weights.send_own(n + 2)

        for shard, index in sources(n):
            vhand(shard, index, V_CHUNKS - 1).wait_recv()
            vhand(shard, index + 16, V_CHUNKS - 1).start()

        @pl.when(n > 0)
        def _():
            weights.last(n - 1)

        return carry

    lax.fori_loop(0, NZ, rest, 0)
    weights.last(W_CHUNKS - 1)

    def text_rest(n, carry):
        for shard, index in sources(n):
            thand(shard, index).wait_recv()
            thand(shard, index + 16).start()
        return carry

    lax.fori_loop(0, NZ, text_rest, 0)

    def finish(n, carry):
        for b in range(2):
            shard = n * NX + 2 * (1 - c) + b
            index = 2 * n + b + 16
            for k in range(V_CHUNKS):
                vhand(shard, index, k).wait_recv()
                vhand(shard, index, k).wait_send()
            thand(shard, index).wait_recv()
            thand(shard, index).wait_send()
        return carry

    lax.fori_loop(0, NZ, finish, 0)
    for k in range(V_CHUNKS):
        drained(lambda n, hl: vcopy(n, hl, k))
    drained(tcopy)
    lax.fori_loop(0, W_CHUNKS, lambda k, carry: (weights.side(k), carry)[1], 0)
    for one in (text, frames, inner, weights):
        one.finish()


def project_all(holder, raw, video, refine_w, w_qkv, w_out, *small):
    f32, bf = jnp.float32, jnp.bfloat16
    vm = pl.BlockSpec(memory_space=pltpu.VMEM)
    return pl.pallas_call(
        project_kernel,
        out_shape=[
            jax.ShapeDtypeStruct((3, N_SEQ * 128, HD), bf),
            jax.ShapeDtypeStruct((5, N_SEQ * 8, HD), bf),
            jax.ShapeDtypeStruct((N_JOB, *w_out.shape[1:]), bf),
        ],
        in_specs=[pl.BlockSpec(memory_space=pltpu.SMEM)] + [ANY] * 5 + [vm] * 6,
        out_specs=[ANY] * 3,
        scratch_shapes=[
            pltpu.VMEM((N_JOB, 8, 4096), bf),
            pltpu.VMEM((N_JOB, 128, 3072), bf),
            pltpu.VMEM((64, 384), bf),
            pltpu.VMEM((N_JOB, 64, 384), bf),
            pltpu.VMEM((4096, 384), bf),
            pltpu.VMEM((3072, 768), bf),
            pltpu.VMEM((64, 4096), f32),
            pltpu.VMEM((8 * V_ROWS, 3072), bf),
            pltpu.VMEM((64, 3072), f32),
            pltpu.VMEM((16, 3, 128, HD), bf),
            pltpu.VMEM((16, 5, 8, HD), bf),
            pltpu.VMEM(w_out.shape[1:], bf),
            DMA((2,)),
            *gather_sems(1),
            *gather_sems(V_CHUNKS),
            *gather_sems(1),
            *gather_sems(W_CHUNKS),
            DMA((32, V_CHUNKS)),
            DMA((32, V_CHUNKS)),
            DMA((32,)),
            DMA((32,)),
        ],
        compiler_params=pltpu.CompilerParams(
            collective_id=5, has_side_effects=True, vmem_limit_bytes=58 << 20
        ),
        name="project_all",
    )(holder, raw, video, refine_w, w_qkv, w_out, *small)


def attend_kernel(
    counts, vid, txt, slots, w_out, rv, rt, w_all,
    q, k, tx, vext, text_out, ov, ot, loads, vsend, vrecv, tsend, trecv, buf, wsend, wrecv, wlocal,
):
    y, c, z, x = place()
    seq = z * NX + x
    mine = y * NC + c
    job = (z + NZ - 2 * y) % NZ
    head = (x % 2) * 8 + 2 * y + x // 2
    incoming = [
        pltpu.make_async_copy(vid.at[0], q, loads.at[0]),
        pltpu.make_async_copy(vid.at[1], k, loads.at[1]),
        pltpu.make_async_copy(vid.at[2], vext.at[pl.ds(0, 4096), pl.ds(0, HD)], loads.at[2]),
        pltpu.make_async_copy(txt.at[2], vext.at[pl.ds(4096, 256), pl.ds(0, HD)], loads.at[3]),
        pltpu.make_async_copy(txt, tx, loads.at[4]),
    ]
    for one in incoming:
        one.start()

    def greet(n, carry):
        for b in range(NX):
            from_job = n * NC + x // 2
            from_seq = ((mine + 2 * n) % NZ) * NX + b

            @pl.when(jnp.logical_or(from_job != mine, from_seq != seq))
            def _():
                signal(from_job, from_seq)

        return carry

    lax.fori_loop(0, NY, greet, 0)
    for device in near():
        signal(*device)
    inside = jnp.logical_and(job == mine, x // 2 == c).astype(jnp.int32)
    pl.semaphore_wait(pltpu.get_barrier_semaphore(), 19 - inside)
    weights = JobGather(w_out.at[1], w_all, wsend, wrecv, wlocal, HD, W_CHUNKS, buf)
    weights.load()
    for ahead in range(AHEAD):
        weights.send_own(ahead)
    weights.loaded()

    count = counts[job]
    vext[:, HD:] = jnp.ones((4352, HD), jnp.bfloat16)
    for one in incoming:
        one.wait()
    factor = (HD**-0.5) * 1.4426950408889634
    contract = (((1,), (1,)), ((), ()))

    def block(part):
        sv = lax.dot_general(part, k[...], contract, preferred_element_type=jnp.float32)
        st = lax.dot_general(part, tx[1], contract, preferred_element_type=jnp.float32)
        st = jnp.where(lax.broadcasted_iota(jnp.int32, st.shape, 1) < count, st, -1e30)
        top = jnp.maximum(
            jnp.max(sv, axis=-1, keepdims=True), jnp.max(st, axis=-1, keepdims=True)
        )
        pv = jnp.exp2((sv - top) * factor).astype(jnp.bfloat16)
        pt = jnp.exp2((st - top) * factor).astype(jnp.bfloat16)
        both = jnp.dot(pv, vext[0:4096], preferred_element_type=jnp.float32)
        both += jnp.dot(pt, vext[4096:4352], preferred_element_type=jnp.float32)
        return (both[:, 0:HD] / both[:, HD:]).astype(jnp.bfloat16)

    text_out[...] = block(tx[0])
    pick = (slots[...] == lax.broadcasted_iota(jnp.int32, (256, 256), 1)).astype(jnp.bfloat16)
    for part in range(3):
        rows = text_out[...] if part == 0 else tx[part + 2]
        moved = jnp.dot(pick, rows, preferred_element_type=jnp.float32).astype(jnp.bfloat16)
        ot[:, part] = moved.reshape(16, 16, HD)

    def copies(n, b):
        zd = (z + far_first(n)) % NZ
        part = 2 * zd + b
        to = zd * NX + 2 * c + b
        away = jnp.logical_or(to != seq, job != mine)
        remote = (
            pltpu.make_async_remote_copy(
                ov.at[part], rv.at[head], vsend.at[part], vrecv.at[head], (job, to), MESH
            ),
            pltpu.make_async_remote_copy(
                ot.at[part], rt.at[head], tsend.at[part], trecv.at[head], (job, to), MESH
            ),
        )
        local = (
            pltpu.make_async_copy(ov.at[part], rv.at[head], vrecv.at[head]),
            pltpu.make_async_copy(ot.at[part], rt.at[head], trecv.at[head]),
        )
        return away, remote, local

    def start(n):
        for b in range(2):
            away, remote, local = copies(n, b)

            @pl.when(away)
            def _():
                for one in remote:
                    one.start()

            @pl.when(jnp.logical_not(away))
            def _():
                for one in local:
                    one.start()

    def step(n, carry):
        zd = (z + far_first(n)) % NZ
        rows = pl.ds(pl.multiple_of(zd * 512 + c * 256, 256), 256)
        ov[pl.ds(2 * zd, 2)] = block(q[rows, :]).reshape(2, 128, HD)

        @pl.when(n > 0)
        def _():
            start(n - 1)

        weights.middle(n)

        @pl.when(n + AHEAD < W_CHUNKS)
        def _():
            weights.send_own(n + AHEAD)

        @pl.when(n > 0)
        def _():
            weights.last(n - 1)

        return carry

    lax.fori_loop(0, NZ, step, 0)
    start(NZ - 1)
    weights.last(W_CHUNKS - 1)

    def finish(n, carry):
        pltpu.make_async_copy(ov.at[n], rv.at[n], vrecv.at[n]).wait()
        pltpu.make_async_copy(ot.at[n], rt.at[n], trecv.at[n]).wait()
        return carry

    lax.fori_loop(0, 16, finish, 0)

    def sent(n, carry):
        for b in range(2):
            away, remote, _ = copies(n, b)

            @pl.when(away)
            def _():
                for one in remote:
                    one.wait_send()

        return carry

    lax.fori_loop(0, NZ, sent, 0)
    lax.fori_loop(0, W_CHUNKS, lambda k, carry: (weights.side(k), carry)[1], 0)
    weights.finish()


def attend(counts, vid, txt, slots, w_out):
    bf = jnp.bfloat16
    vm = pl.BlockSpec(memory_space=pltpu.VMEM)
    half = (HD, w_out.shape[2])
    return pl.pallas_call(
        attend_kernel,
        out_shape=[
            jax.ShapeDtypeStruct((16, 128, HD), bf),
            jax.ShapeDtypeStruct((16, 3, 16, HD), bf),
            jax.ShapeDtypeStruct((N_JOB, *half), bf),
        ],
        in_specs=[pl.BlockSpec(memory_space=pltpu.SMEM), ANY, ANY, vm, ANY],
        out_specs=[ANY] * 3,
        scratch_shapes=[
            pltpu.VMEM((4096, HD), bf),
            pltpu.VMEM((4096, HD), bf),
            pltpu.VMEM((5, 256, HD), bf),
            pltpu.VMEM((4352, 2 * HD), bf),
            pltpu.VMEM((256, HD), bf),
            pltpu.VMEM((16, 128, HD), bf),
            pltpu.VMEM((16, 3, 16, HD), bf),
            DMA((5,)),
            DMA((16,)),
            DMA((16,)),
            DMA((16,)),
            DMA((16,)),
            pltpu.VMEM(half, bf),
            *gather_sems(W_CHUNKS),
        ],
        compiler_params=pltpu.CompilerParams(
            collective_id=6, has_side_effects=True, vmem_limit_bytes=56 << 20
        ),
        name="attend",
    )(counts, vid, txt, slots, w_out)


def body(
    video,
    text_cache,
    text_count,
    holder,
    text_splits,
    mod_shift,
    mod_scale,
    mod_gate,
    text_gain,
    refine_w,
    refine_bias,
    w_qkv,
    q_gain,
    k_gain,
    w_out,
):
    y, c, z, x = place()
    my_job = lax.axis_index("job")
    my_shard = lax.axis_index("seq")
    bf = jnp.bfloat16
    own_video = video[0]
    rvid, rtxt, w_even = project_all(
        holder,
        text_cache[0],
        own_video,
        refine_w,
        w_qkv.reshape(w_qkv.shape[0], -1),
        w_out,
        text_gain[None],
        refine_bias[None],
        mod_scale,
        mod_shift,
        q_gain,
        k_gain,
    )

    offsets = jnp.cumsum(text_splits, axis=1) - text_splits
    ids = jnp.arange(16, dtype=jnp.int32)
    where_to = offsets[:, :, None] + ids
    valid = (ids < text_splits[:, :, None]) & (where_to < text_count[:, None, None])
    where_to = jnp.where(valid, where_to, -1).reshape(8, NZ, NC, 2, 16)
    job_here = (z + NZ - 2 * y) % NZ
    slots = lax.dynamic_slice(where_to, (job_here, 0, c, 0, 0), (1, NZ, 1, 2, 16))
    rv, rt, w_odd = attend(text_count, rvid, rtxt, slots.reshape(256, 1), w_out)

    attended = jnp.concatenate([rv, rt[:, 0]], axis=1)
    attended = jnp.transpose(attended, (1, 0, 2)).reshape(144, 2048)
    f32 = jnp.float32
    projected = jnp.dot(
        attended[:, :1024], w_even.reshape(1024, -1), preferred_element_type=f32
    ) + jnp.dot(attended[:, 1024:], w_odd.reshape(1024, -1), preferred_element_type=f32)
    kept = jnp.concatenate([rt[:8, 1:], rt[8:, 1:2]], axis=1)
    kept = jnp.transpose(kept, (2, 0, 1, 3)).reshape(16, -1)
    own_rows = jnp.concatenate([own_video, kept], axis=0).astype(jnp.float32)
    gate = lax.dynamic_index_in_dim(mod_gate, my_job, 0, keepdims=True)
    result = (own_rows + gate * projected).astype(bf)
    ok = lax.dynamic_slice(valid, (my_job, my_shard, 0), (1, 1, 16)).reshape(16, 1)
    text_result = jnp.where(ok, result[128:], jnp.zeros_like(result[128:]))
    return (result[:128][None], text_result[None])


def solution(mesh):
    placed = (
        P("job", "seq", None),
        P("job", "seq", None),
        P(),
        P(),
        P(),
        P(),
        P(),
        P(),
        P(),
        P(None, "job"),
        P("job"),
        P(None, "job", None, None),
        P("job", None),
        P("job", None),
        P("job", None, None),
    )
    return jax.shard_map(
        body,
        mesh=mesh,
        in_specs=placed,
        out_specs=(P("job", "seq", None), P("job", "seq", None)),
        check_vma=False,
    )
```

```python
import functools

import jax
import jax.numpy as jnp
from jax import lax
from jax.experimental import pallas as pl
from jax.experimental.pallas import tpu as pltpu
from jax.sharding import PartitionSpec as P

HD = 128
NY, NC, NZ, NX = 4, 2, 8, 4
N_JOB = NY * NC
N_SEQ = NZ * NX
MESH = pl.DeviceIdType.MESH
epsilon = 1e-06
ANY = pl.BlockSpec(memory_space=pl.ANY)
DMA = pltpu.SemaphoreType.DMA


def rms_scale(values, gains):
    mean_square = jnp.mean(values * values, axis=-1, keepdims=True)
    return values * lax.rsqrt(mean_square + epsilon) * gains


def place():
    job = lax.axis_index("job")
    seq = lax.axis_index("seq")
    return job // NC, job % NC, seq // NX, seq % NX


def signal(job, seq):
    pl.semaphore_signal(
        pltpu.get_barrier_semaphore(), inc=1, device_id=(job, seq), device_id_type=MESH
    )


def near():
    y, c, z, x = place()
    seq = z * NX + x
    up = (((y + 1) % NY) * NC + c, seq)
    down = (((y + NY - 1) % NY) * NC + c, seq)
    other = (y * NC + 1 - c, seq)
    return up, down, other


def span(k, step):
    if isinstance(k, int):
        return pl.ds(k * step, step)
    return pl.ds(pl.multiple_of(k * step, step), step)


class JobGather:
    def __init__(self, src, dst, send, recv, local, rows, chunks, buf=None):
        self.src, self.dst, self.buf = src, dst, buf
        self.send, self.recv, self.local = send, recv, local
        self.step, self.chunks = rows // chunks, chunks

    def piece(self, k):
        return span(k, self.step)

    def copy(self, source, block, role, k, device):
        return pltpu.make_async_remote_copy(
            src_ref=source.at[self.piece(k)],
            dst_ref=self.dst.at[block, self.piece(k)],
            send_sem=self.send.at[role, k],
            recv_sem=self.recv.at[role, k],
            device_id=device,
            device_id_type=MESH,
        )

    def block(self, role):
        y, c, _, _ = place()
        return {
            0: ((y + NY - 1) % NY) * NC + c,
            1: ((y + 1) % NY) * NC + c,
            2: ((y + 2) % NY) * NC + c,
            3: y * NC + 1 - c,
            4: ((y + NY - 1) % NY) * NC + 1 - c,
            5: ((y + 1) % NY) * NC + 1 - c,
            6: ((y + 2) % NY) * NC + 1 - c,
        }[role]

    def own(self):
        y, c, _, _ = place()
        return y * NC + c

    def load(self):
        into = self.dst.at[self.own()] if self.buf is None else self.buf
        pltpu.make_async_copy(self.src, into, self.local.at[0]).start()

    def loaded(self):
        into = self.dst.at[self.own()] if self.buf is None else self.buf
        pltpu.make_async_copy(self.src, into, self.local.at[0]).wait()
        if self.buf is not None:
            pltpu.make_async_copy(self.buf, self.dst.at[self.own()], self.local.at[1]).start()

    def send_own(self, k):
        up, down, other = near()
        own = self.own()
        self.copy(self.src, own, 0, k, up).start()
        self.copy(self.src, own, 1, k, down).start()
        self.copy(self.src, own, 3, k, other).start()

    def arrived(self, role, k):
        block = self.block(role)
        self.copy(self.dst.at[block], block, role, k, near()[2]).wait_recv()

    def handon(self, role, k):
        block = self.block(role)
        self.copy(self.dst.at[block], block, role + 4, k, near()[2]).start()

    def middle(self, k):
        y, c, _, _ = place()
        up, down, other = near()
        self.arrived(0, k)

        @pl.when(c == 0)
        def _():
            self.copy(self.dst.at[self.block(0)], self.block(0), 2, k, up).start()

        self.handon(0, k)
        self.arrived(1, k)

        @pl.when(c == 1)
        def _():
            self.copy(self.dst.at[self.block(1)], self.block(1), 2, k, down).start()

        self.handon(1, k)

    def last(self, k):
        self.arrived(2, k)
        self.handon(2, k)

    def side(self, k):
        for role in (3, 4, 5, 6):
            self.arrived(role, k)

    def finish(self):
        own = self.own()
        other = near()[2]

        def go(k, carry):
            for role in range(7):
                self.copy(self.src, own, role, k, other).wait_send()
            return carry

        lax.fori_loop(0, self.chunks, go, 0)
        if self.buf is not None:
            pltpu.make_async_copy(self.buf, self.dst.at[own], self.local.at[1]).wait()


def gather_sems(chunks):
    return [DMA((7, chunks)), DMA((7, chunks)), DMA((2,))]


def far_first(n):
    return 4 + ((n + 1) // 2) * (1 - 2 * (n % 2))


W_CHUNKS = 8
AHEAD = 4
V_CHUNKS = 4
V_ROWS = 128 // V_CHUNKS


def project_kernel(
    holder, raw, video, refine_w, w_qkv, w_out, gain, bias, scale, shift, q_gain, k_gain,
    rvid, rtxt, w_all,
    raw_all, video_all, refined, refined_all, wr, wq, normed, modded, text_rows, svid, stxt, buf,
    loads, rsend, rrecv, rlocal, fsend, frecv, flocal, isend, irecv, ilocal,
    wsend, wrecv, wlocal, vsend, vrecv, tsend, trecv,
):
    y, c, z, x = place()
    seq = z * NX + x
    f32, bf = jnp.float32, jnp.bfloat16
    other = near()[2]
    here = (x // 2 == c).astype(jnp.int32)
    peer_job = y * NC + x // 2
    text = JobGather(raw, raw_all, rsend, rrecv, rlocal, 8, 1)
    frames = JobGather(video, video_all, fsend, frecv, flocal, 128, V_CHUNKS)
    inner = JobGather(refined, refined_all, isend, irecv, ilocal, 64, 1)
    weights = JobGather(w_out.at[0], w_all, wsend, wrecv, wlocal, HD, W_CHUNKS, buf)
    text.load()
    frames.load()
    load_r = pltpu.make_async_copy(refine_w, wr, loads.at[0])
    load_q = [
        pltpu.make_async_copy(
            w_qkv.at[part, hl], wq.at[:, pl.ds((hl * 3 + part) * HD, HD)], loads.at[1 + 2 * part + hl]
        )
        for part in range(3)
        for hl in range(2)
    ]
    load_r.start()
    for one in load_q:
        one.start()

    def greet(n, carry):
        for hl in range(2):
            to = n * NX + 2 * c + hl

            @pl.when(jnp.logical_or(to != seq, here == 0))
            def _():
                signal(peer_job, to)

        return carry

    lax.fori_loop(0, NZ, greet, 0)
    for device in near():
        signal(*device)
    pl.semaphore_wait(pltpu.get_barrier_semaphore(), 19 - here)

    text.send_own(0)
    for k in range(3):
        frames.send_own(k)
    text.middle(0)
    text.last(0)
    frames.middle(0)
    frames.send_own(3)
    text.side(0)
    text.loaded()
    for j in range(N_JOB):
        rows = raw_all[holder[j]].astype(f32)
        normed[pl.ds(8 * j, 8)] = rms_scale(rows, gain[...])
    load_r.wait()
    lifted = jnp.dot(normed[...].astype(bf), wr[...], preferred_element_type=f32)
    refined[...] = (lifted + bias[...]).astype(bf)
    inner_own = pltpu.make_async_copy(refined, refined_all.at[inner.own()], ilocal.at[0])

    def vrows(shard, k):
        first = pl.multiple_of(shard * 128 + k * V_ROWS, V_ROWS)
        return rvid.at[:, pl.ds(first, V_ROWS), :]

    def trows(shard):
        return rtxt.at[:, pl.ds(pl.multiple_of(shard * 8, 8), 8), :]

    slot = 2 * z + x % 2

    def target(n, hl):
        zd = (z + far_first(n)) % NZ
        j = (zd + NZ - 2 * y) % NZ
        to = zd * NX + 2 * c + hl
        return 2 * j + hl, to, jnp.logical_or(to != seq, here == 0)

    def vcopy(n, hl, k):
        pair, to, away = target(n, hl)
        source = svid.at[pair, :, span(k, V_ROWS), :]
        remote = pltpu.make_async_remote_copy(
            source, vrows(seq, k), vsend.at[2 * n + hl, k], vrecv.at[slot, k],
            (peer_job, to), MESH,
        )
        return away, remote, pltpu.make_async_copy(source, vrows(seq, k), vrecv.at[slot, k])

    def tcopy(n, hl):
        pair, to, away = target(n, hl)
        remote = pltpu.make_async_remote_copy(
            stxt.at[pair], trows(seq), tsend.at[2 * n + hl], trecv.at[slot], (peer_job, to), MESH
        )
        return away, remote, pltpu.make_async_copy(stxt.at[pair], trows(seq), trecv.at[slot])

    def launch(make):
        def go(n, carry):
            for hl in range(2):
                away, remote, local = make(n, hl)

                @pl.when(away)
                def _():
                    remote.start()

                @pl.when(jnp.logical_not(away))
                def _():
                    local.start()

            return carry

        lax.fori_loop(0, NZ, go, 0)

    def drained(make):
        def go(n, carry):
            for hl in range(2):
                away, remote, _ = make(n, hl)

                @pl.when(away)
                def _():
                    remote.wait_send()

            return carry

        lax.fori_loop(0, NZ, go, 0)

    def vhand(shard, index, k):
        return pltpu.make_async_remote_copy(
            vrows(shard, k), vrows(shard, k), vsend.at[index, k], vrecv.at[index, k], other, MESH
        )

    def thand(shard, index):
        return pltpu.make_async_remote_copy(
            trows(shard), trows(shard), tsend.at[index], trecv.at[index], other, MESH
        )

    def sources(n):
        zs = (z + NZ - far_first(n)) % NZ
        return [(zs * NX + 2 * c + b, 2 * zs + b) for b in range(2)]

    def take(k):
        def go(n, carry):
            for shard, index in sources(n):
                vhand(shard, index, k).wait_recv()
                vhand(shard, index + 16, k).start()
            return carry

        lax.fori_loop(0, NZ, go, 0)

    def normalise(rows, j):
        centre = jnp.mean(rows, axis=-1, keepdims=True)
        moved = rows - centre
        spread_sq = jnp.mean(moved * moved, axis=-1, keepdims=True)
        out = moved * lax.rsqrt(spread_sq + epsilon)
        return (out * (1.0 + scale[pl.ds(j, 1), :]) + shift[pl.ds(j, 1), :]).astype(bf)

    def project(rows):
        got = jnp.dot(rows, wq[...], preferred_element_type=f32)
        out = []
        for hl in range(2):
            for part in range(3):
                piece = got[:, (hl * 3 + part) * HD : (hl * 3 + part + 1) * HD]
                if part == 0:
                    piece = rms_scale(piece, q_gain[pl.ds(hl, 1), :])
                if part == 1:
                    piece = rms_scale(piece, k_gain[pl.ds(hl, 1), :])
                out.append(piece.astype(bf))
        return out

    frames.loaded()

    def round_(k, carry):
        @pl.when(k + 1 < V_CHUNKS)
        def _():
            frames.middle(k + 1)

        @pl.when(k == 0)
        def _():
            inner_own.start()
            inner.send_own(0)
            for one in load_q:
                one.wait()

        @pl.when(k == 1)
        def _():
            inner.middle(0)
            inner.last(0)

        @pl.when(k == 2)
        def _():
            for ahead in range(AHEAD):
                weights.send_own(ahead)

        frames.last(k)
        frames.side(k)

        @pl.when(k > 0)
        def _():
            launch(lambda n, hl: vcopy(n, hl, k - 1))

        rows_k = span(k, V_ROWS)
        for j in range(N_JOB):
            modded[pl.ds(V_ROWS * j, V_ROWS)] = normalise(video_all[j, rows_k, :].astype(f32), j)
        for i, piece in enumerate(project(modded[...])):
            for j in range(N_JOB):
                svid[2 * j + i // 3, i % 3, rows_k, :] = piece[V_ROWS * j : V_ROWS * (j + 1)]

        @pl.when(k >= 2)
        def _():
            take(k - 2)

        return carry

    weights.load()
    lax.fori_loop(0, V_CHUNKS, round_, 0)
    inner.side(0)
    inner_own.wait()
    for g in range(N_JOB):
        text_rows[:, 384 * g : 384 * (g + 1)] = refined_all[g].astype(f32)
    for j in range(N_JOB):
        normed[pl.ds(8 * j, 8), 0:3072] = normalise(text_rows[pl.ds(8 * j, 8)], j).astype(f32)
    launch(lambda n, hl: vcopy(n, hl, V_CHUNKS - 1))
    for i, piece in enumerate(project(normed[:, 0:3072].astype(bf))):
        for j in range(N_JOB):
            stxt[2 * j + i // 3, i % 3] = piece[8 * j : 8 * (j + 1)]
    for j in range(N_JOB):
        for group in range(4):
            at = min(group, 2) * HD
            stxt[2 * j + group // 2, 3 + group % 2] = refined[8 * j : 8 * (j + 1), at : at + HD]
    weights.loaded()
    take(V_CHUNKS - 2)
    launch(tcopy)

    def rest(n, carry):
        weights.middle(n)

        @pl.when(n + AHEAD < W_CHUNKS)
        def _():
            weights.send_own(n + AHEAD)

        for shard, index in sources(n):
            vhand(shard, index, V_CHUNKS - 1).wait_recv()
            vhand(shard, index + 16, V_CHUNKS - 1).start()

        @pl.when(n > 0)
        def _():
            weights.last(n - 1)

        return carry

    lax.fori_loop(0, NZ, rest, 0)
    weights.last(W_CHUNKS - 1)

    def text_rest(n, carry):
        for shard, index in sources(n):
            thand(shard, index).wait_recv()
            thand(shard, index + 16).start()
        return carry

    lax.fori_loop(0, NZ, text_rest, 0)

    def finish(n, carry):
        for b in range(2):
            shard = n * NX + 2 * (1 - c) + b
            index = 2 * n + b + 16
            for k in range(V_CHUNKS):
                vhand(shard, index, k).wait_recv()
                vhand(shard, index, k).wait_send()
            thand(shard, index).wait_recv()
            thand(shard, index).wait_send()
        return carry

    lax.fori_loop(0, NZ, finish, 0)
    for k in range(V_CHUNKS):
        drained(lambda n, hl: vcopy(n, hl, k))
    drained(tcopy)
    lax.fori_loop(0, W_CHUNKS, lambda k, carry: (weights.side(k), carry)[1], 0)
    for one in (text, frames, inner, weights):
        one.finish()


def project_all(holder, raw, video, refine_w, w_qkv, w_out, *small):
    f32, bf = jnp.float32, jnp.bfloat16
    vm = pl.BlockSpec(memory_space=pltpu.VMEM)
    return pl.pallas_call(
        project_kernel,
        out_shape=[
            jax.ShapeDtypeStruct((3, N_SEQ * 128, HD), bf),
            jax.ShapeDtypeStruct((5, N_SEQ * 8, HD), bf),
            jax.ShapeDtypeStruct((N_JOB, *w_out.shape[1:]), bf),
        ],
        in_specs=[pl.BlockSpec(memory_space=pltpu.SMEM)] + [ANY] * 5 + [vm] * 6,
        out_specs=[ANY] * 3,
        scratch_shapes=[
            pltpu.VMEM((N_JOB, 8, 4096), bf),
            pltpu.VMEM((N_JOB, 128, 3072), bf),
            pltpu.VMEM((64, 384), bf),
            pltpu.VMEM((N_JOB, 64, 384), bf),
            pltpu.VMEM((4096, 384), bf),
            pltpu.VMEM((3072, 768), bf),
            pltpu.VMEM((64, 4096), f32),
            pltpu.VMEM((8 * V_ROWS, 3072), bf),
            pltpu.VMEM((64, 3072), f32),
            pltpu.VMEM((16, 3, 128, HD), bf),
            pltpu.VMEM((16, 5, 8, HD), bf),
            pltpu.VMEM(w_out.shape[1:], bf),
            DMA((7,)),
            *gather_sems(1),
            *gather_sems(V_CHUNKS),
            *gather_sems(1),
            *gather_sems(W_CHUNKS),
            DMA((32, V_CHUNKS)),
            DMA((32, V_CHUNKS)),
            DMA((32,)),
            DMA((32,)),
        ],
        compiler_params=pltpu.CompilerParams(
            collective_id=5, has_side_effects=True, vmem_limit_bytes=58 << 20
        ),
        name="project_all",
    )(holder, raw, video, refine_w, w_qkv, w_out, *small)


def attend_kernel(
    counts, splits, vid, txt, w_out, rv, rt, w_all,
    q, k, tx, vext, text_out, ov, ot, loads, vsend, vrecv, tsend, trecv, buf, wsend, wrecv, wlocal,
):
    y, c, z, x = place()
    seq = z * NX + x
    mine = y * NC + c
    job = (z + NZ - 2 * y) % NZ
    head = (x % 2) * 8 + 2 * y + x // 2
    incoming = [
        pltpu.make_async_copy(vid.at[0], q, loads.at[0]),
        pltpu.make_async_copy(vid.at[1], k, loads.at[1]),
        pltpu.make_async_copy(vid.at[2], vext.at[pl.ds(0, 4096), pl.ds(0, HD)], loads.at[2]),
        pltpu.make_async_copy(txt.at[2], vext.at[pl.ds(4096, 256), pl.ds(0, HD)], loads.at[3]),
        pltpu.make_async_copy(txt, tx, loads.at[4]),
    ]
    for one in incoming:
        one.start()

    def greet(n, carry):
        for b in range(NX):
            from_job = n * NC + x // 2
            from_seq = ((mine + 2 * n) % NZ) * NX + b

            @pl.when(jnp.logical_or(from_job != mine, from_seq != seq))
            def _():
                signal(from_job, from_seq)

        return carry

    lax.fori_loop(0, NY, greet, 0)
    for device in near():
        signal(*device)
    inside = jnp.logical_and(job == mine, x // 2 == c).astype(jnp.int32)
    pl.semaphore_wait(pltpu.get_barrier_semaphore(), 19 - inside)
    weights = JobGather(w_out.at[1], w_all, wsend, wrecv, wlocal, HD, W_CHUNKS, buf)
    weights.load()
    for ahead in range(AHEAD):
        weights.send_own(ahead)
    weights.loaded()

    count = counts[job]
    vext[:, HD:] = jnp.ones((4352, HD), jnp.bfloat16)
    for one in incoming:
        one.wait()
    factor = (HD**-0.5) * 1.4426950408889634
    contract = (((1,), (1,)), ((), ()))

    def block(part):
        sv = lax.dot_general(part, k[...], contract, preferred_element_type=jnp.float32)
        st = lax.dot_general(part, tx[1], contract, preferred_element_type=jnp.float32)
        st = jnp.where(lax.broadcasted_iota(jnp.int32, st.shape, 1) < count, st, -1e30)
        top = jnp.maximum(
            jnp.max(sv, axis=-1, keepdims=True), jnp.max(st, axis=-1, keepdims=True)
        )
        pv = jnp.exp2((sv - top) * factor).astype(jnp.bfloat16)
        pt = jnp.exp2((st - top) * factor).astype(jnp.bfloat16)
        both = jnp.dot(pv, vext[0:4096], preferred_element_type=jnp.float32)
        both += jnp.dot(pt, vext[4096:4352], preferred_element_type=jnp.float32)
        return (both[:, 0:HD] / both[:, HD:]).astype(jnp.bfloat16)

    text_out[...] = block(tx[0])
    across = lax.broadcasted_iota(jnp.int32, (16, 256), 1)
    down = lax.broadcasted_iota(jnp.int32, (16, 256), 0)
    base = jnp.int32(0)
    picks = []
    for zs in range(NZ):
        quad = [splits[job, NX * zs + i] for i in range(NX)]
        at = base + c * (quad[0] + quad[1])
        for b in range(2):
            length = quad[b] + c * (quad[2 + b] - quad[b])
            hit = (across == at + down) & (down < length) & (across < count)
            picks.append(jnp.where(hit, 1.0, 0.0).astype(jnp.bfloat16))
            at = at + length
        base = base + quad[0] + quad[1] + quad[2] + quad[3]
    pick = jnp.concatenate(picks, axis=0)
    for part in range(3):
        rows = text_out[...] if part == 0 else tx[part + 2]
        moved = jnp.dot(pick, rows, preferred_element_type=jnp.float32).astype(jnp.bfloat16)
        ot[:, part] = moved.reshape(16, 16, HD)

    def copies(n, b):
        zd = (z + far_first(n)) % NZ
        part = 2 * zd + b
        to = zd * NX + 2 * c + b
        away = jnp.logical_or(to != seq, job != mine)
        remote = (
            pltpu.make_async_remote_copy(
                ov.at[part], rv.at[head], vsend.at[part], vrecv.at[head], (job, to), MESH
            ),
            pltpu.make_async_remote_copy(
                ot.at[part], rt.at[head], tsend.at[part], trecv.at[head], (job, to), MESH
            ),
        )
        local = (
            pltpu.make_async_copy(ov.at[part], rv.at[head], vrecv.at[head]),
            pltpu.make_async_copy(ot.at[part], rt.at[head], trecv.at[head]),
        )
        return away, remote, local

    def start(n):
        for b in range(2):
            away, remote, local = copies(n, b)

            @pl.when(away)
            def _():
                for one in remote:
                    one.start()

            @pl.when(jnp.logical_not(away))
            def _():
                for one in local:
                    one.start()

    def relays(m):
        weights.middle(m)

        @pl.when(m + AHEAD < W_CHUNKS)
        def _():
            weights.send_own(m + AHEAD)

        @pl.when(m > 0)
        def _():
            weights.last(m - 1)

    def step(n, carry):
        rows = []
        for i in range(2):
            zd = (z + far_first(2 * n + i)) % NZ
            rows.append(q[pl.ds(pl.multiple_of(zd * 512 + c * 256, 256), 256), :])
        done = block(jnp.concatenate(rows, axis=0)).reshape(4, 128, HD)
        for i in range(2):
            zd = (z + far_first(2 * n + i)) % NZ
            ov[pl.ds(2 * zd, 2)] = done[2 * i : 2 * i + 2]

        @pl.when(n > 0)
        def _():
            start(2 * n - 2)
            start(2 * n - 1)

        relays(2 * n)
        relays(2 * n + 1)
        return carry

    lax.fori_loop(0, NZ // 2, step, 0)
    start(NZ - 2)
    start(NZ - 1)
    weights.last(W_CHUNKS - 1)

    def finish(n, carry):
        pltpu.make_async_copy(ov.at[n], rv.at[n], vrecv.at[n]).wait()
        pltpu.make_async_copy(ot.at[n], rt.at[n], trecv.at[n]).wait()
        return carry

    lax.fori_loop(0, 16, finish, 0)

    def sent(n, carry):
        for b in range(2):
            away, remote, _ = copies(n, b)

            @pl.when(away)
            def _():
                for one in remote:
                    one.wait_send()

        return carry

    lax.fori_loop(0, NZ, sent, 0)
    lax.fori_loop(0, W_CHUNKS, lambda k, carry: (weights.side(k), carry)[1], 0)
    weights.finish()


def attend(counts, splits, vid, txt, w_out):
    bf = jnp.bfloat16
    half = (HD, w_out.shape[2])
    return pl.pallas_call(
        attend_kernel,
        out_shape=[
            jax.ShapeDtypeStruct((16, 128, HD), bf),
            jax.ShapeDtypeStruct((16, 3, 16, HD), bf),
            jax.ShapeDtypeStruct((N_JOB, *half), bf),
        ],
        in_specs=[pl.BlockSpec(memory_space=pltpu.SMEM)] * 2 + [ANY] * 3,
        out_specs=[ANY] * 3,
        scratch_shapes=[
            pltpu.VMEM((4096, HD), bf),
            pltpu.VMEM((4096, HD), bf),
            pltpu.VMEM((5, 256, HD), bf),
            pltpu.VMEM((4352, 2 * HD), bf),
            pltpu.VMEM((256, HD), bf),
            pltpu.VMEM((16, 128, HD), bf),
            pltpu.VMEM((16, 3, 16, HD), bf),
            DMA((5,)),
            DMA((16,)),
            DMA((16,)),
            DMA((16,)),
            DMA((16,)),
            pltpu.VMEM(half, bf),
            *gather_sems(W_CHUNKS),
        ],
        compiler_params=pltpu.CompilerParams(
            collective_id=6, has_side_effects=True, vmem_limit_bytes=56 << 20
        ),
        name="attend",
    )(counts, splits, vid, txt, w_out)


def final_kernel(counts, splits, rv, rt, w_even, w_odd, video, gate, out, text_out):
    job, shard = lax.axis_index("job"), lax.axis_index("seq")
    f32, bf = jnp.float32, jnp.bfloat16
    total = None
    for g in range(N_JOB):
        rows = jnp.concatenate(
            [
                jnp.concatenate([rv[g], rv[8 + g]], axis=1),
                jnp.concatenate([rt[g, 0], rt[8 + g, 0]], axis=1),
            ],
            axis=0,
        )
        weight = jnp.concatenate([w_even[g], w_odd[g]], axis=0)
        part = jnp.dot(rows, weight, preferred_element_type=f32).astype(bf).astype(f32)
        total = part if total is None else total + part
    change = gate[pl.ds(job, 1), :] * total
    out[...] = (video[...].astype(f32) + change[:128]).astype(bf)
    kept = []
    for i in range(N_SPLIT // HD):
        group = pl.program_id(0) * (N_SPLIT // HD) + i
        g, third = group // 3, group % 3
        kept.append(rt[jnp.where(third == 2, 8 + g, g), jnp.where(third == 1, 2, 1)])
    text = (jnp.concatenate(kept, axis=1).astype(f32) + change[128:]).astype(bf)
    first = lax.fori_loop(0, shard, lambda i, sum_: sum_ + splits[job, i], jnp.int32(0))
    ids = lax.broadcasted_iota(jnp.int32, text.shape, 0)
    ok = (ids < splits[job, shard]) & (first + ids < counts[job])
    text_out[...] = jnp.where(ok, text, jnp.zeros_like(text))


N_SPLIT = 768


def final(counts, splits, rv, rt, w_even, w_odd, video, gate):
    bf = jnp.bfloat16
    smem = pl.BlockSpec(memory_space=pltpu.SMEM)
    width = video.shape[1]

    def whole(a):
        return pl.BlockSpec(a.shape, lambda n: (0,) * a.ndim)

    def cut(a):
        return pl.BlockSpec((*a.shape[:-1], N_SPLIT), lambda n: (0,) * (a.ndim - 1) + (n,))

    return pl.pallas_call(
        final_kernel,
        grid=(width // N_SPLIT,),
        out_shape=[
            jax.ShapeDtypeStruct((128, width), bf),
            jax.ShapeDtypeStruct((16, width), bf),
        ],
        in_specs=[smem, smem, whole(rv), whole(rt), cut(w_even), cut(w_odd), cut(video), cut(gate)],
        out_specs=[
            pl.BlockSpec((128, N_SPLIT), lambda n: (0, n)),
            pl.BlockSpec((16, N_SPLIT), lambda n: (0, n)),
        ],
        compiler_params=pltpu.CompilerParams(vmem_limit_bytes=48 << 20),
        name="final",
    )(counts, splits, rv, rt, w_even, w_odd, video, gate)


def body(
    video,
    text_cache,
    text_count,
    holder,
    text_splits,
    mod_shift,
    mod_scale,
    mod_gate,
    text_gain,
    refine_w,
    refine_bias,
    w_qkv,
    q_gain,
    k_gain,
    w_out,
):
    own_video = video[0]
    rvid, rtxt, w_even = project_all(
        holder,
        text_cache[0],
        own_video,
        refine_w,
        jnp.transpose(w_qkv, (2, 1, 0, 3)),
        w_out,
        text_gain[None],
        refine_bias[None],
        mod_scale,
        mod_shift,
        q_gain,
        k_gain,
    )

    rv, rt, w_odd = attend(text_count, text_splits, rvid, rtxt, w_out)
    out, text_out = final(text_count, text_splits, rv, rt, w_even, w_odd, own_video, mod_gate)
    return out[None], text_out[None]


def solution(mesh):
    placed = (
        P("job", "seq", None),
        P("job", "seq", None),
        P(),
        P(),
        P(),
        P(),
        P(),
        P(),
        P(),
        P(None, "job"),
        P("job"),
        P(None, "job", None, None),
        P("job", None),
        P("job", None),
        P("job", None, None),
    )
    return jax.shard_map(
        body,
        mesh=mesh,
        in_specs=placed,
        out_specs=(P("job", "seq", None), P("job", "seq", None)),
        check_vma=False,
    )
```

```python
import functools

import jax
import jax.numpy as jnp
from jax import lax
from jax.experimental import pallas as pl
from jax.experimental.pallas import tpu as pltpu
from jax.sharding import PartitionSpec as P

HD = 128
NY, NC, NZ, NX = 4, 2, 8, 4
N_JOB = NY * NC
N_SEQ = NZ * NX
MESH = pl.DeviceIdType.MESH
epsilon = 1e-06
ANY = pl.BlockSpec(memory_space=pl.ANY)
DMA = pltpu.SemaphoreType.DMA


def rms_scale(values, gains):
    mean_square = jnp.mean(values * values, axis=-1, keepdims=True)
    return values * lax.rsqrt(mean_square + epsilon) * gains


def place():
    job = lax.axis_index("job")
    seq = lax.axis_index("seq")
    return job // NC, job % NC, seq // NX, seq % NX


def signal(job, seq):
    pl.semaphore_signal(
        pltpu.get_barrier_semaphore(), inc=1, device_id=(job, seq), device_id_type=MESH
    )


def near():
    y, c, z, x = place()
    seq = z * NX + x
    up = (((y + 1) % NY) * NC + c, seq)
    down = (((y + NY - 1) % NY) * NC + c, seq)
    other = (y * NC + 1 - c, seq)
    return up, down, other


def span(k, step):
    if isinstance(k, int):
        return pl.ds(k * step, step)
    return pl.ds(pl.multiple_of(k * step, step), step)


class JobGather:
    def __init__(self, src, dst, send, recv, local, rows, chunks, buf=None):
        self.src, self.dst, self.buf = src, dst, buf
        self.send, self.recv, self.local = send, recv, local
        self.step, self.chunks = rows // chunks, chunks

    def piece(self, k):
        return span(k, self.step)

    def copy(self, source, block, role, k, device):
        return pltpu.make_async_remote_copy(
            src_ref=source.at[self.piece(k)],
            dst_ref=self.dst.at[block, self.piece(k)],
            send_sem=self.send.at[role, k],
            recv_sem=self.recv.at[role, k],
            device_id=device,
            device_id_type=MESH,
        )

    def block(self, role):
        y, c, _, _ = place()
        return {
            0: ((y + NY - 1) % NY) * NC + c,
            1: ((y + 1) % NY) * NC + c,
            2: ((y + 2) % NY) * NC + c,
            3: y * NC + 1 - c,
            4: ((y + NY - 1) % NY) * NC + 1 - c,
            5: ((y + 1) % NY) * NC + 1 - c,
            6: ((y + 2) % NY) * NC + 1 - c,
        }[role]

    def own(self):
        y, c, _, _ = place()
        return y * NC + c

    def load(self):
        into = self.dst.at[self.own()] if self.buf is None else self.buf
        pltpu.make_async_copy(self.src, into, self.local.at[0]).start()

    def loaded(self):
        into = self.dst.at[self.own()] if self.buf is None else self.buf
        pltpu.make_async_copy(self.src, into, self.local.at[0]).wait()
        if self.buf is not None:
            pltpu.make_async_copy(self.buf, self.dst.at[self.own()], self.local.at[1]).start()

    def send_own(self, k):
        up, down, other = near()
        own = self.own()
        self.copy(self.src, own, 0, k, up).start()
        self.copy(self.src, own, 1, k, down).start()
        self.copy(self.src, own, 3, k, other).start()

    def arrived(self, role, k):
        block = self.block(role)
        self.copy(self.dst.at[block], block, role, k, near()[2]).wait_recv()

    def handon(self, role, k):
        block = self.block(role)
        self.copy(self.dst.at[block], block, role + 4, k, near()[2]).start()

    def middle(self, k):
        y, c, _, _ = place()
        up, down, other = near()
        self.arrived(0, k)

        @pl.when(c == 0)
        def _():
            self.copy(self.dst.at[self.block(0)], self.block(0), 2, k, up).start()

        self.handon(0, k)
        self.arrived(1, k)

        @pl.when(c == 1)
        def _():
            self.copy(self.dst.at[self.block(1)], self.block(1), 2, k, down).start()

        self.handon(1, k)

    def last(self, k):
        self.arrived(2, k)
        self.handon(2, k)

    def side(self, k):
        for role in (3, 4, 5, 6):
            self.arrived(role, k)

    def finish(self):
        own = self.own()
        other = near()[2]

        def go(k, carry):
            for role in range(7):
                self.copy(self.src, own, role, k, other).wait_send()
            return carry

        lax.fori_loop(0, self.chunks, go, 0)
        if self.buf is not None:
            pltpu.make_async_copy(self.buf, self.dst.at[own], self.local.at[1]).wait()


def gather_sems(chunks):
    return [DMA((7, chunks)), DMA((7, chunks)), DMA((2,))]


def far_first(n):
    return 4 + ((n + 1) // 2) * (1 - 2 * (n % 2))


W_CHUNKS = 8
AHEAD = 4
W_FIRST = 192
W_REST = 2 * HD - W_FIRST
R_CHUNKS = 4
V_CHUNKS = 4
V_ROWS = 128 // V_CHUNKS


def project_kernel(
    holder, raw, video, refine_w, w_qkv, w_out, gain, bias, scale, shift, q_gain, k_gain,
    rvid, rtxt, w_all,
    raw_all, video_all, refined, refined_all, wr, wq, normed, modded, text_rows, svid, stxt, buf,
    loads, rsend, rrecv, rlocal, fsend, frecv, flocal, isend, irecv, ilocal,
    wsend, wrecv, wlocal, vsend, vrecv, tsend, trecv,
):
    y, c, z, x = place()
    seq = z * NX + x
    f32, bf = jnp.float32, jnp.bfloat16
    other = near()[2]
    here = (x // 2 == c).astype(jnp.int32)
    peer_job = y * NC + x // 2
    text = JobGather(raw, raw_all, rsend, rrecv, rlocal, 8, 1)
    frames = JobGather(video, video_all, fsend, frecv, flocal, 128, V_CHUNKS)
    inner = JobGather(refined, refined_all, isend, irecv, ilocal, 64, 1)
    weights = JobGather(
        w_out.at[pl.ds(0, W_FIRST)], w_all, wsend, wrecv, wlocal, W_FIRST, W_CHUNKS, buf
    )
    text.load()
    frames.load()
    load_r = pltpu.make_async_copy(refine_w, wr, loads.at[0])
    load_q = [
        pltpu.make_async_copy(
            w_qkv.at[part, hl], wq.at[:, pl.ds((hl * 3 + part) * HD, HD)], loads.at[1 + 2 * part + hl]
        )
        for part in range(3)
        for hl in range(2)
    ]
    load_r.start()
    for one in load_q:
        one.start()

    def greet(n, carry):
        for hl in range(2):
            to = n * NX + 2 * c + hl

            @pl.when(jnp.logical_or(to != seq, here == 0))
            def _():
                signal(peer_job, to)

        return carry

    lax.fori_loop(0, NZ, greet, 0)
    for device in near():
        signal(*device)
    pl.semaphore_wait(pltpu.get_barrier_semaphore(), 19 - here)

    text.send_own(0)
    for k in range(2):
        frames.send_own(k)

    def refine():
        for j in range(N_JOB):
            rows = raw_all[holder[j]].astype(f32)
            normed[pl.ds(8 * j, 8)] = rms_scale(rows, gain[...])
        lifted = jnp.dot(normed[...].astype(bf), wr[...], preferred_element_type=f32)
        refined[...] = (lifted + bias[...]).astype(bf)

    inner_own = pltpu.make_async_copy(refined, refined_all.at[inner.own()], ilocal.at[0])

    def vrows(shard, k):
        first = pl.multiple_of(shard * 128 + k * V_ROWS, V_ROWS)
        return rvid.at[:, pl.ds(first, V_ROWS), :]

    def trows(shard):
        return rtxt.at[:, pl.ds(pl.multiple_of(shard * 8, 8), 8), :]

    slot = 2 * z + x % 2

    def target(n, hl):
        zd = (z + far_first(n)) % NZ
        j = (zd + NZ - 2 * y) % NZ
        to = zd * NX + 2 * c + hl
        return 2 * j + hl, to, jnp.logical_or(to != seq, here == 0)

    def vcopy(n, hl, k):
        pair, to, away = target(n, hl)
        source = svid.at[pair, :, span(k, V_ROWS), :]
        remote = pltpu.make_async_remote_copy(
            source, vrows(seq, k), vsend.at[2 * n + hl, k], vrecv.at[slot, k],
            (peer_job, to), MESH,
        )
        return away, remote, pltpu.make_async_copy(source, vrows(seq, k), vrecv.at[slot, k])

    def tcopy(n, hl):
        pair, to, away = target(n, hl)
        remote = pltpu.make_async_remote_copy(
            stxt.at[pair], trows(seq), tsend.at[2 * n + hl], trecv.at[slot], (peer_job, to), MESH
        )
        return away, remote, pltpu.make_async_copy(stxt.at[pair], trows(seq), trecv.at[slot])

    def launch(make):
        def go(n, carry):
            for hl in range(2):
                away, remote, local = make(n, hl)

                @pl.when(away)
                def _():
                    remote.start()

                @pl.when(jnp.logical_not(away))
                def _():
                    local.start()

            return carry

        lax.fori_loop(0, NZ, go, 0)

    def drained(make):
        def go(n, carry):
            for hl in range(2):
                away, remote, _ = make(n, hl)

                @pl.when(away)
                def _():
                    remote.wait_send()

            return carry

        lax.fori_loop(0, NZ, go, 0)

    def vhand(shard, index, k):
        return pltpu.make_async_remote_copy(
            vrows(shard, k), vrows(shard, k), vsend.at[index, k], vrecv.at[index, k], other, MESH
        )

    def thand(shard, index):
        return pltpu.make_async_remote_copy(
            trows(shard), trows(shard), tsend.at[index], trecv.at[index], other, MESH
        )

    def sources(n):
        zs = (z + NZ - far_first(n)) % NZ
        return [(zs * NX + 2 * c + b, 2 * zs + b) for b in range(2)]

    def take(k):
        def go(n, carry):
            for shard, index in sources(n):
                vhand(shard, index, k).wait_recv()
                vhand(shard, index + 16, k).start()
            return carry

        lax.fori_loop(0, NZ, go, 0)

    def normalise(rows, j):
        centre = jnp.mean(rows, axis=-1, keepdims=True)
        moved = rows - centre
        spread_sq = jnp.mean(moved * moved, axis=-1, keepdims=True)
        out = moved * lax.rsqrt(spread_sq + epsilon)
        return (out * (1.0 + scale[pl.ds(j, 1), :]) + shift[pl.ds(j, 1), :]).astype(bf)

    def project(rows):
        got = jnp.dot(rows, wq[...], preferred_element_type=f32)
        out = []
        for hl in range(2):
            for part in range(3):
                piece = got[:, (hl * 3 + part) * HD : (hl * 3 + part + 1) * HD]
                if part == 0:
                    piece = rms_scale(piece, q_gain[pl.ds(hl, 1), :])
                if part == 1:
                    piece = rms_scale(piece, k_gain[pl.ds(hl, 1), :])
                out.append(piece.astype(bf))
        return out

    frames.loaded()
    frames.middle(0)
    frames.send_own(2)
    text.middle(0)
    text.loaded()

    def round_(k, carry):
        @pl.when(k + 1 < V_CHUNKS)
        def _():
            frames.middle(k + 1)

        @pl.when(k == 0)
        def _():
            frames.send_own(3)
            text.last(0)
            for one in load_q:
                one.wait()

        @pl.when(k == 2)
        def _():
            inner_own.start()
            inner.send_own(0)
            for ahead in range(AHEAD):
                weights.send_own(ahead)

        @pl.when(k == 3)
        def _():
            inner.middle(0)
            inner.last(0)

        frames.last(k)
        frames.side(k)

        @pl.when(k > 0)
        def _():
            launch(lambda n, hl: vcopy(n, hl, k - 1))

        rows_k = span(k, V_ROWS)
        for j in range(N_JOB):
            modded[pl.ds(V_ROWS * j, V_ROWS)] = normalise(video_all[j, rows_k, :].astype(f32), j)
        for i, piece in enumerate(project(modded[...])):
            for j in range(N_JOB):
                svid[2 * j + i // 3, i % 3, rows_k, :] = piece[V_ROWS * j : V_ROWS * (j + 1)]

        @pl.when(k == 1)
        def _():
            text.side(0)
            load_r.wait()
            refine()

        @pl.when(k >= 2)
        def _():
            take(k - 2)

        return carry

    weights.load()
    lax.fori_loop(0, V_CHUNKS, round_, 0)
    inner.side(0)
    inner_own.wait()
    for g in range(N_JOB):
        text_rows[:, 384 * g : 384 * (g + 1)] = refined_all[g].astype(f32)
    for j in range(N_JOB):
        normed[pl.ds(8 * j, 8), 0:3072] = normalise(text_rows[pl.ds(8 * j, 8)], j).astype(f32)
    launch(lambda n, hl: vcopy(n, hl, V_CHUNKS - 1))
    for i, piece in enumerate(project(normed[:, 0:3072].astype(bf))):
        for j in range(N_JOB):
            stxt[2 * j + i // 3, i % 3] = piece[8 * j : 8 * (j + 1)]
    for j in range(N_JOB):
        for group in range(4):
            at = min(group, 2) * HD
            stxt[2 * j + group // 2, 3 + group % 2] = refined[8 * j : 8 * (j + 1), at : at + HD]
    weights.loaded()
    take(V_CHUNKS - 2)
    launch(tcopy)

    def rest(n, carry):
        weights.middle(n)

        @pl.when(n + AHEAD < W_CHUNKS)
        def _():
            weights.send_own(n + AHEAD)

        for shard, index in sources(n):
            vhand(shard, index, V_CHUNKS - 1).wait_recv()
            vhand(shard, index + 16, V_CHUNKS - 1).start()

        @pl.when(n > 0)
        def _():
            weights.last(n - 1)

        return carry

    lax.fori_loop(0, NZ, rest, 0)
    weights.last(W_CHUNKS - 1)

    def text_rest(n, carry):
        for shard, index in sources(n):
            thand(shard, index).wait_recv()
            thand(shard, index + 16).start()
        return carry

    lax.fori_loop(0, NZ, text_rest, 0)

    def finish(n, carry):
        for b in range(2):
            shard = n * NX + 2 * (1 - c) + b
            index = 2 * n + b + 16
            for k in range(V_CHUNKS):
                vhand(shard, index, k).wait_recv()
                vhand(shard, index, k).wait_send()
            thand(shard, index).wait_recv()
            thand(shard, index).wait_send()
        return carry

    lax.fori_loop(0, NZ, finish, 0)
    for k in range(V_CHUNKS):
        drained(lambda n, hl: vcopy(n, hl, k))
    drained(tcopy)
    lax.fori_loop(0, W_CHUNKS, lambda k, carry: (weights.side(k), carry)[1], 0)
    for one in (text, frames, inner, weights):
        one.finish()


def project_all(holder, raw, video, refine_w, w_qkv, w_out, *small):
    f32, bf = jnp.float32, jnp.bfloat16
    vm = pl.BlockSpec(memory_space=pltpu.VMEM)
    return pl.pallas_call(
        project_kernel,
        out_shape=[
            jax.ShapeDtypeStruct((3, N_SEQ * 128, HD), bf),
            jax.ShapeDtypeStruct((5, N_SEQ * 8, HD), bf),
            jax.ShapeDtypeStruct((N_JOB, W_FIRST, w_out.shape[1]), bf),
        ],
        in_specs=[pl.BlockSpec(memory_space=pltpu.SMEM)] + [ANY] * 5 + [vm] * 6,
        out_specs=[ANY] * 3,
        scratch_shapes=[
            pltpu.VMEM((N_JOB, 8, 4096), bf),
            pltpu.VMEM((N_JOB, 128, 3072), bf),
            pltpu.VMEM((64, 384), bf),
            pltpu.VMEM((N_JOB, 64, 384), bf),
            pltpu.VMEM((4096, 384), bf),
            pltpu.VMEM((3072, 768), bf),
            pltpu.VMEM((64, 4096), f32),
            pltpu.VMEM((8 * V_ROWS, 3072), bf),
            pltpu.VMEM((64, 3072), f32),
            pltpu.VMEM((16, 3, 128, HD), bf),
            pltpu.VMEM((16, 5, 8, HD), bf),
            pltpu.VMEM((W_FIRST, w_out.shape[1]), bf),
            DMA((7,)),
            *gather_sems(1),
            *gather_sems(V_CHUNKS),
            *gather_sems(1),
            *gather_sems(W_CHUNKS),
            DMA((32, V_CHUNKS)),
            DMA((32, V_CHUNKS)),
            DMA((32,)),
            DMA((32,)),
        ],
        compiler_params=pltpu.CompilerParams(
            collective_id=5, has_side_effects=True, vmem_limit_bytes=58 << 20
        ),
        name="project_all",
    )(holder, raw, video, refine_w, w_qkv, w_out, *small)


def attend_kernel(
    counts, splits, vid, txt, w_out, rv, rt, w_all,
    q, k, tx, vext, text_out, ov, ot, loads, vsend, vrecv, tsend, trecv, buf, wsend, wrecv, wlocal,
):
    y, c, z, x = place()
    seq = z * NX + x
    mine = y * NC + c
    job = (z + NZ - 2 * y) % NZ
    head = (x % 2) * 8 + 2 * y + x // 2
    incoming = [
        pltpu.make_async_copy(vid.at[0], q, loads.at[0]),
        pltpu.make_async_copy(vid.at[1], k, loads.at[1]),
        pltpu.make_async_copy(vid.at[2], vext.at[pl.ds(0, 4096), pl.ds(0, HD)], loads.at[2]),
        pltpu.make_async_copy(txt.at[2], vext.at[pl.ds(4096, 256), pl.ds(0, HD)], loads.at[3]),
        pltpu.make_async_copy(txt, tx, loads.at[4]),
    ]
    for one in incoming:
        one.start()

    def greet(n, carry):
        for b in range(NX):
            from_job = n * NC + x // 2
            from_seq = ((mine + 2 * n) % NZ) * NX + b

            @pl.when(jnp.logical_or(from_job != mine, from_seq != seq))
            def _():
                signal(from_job, from_seq)

        return carry

    lax.fori_loop(0, NY, greet, 0)
    for device in near():
        signal(*device)
    inside = jnp.logical_and(job == mine, x // 2 == c).astype(jnp.int32)
    pl.semaphore_wait(pltpu.get_barrier_semaphore(), 19 - inside)
    weights = JobGather(
        w_out.at[pl.ds(W_FIRST, W_REST)], w_all, wsend, wrecv, wlocal, W_REST, R_CHUNKS, buf
    )
    weights.load()
    for ahead in range(R_CHUNKS):
        weights.send_own(ahead)
    weights.loaded()

    count = counts[job]
    vext[:, HD:] = jnp.ones((4352, HD), jnp.bfloat16)
    for one in incoming:
        one.wait()
    factor = (HD**-0.5) * 1.4426950408889634
    contract = (((1,), (1,)), ((), ()))

    def block(part):
        sv = lax.dot_general(part, k[...], contract, preferred_element_type=jnp.float32)
        st = lax.dot_general(part, tx[1], contract, preferred_element_type=jnp.float32)
        st = jnp.where(lax.broadcasted_iota(jnp.int32, st.shape, 1) < count, st, -1e30)
        top = jnp.maximum(
            jnp.max(sv, axis=-1, keepdims=True), jnp.max(st, axis=-1, keepdims=True)
        )
        pv = jnp.exp2((sv - top) * factor).astype(jnp.bfloat16)
        pt = jnp.exp2((st - top) * factor).astype(jnp.bfloat16)
        both = jnp.dot(pv, vext[0:4096], preferred_element_type=jnp.float32)
        both += jnp.dot(pt, vext[4096:4352], preferred_element_type=jnp.float32)
        return (both[:, 0:HD] / both[:, HD:]).astype(jnp.bfloat16)

    text_out[...] = block(tx[0])
    across = lax.broadcasted_iota(jnp.int32, (16, 256), 1)
    down = lax.broadcasted_iota(jnp.int32, (16, 256), 0)
    base = jnp.int32(0)
    picks = []
    for zs in range(NZ):
        quad = [splits[job, NX * zs + i] for i in range(NX)]
        at = base + c * (quad[0] + quad[1])
        for b in range(2):
            length = quad[b] + c * (quad[2 + b] - quad[b])
            hit = (across == at + down) & (down < length) & (across < count)
            picks.append(jnp.where(hit, 1.0, 0.0).astype(jnp.bfloat16))
            at = at + length
        base = base + quad[0] + quad[1] + quad[2] + quad[3]
    pick = jnp.concatenate(picks, axis=0)
    for part in range(3):
        rows = text_out[...] if part == 0 else tx[part + 2]
        moved = jnp.dot(pick, rows, preferred_element_type=jnp.float32).astype(jnp.bfloat16)
        ot[:, part] = moved.reshape(16, 16, HD)

    def copies(n, b):
        zd = (z + far_first(n)) % NZ
        part = 2 * zd + b
        to = zd * NX + 2 * c + b
        away = jnp.logical_or(to != seq, job != mine)
        remote = (
            pltpu.make_async_remote_copy(
                ov.at[part], rv.at[head], vsend.at[part], vrecv.at[head], (job, to), MESH
            ),
            pltpu.make_async_remote_copy(
                ot.at[part], rt.at[head], tsend.at[part], trecv.at[head], (job, to), MESH
            ),
        )
        local = (
            pltpu.make_async_copy(ov.at[part], rv.at[head], vrecv.at[head]),
            pltpu.make_async_copy(ot.at[part], rt.at[head], trecv.at[head]),
        )
        return away, remote, local

    def start(n):
        for b in range(2):
            away, remote, local = copies(n, b)

            @pl.when(away)
            def _():
                for one in remote:
                    one.start()

            @pl.when(jnp.logical_not(away))
            def _():
                for one in local:
                    one.start()

    weights.middle(0)

    def step(n, carry):
        rows = []
        for i in range(2):
            zd = (z + far_first(2 * n + i)) % NZ
            rows.append(q[pl.ds(pl.multiple_of(zd * 512 + c * 256, 256), 256), :])
        done = block(jnp.concatenate(rows, axis=0)).reshape(4, 128, HD)
        for i in range(2):
            zd = (z + far_first(2 * n + i)) % NZ
            ov[pl.ds(2 * zd, 2)] = done[2 * i : 2 * i + 2]

        @pl.when(n > 0)
        def _():
            start(2 * n - 2)
            start(2 * n - 1)

        @pl.when(n == 0)
        def _():
            weights.middle(1)
            weights.middle(2)

        @pl.when(n == 1)
        def _():
            weights.middle(3)
            weights.last(0)
            weights.last(1)

        @pl.when(n == 2)
        def _():
            weights.last(2)
            weights.last(3)

        return carry

    lax.fori_loop(0, NZ // 2, step, 0)
    start(NZ - 2)
    start(NZ - 1)

    def finish(n, carry):
        pltpu.make_async_copy(ov.at[n], rv.at[n], vrecv.at[n]).wait()
        pltpu.make_async_copy(ot.at[n], rt.at[n], trecv.at[n]).wait()
        return carry

    lax.fori_loop(0, 16, finish, 0)

    def sent(n, carry):
        for b in range(2):
            away, remote, _ = copies(n, b)

            @pl.when(away)
            def _():
                for one in remote:
                    one.wait_send()

        return carry

    lax.fori_loop(0, NZ, sent, 0)
    lax.fori_loop(0, R_CHUNKS, lambda k, carry: (weights.side(k), carry)[1], 0)
    weights.finish()


def attend(counts, splits, vid, txt, w_out):
    bf = jnp.bfloat16
    half = (W_REST, w_out.shape[1])
    return pl.pallas_call(
        attend_kernel,
        out_shape=[
            jax.ShapeDtypeStruct((16, 128, HD), bf),
            jax.ShapeDtypeStruct((16, 3, 16, HD), bf),
            jax.ShapeDtypeStruct((N_JOB, *half), bf),
        ],
        in_specs=[pl.BlockSpec(memory_space=pltpu.SMEM)] * 2 + [ANY] * 3,
        out_specs=[ANY] * 3,
        scratch_shapes=[
            pltpu.VMEM((4096, HD), bf),
            pltpu.VMEM((4096, HD), bf),
            pltpu.VMEM((5, 256, HD), bf),
            pltpu.VMEM((4352, 2 * HD), bf),
            pltpu.VMEM((256, HD), bf),
            pltpu.VMEM((16, 128, HD), bf),
            pltpu.VMEM((16, 3, 16, HD), bf),
            DMA((5,)),
            DMA((16,)),
            DMA((16,)),
            DMA((16,)),
            DMA((16,)),
            pltpu.VMEM(half, bf),
            *gather_sems(R_CHUNKS),
        ],
        compiler_params=pltpu.CompilerParams(
            collective_id=6, has_side_effects=True, vmem_limit_bytes=56 << 20
        ),
        name="attend",
    )(counts, splits, vid, txt, w_out)


def final_kernel(counts, splits, rv, rt, w_first, w_rest, video, gate, out, text_out):
    job, shard = lax.axis_index("job"), lax.axis_index("seq")
    f32, bf = jnp.float32, jnp.bfloat16
    total = None
    for g in range(N_JOB):
        rows = jnp.concatenate(
            [
                jnp.concatenate([rv[g], rv[8 + g]], axis=1),
                jnp.concatenate([rt[g, 0], rt[8 + g, 0]], axis=1),
            ],
            axis=0,
        )
        weight = jnp.concatenate([w_first[g], w_rest[g]], axis=0)
        part = jnp.dot(rows, weight, preferred_element_type=f32).astype(bf).astype(f32)
        total = part if total is None else total + part
    change = gate[pl.ds(job, 1), :] * total
    out[...] = (video[...].astype(f32) + change[:128]).astype(bf)
    kept = []
    for i in range(N_SPLIT // HD):
        group = pl.program_id(0) * (N_SPLIT // HD) + i
        g, third = group // 3, group % 3
        kept.append(rt[jnp.where(third == 2, 8 + g, g), jnp.where(third == 1, 2, 1)])
    text = (jnp.concatenate(kept, axis=1).astype(f32) + change[128:]).astype(bf)
    first = lax.fori_loop(0, shard, lambda i, sum_: sum_ + splits[job, i], jnp.int32(0))
    ids = lax.broadcasted_iota(jnp.int32, text.shape, 0)
    ok = (ids < splits[job, shard]) & (first + ids < counts[job])
    text_out[...] = jnp.where(ok, text, jnp.zeros_like(text))


N_SPLIT = 768


def final(counts, splits, rv, rt, w_first, w_rest, video, gate):
    bf = jnp.bfloat16
    smem = pl.BlockSpec(memory_space=pltpu.SMEM)
    width = video.shape[1]

    def whole(a):
        return pl.BlockSpec(a.shape, lambda n: (0,) * a.ndim)

    def cut(a):
        return pl.BlockSpec((*a.shape[:-1], N_SPLIT), lambda n: (0,) * (a.ndim - 1) + (n,))

    return pl.pallas_call(
        final_kernel,
        grid=(width // N_SPLIT,),
        out_shape=[
            jax.ShapeDtypeStruct((128, width), bf),
            jax.ShapeDtypeStruct((16, width), bf),
        ],
        in_specs=[smem, smem, whole(rv), whole(rt), cut(w_first), cut(w_rest), cut(video), cut(gate)],
        out_specs=[
            pl.BlockSpec((128, N_SPLIT), lambda n: (0, n)),
            pl.BlockSpec((16, N_SPLIT), lambda n: (0, n)),
        ],
        compiler_params=pltpu.CompilerParams(vmem_limit_bytes=48 << 20),
        name="final",
    )(counts, splits, rv, rt, w_first, w_rest, video, gate)


def body(
    video,
    text_cache,
    text_count,
    holder,
    text_splits,
    mod_shift,
    mod_scale,
    mod_gate,
    text_gain,
    refine_w,
    refine_bias,
    w_qkv,
    q_gain,
    k_gain,
    w_out,
):
    own_video = video[0]
    w_out = w_out.reshape(2 * HD, -1)
    rvid, rtxt, w_first = project_all(
        holder,
        text_cache[0],
        own_video,
        refine_w,
        jnp.transpose(w_qkv, (2, 1, 0, 3)),
        w_out,
        text_gain[None],
        refine_bias[None],
        mod_scale,
        mod_shift,
        q_gain,
        k_gain,
    )

    rv, rt, w_rest = attend(text_count, text_splits, rvid, rtxt, w_out)
    out, text_out = final(text_count, text_splits, rv, rt, w_first, w_rest, own_video, mod_gate)
    return out[None], text_out[None]


def solution(mesh):
    placed = (
        P("job", "seq", None),
        P("job", "seq", None),
        P(),
        P(),
        P(),
        P(),
        P(),
        P(),
        P(),
        P(None, "job"),
        P("job"),
        P(None, "job", None, None),
        P("job", None),
        P("job", None),
        P("job", None, None),
    )
    return jax.shard_map(
        body,
        mesh=mesh,
        in_specs=placed,
        out_specs=(P("job", "seq", None), P("job", "seq", None)),
        check_vma=False,
    )
```

```python
import functools

import jax
import jax.numpy as jnp
from jax import lax
from jax.experimental import pallas as pl
from jax.experimental.pallas import tpu as pltpu
from jax.sharding import PartitionSpec as P

HD = 128
NY, NC, NZ, NX = 4, 2, 8, 4
N_JOB = NY * NC
N_SEQ = NZ * NX
MESH = pl.DeviceIdType.MESH
epsilon = 1e-06
ANY = pl.BlockSpec(memory_space=pl.ANY)
DMA = pltpu.SemaphoreType.DMA


def rms_scale(values, gains):
    mean_square = jnp.mean(values * values, axis=-1, keepdims=True)
    return values * lax.rsqrt(mean_square + epsilon) * gains


def place():
    job = lax.axis_index("job")
    seq = lax.axis_index("seq")
    return job // NC, job % NC, seq // NX, seq % NX


def signal(job, seq):
    pl.semaphore_signal(
        pltpu.get_barrier_semaphore(), inc=1, device_id=(job, seq), device_id_type=MESH
    )


def near():
    y, c, z, x = place()
    seq = z * NX + x
    up = (((y + 1) % NY) * NC + c, seq)
    down = (((y + NY - 1) % NY) * NC + c, seq)
    other = (y * NC + 1 - c, seq)
    return up, down, other


def span(k, step):
    if isinstance(k, int):
        return pl.ds(k * step, step)
    return pl.ds(pl.multiple_of(k * step, step), step)


class JobGather:
    def __init__(self, src, dst, send, recv, local, rows, chunks, buf=None):
        self.src, self.dst, self.buf = src, dst, buf
        self.send, self.recv, self.local = send, recv, local
        self.step, self.chunks = rows // chunks, chunks

    def piece(self, k):
        return span(k, self.step)

    def copy(self, source, block, role, k, device):
        return pltpu.make_async_remote_copy(
            src_ref=source.at[self.piece(k)],
            dst_ref=self.dst.at[block, self.piece(k)],
            send_sem=self.send.at[role, k],
            recv_sem=self.recv.at[role, k],
            device_id=device,
            device_id_type=MESH,
        )

    def block(self, role):
        y, c, _, _ = place()
        return {
            0: ((y + NY - 1) % NY) * NC + c,
            1: ((y + 1) % NY) * NC + c,
            2: ((y + 2) % NY) * NC + c,
            3: y * NC + 1 - c,
            4: ((y + NY - 1) % NY) * NC + 1 - c,
            5: ((y + 1) % NY) * NC + 1 - c,
            6: ((y + 2) % NY) * NC + 1 - c,
        }[role]

    def own(self):
        y, c, _, _ = place()
        return y * NC + c

    def load(self):
        into = self.dst.at[self.own()] if self.buf is None else self.buf
        pltpu.make_async_copy(self.src, into, self.local.at[0]).start()

    def loaded(self):
        into = self.dst.at[self.own()] if self.buf is None else self.buf
        pltpu.make_async_copy(self.src, into, self.local.at[0]).wait()
        if self.buf is not None:
            pltpu.make_async_copy(self.buf, self.dst.at[self.own()], self.local.at[1]).start()

    def send_own(self, k):
        up, down, other = near()
        own = self.own()
        self.copy(self.src, own, 0, k, up).start()
        self.copy(self.src, own, 1, k, down).start()
        self.copy(self.src, own, 3, k, other).start()

    def arrived(self, role, k):
        block = self.block(role)
        self.copy(self.dst.at[block], block, role, k, near()[2]).wait_recv()

    def handon(self, role, k):
        block = self.block(role)
        self.copy(self.dst.at[block], block, role + 4, k, near()[2]).start()

    def middle(self, k):
        y, c, _, _ = place()
        up, down, other = near()
        self.arrived(0, k)

        @pl.when(c == 0)
        def _():
            self.copy(self.dst.at[self.block(0)], self.block(0), 2, k, up).start()

        self.handon(0, k)
        self.arrived(1, k)

        @pl.when(c == 1)
        def _():
            self.copy(self.dst.at[self.block(1)], self.block(1), 2, k, down).start()

        self.handon(1, k)

    def last(self, k):
        self.arrived(2, k)
        self.handon(2, k)

    def side(self, k):
        for role in (3, 4, 5, 6):
            self.arrived(role, k)

    def finish(self):
        own = self.own()
        other = near()[2]

        def go(k, carry):
            for role in range(7):
                self.copy(self.src, own, role, k, other).wait_send()
            return carry

        lax.fori_loop(0, self.chunks, go, 0)
        if self.buf is not None:
            pltpu.make_async_copy(self.buf, self.dst.at[own], self.local.at[1]).wait()


def gather_sems(chunks):
    return [DMA((7, chunks)), DMA((7, chunks)), DMA((2,))]


def far_first(n):
    return 4 + ((n + 1) // 2) * (1 - 2 * (n % 2))


W_CHUNKS = 8
AHEAD = 4
W_FIRST = 192
W_REST = 2 * HD - W_FIRST
R_CHUNKS = 4
V_CHUNKS = 4
V_ROWS = 128 // V_CHUNKS


def project_kernel(
    holder, raw, video, refine_w, w_qkv, w_out, gain, bias, scale, shift, q_gain, k_gain,
    rvid, rtxt, w_all,
    raw_all, video_all, refined, refined_all, wr, wq, normed, modded, text_rows, svid, stxt, buf,
    loads, rsend, rrecv, rlocal, fsend, frecv, flocal, isend, irecv, ilocal,
    wsend, wrecv, wlocal, vsend, vrecv, tsend, trecv,
):
    y, c, z, x = place()
    seq = z * NX + x
    f32, bf = jnp.float32, jnp.bfloat16
    other = near()[2]
    here = (x // 2 == c).astype(jnp.int32)
    peer_job = y * NC + x // 2
    text = JobGather(raw, raw_all, rsend, rrecv, rlocal, 8, 1)
    frames = JobGather(video, video_all, fsend, frecv, flocal, 128, V_CHUNKS)
    inner = JobGather(refined, refined_all, isend, irecv, ilocal, 64, 1)
    weights = JobGather(
        w_out.at[pl.ds(0, W_FIRST)], w_all, wsend, wrecv, wlocal, W_FIRST, W_CHUNKS, buf
    )
    text.load()
    frames.load()
    load_r = pltpu.make_async_copy(refine_w, wr, loads.at[0])
    load_q = [
        pltpu.make_async_copy(
            w_qkv.at[part, hl], wq.at[:, pl.ds((hl * 3 + part) * HD, HD)], loads.at[1 + 2 * part + hl]
        )
        for part in range(3)
        for hl in range(2)
    ]
    load_r.start()
    for one in load_q:
        one.start()

    def greet(n, carry):
        for hl in range(2):
            to = n * NX + 2 * c + hl

            @pl.when(jnp.logical_or(to != seq, here == 0))
            def _():
                signal(peer_job, to)

        return carry

    lax.fori_loop(0, NZ, greet, 0)
    for device in near():
        signal(*device)
    pl.semaphore_wait(pltpu.get_barrier_semaphore(), 19 - here)

    text.send_own(0)
    for k in range(2):
        frames.send_own(k)

    def refine():
        for j in range(N_JOB):
            rows = raw_all[holder[j]].astype(f32)
            normed[pl.ds(8 * j, 8)] = rms_scale(rows, gain[...])
        lifted = jnp.dot(normed[...].astype(bf), wr[...], preferred_element_type=f32)
        refined[...] = (lifted + bias[...].reshape(1, -1)).astype(bf)

    inner_own = pltpu.make_async_copy(refined, refined_all.at[inner.own()], ilocal.at[0])

    def vrows(shard, k):
        first = pl.multiple_of(shard * 128 + k * V_ROWS, V_ROWS)
        return rvid.at[:, pl.ds(first, V_ROWS), :]

    def trows(shard):
        return rtxt.at[:, pl.ds(pl.multiple_of(shard * 8, 8), 8), :]

    slot = 2 * z + x % 2

    def target(n, hl):
        zd = (z + far_first(n)) % NZ
        j = (zd + NZ - 2 * y) % NZ
        to = zd * NX + 2 * c + hl
        return 2 * j + hl, to, jnp.logical_or(to != seq, here == 0)

    def vcopy(n, hl, k):
        pair, to, away = target(n, hl)
        source = svid.at[pair, :, span(k, V_ROWS), :]
        remote = pltpu.make_async_remote_copy(
            source, vrows(seq, k), vsend.at[2 * n + hl, k], vrecv.at[slot, k],
            (peer_job, to), MESH,
        )
        return away, remote, pltpu.make_async_copy(source, vrows(seq, k), vrecv.at[slot, k])

    def tcopy(n, hl):
        pair, to, away = target(n, hl)
        remote = pltpu.make_async_remote_copy(
            stxt.at[pair], trows(seq), tsend.at[2 * n + hl], trecv.at[slot], (peer_job, to), MESH
        )
        return away, remote, pltpu.make_async_copy(stxt.at[pair], trows(seq), trecv.at[slot])

    def launch(make):
        def go(n, carry):
            for hl in range(2):
                away, remote, local = make(n, hl)

                @pl.when(away)
                def _():
                    remote.start()

                @pl.when(jnp.logical_not(away))
                def _():
                    local.start()

            return carry

        lax.fori_loop(0, NZ, go, 0)

    def drained(make):
        def go(n, carry):
            for hl in range(2):
                away, remote, _ = make(n, hl)

                @pl.when(away)
                def _():
                    remote.wait_send()

            return carry

        lax.fori_loop(0, NZ, go, 0)

    def vhand(shard, index, k):
        return pltpu.make_async_remote_copy(
            vrows(shard, k), vrows(shard, k), vsend.at[index, k], vrecv.at[index, k], other, MESH
        )

    def thand(shard, index):
        return pltpu.make_async_remote_copy(
            trows(shard), trows(shard), tsend.at[index], trecv.at[index], other, MESH
        )

    def sources(n):
        zs = (z + NZ - far_first(n)) % NZ
        return [(zs * NX + 2 * c + b, 2 * zs + b) for b in range(2)]

    def take(k):
        def go(n, carry):
            for shard, index in sources(n):
                vhand(shard, index, k).wait_recv()
                vhand(shard, index + 16, k).start()
            return carry

        lax.fori_loop(0, NZ, go, 0)

    def normalise(rows, j):
        centre = jnp.mean(rows, axis=-1, keepdims=True)
        moved = rows - centre
        spread_sq = jnp.mean(moved * moved, axis=-1, keepdims=True)
        out = moved * lax.rsqrt(spread_sq + epsilon)
        return (out * (1.0 + scale[pl.ds(j, 1), :]) + shift[pl.ds(j, 1), :]).astype(bf)

    def project(rows):
        got = jnp.dot(rows, wq[...], preferred_element_type=f32)
        out = []
        for hl in range(2):
            for part in range(3):
                piece = got[:, (hl * 3 + part) * HD : (hl * 3 + part + 1) * HD]
                if part == 0:
                    piece = rms_scale(piece, q_gain[pl.ds(hl, 1), :])
                if part == 1:
                    piece = rms_scale(piece, k_gain[pl.ds(hl, 1), :])
                out.append(piece.astype(bf))
        return out

    frames.loaded()
    frames.middle(0)
    frames.send_own(2)
    text.middle(0)
    text.loaded()

    def round_(k, carry):
        @pl.when(k + 1 < V_CHUNKS)
        def _():
            frames.middle(k + 1)

        @pl.when(k > 0)
        def _():
            launch(lambda n, hl: vcopy(n, hl, k - 1))

        @pl.when(k == 0)
        def _():
            frames.send_own(3)
            text.last(0)
            for one in load_q:
                one.wait()

        @pl.when(k == 2)
        def _():
            inner_own.start()
            inner.send_own(0)
            for ahead in range(AHEAD):
                weights.send_own(ahead)

        @pl.when(k == 3)
        def _():
            inner.middle(0)
            inner.last(0)

        frames.last(k)
        frames.side(k)

        rows_k = span(k, V_ROWS)
        for j in range(N_JOB):
            modded[pl.ds(V_ROWS * j, V_ROWS)] = normalise(video_all[j, rows_k, :].astype(f32), j)
        for i, piece in enumerate(project(modded[...])):
            for j in range(N_JOB):
                svid[2 * j + i // 3, i % 3, rows_k, :] = piece[V_ROWS * j : V_ROWS * (j + 1)]

        @pl.when(k == 1)
        def _():
            text.side(0)
            load_r.wait()
            refine()

        return carry

    weights.load()
    lax.fori_loop(0, V_CHUNKS, round_, 0)

    def forward(n):
        weights.middle(n)
        if n + AHEAD < W_CHUNKS:
            weights.send_own(n + AHEAD)

    weights.loaded()
    forward(0)
    launch(lambda n, hl: vcopy(n, hl, V_CHUNKS - 1))
    inner.side(0)
    inner_own.wait()
    for g in range(N_JOB):
        text_rows[:, 384 * g : 384 * (g + 1)] = refined_all[g].astype(f32)
    for j in range(N_JOB):
        normed[pl.ds(8 * j, 8), 0:3072] = normalise(text_rows[pl.ds(8 * j, 8)], j).astype(f32)
    for i, piece in enumerate(project(normed[:, 0:3072].astype(bf))):
        for j in range(N_JOB):
            stxt[2 * j + i // 3, i % 3] = piece[8 * j : 8 * (j + 1)]
    for j in range(N_JOB):
        for group in range(4):
            at = min(group, 2) * HD
            stxt[2 * j + group // 2, 3 + group % 2] = refined[8 * j : 8 * (j + 1), at : at + HD]
    forward(1)
    take(0)
    launch(tcopy)
    forward(2)
    weights.last(0)
    forward(3)
    weights.last(1)
    take(1)
    forward(4)
    weights.last(2)
    forward(5)
    weights.last(3)
    take(2)
    forward(6)
    weights.last(4)
    forward(7)
    weights.last(5)
    weights.last(6)
    take(3)
    weights.last(7)

    def text_rest(n, carry):
        for shard, index in sources(n):
            thand(shard, index).wait_recv()
            thand(shard, index + 16).start()
        return carry

    lax.fori_loop(0, NZ, text_rest, 0)

    def finish(n, carry):
        for b in range(2):
            shard = n * NX + 2 * (1 - c) + b
            index = 2 * n + b + 16
            for k in range(V_CHUNKS):
                vhand(shard, index, k).wait_recv()
                vhand(shard, index, k).wait_send()
            thand(shard, index).wait_recv()
            thand(shard, index).wait_send()
        return carry

    lax.fori_loop(0, NZ, finish, 0)
    for k in range(V_CHUNKS):
        drained(lambda n, hl: vcopy(n, hl, k))
    drained(tcopy)
    lax.fori_loop(0, W_CHUNKS, lambda k, carry: (weights.side(k), carry)[1], 0)
    for one in (text, frames, inner, weights):
        one.finish()


def project_all(holder, raw, video, refine_w, w_qkv, w_out, *small):
    f32, bf = jnp.float32, jnp.bfloat16
    vm = pl.BlockSpec(memory_space=pltpu.VMEM)
    return pl.pallas_call(
        project_kernel,
        out_shape=[
            jax.ShapeDtypeStruct((3, N_SEQ * 128, HD), bf),
            jax.ShapeDtypeStruct((5, N_SEQ * 8, HD), bf),
            jax.ShapeDtypeStruct((N_JOB, W_FIRST, w_out.shape[1]), bf),
        ],
        in_specs=[pl.BlockSpec(memory_space=pltpu.SMEM)] + [ANY] * 5 + [vm] * 6,
        out_specs=[ANY] * 3,
        scratch_shapes=[
            pltpu.VMEM((N_JOB, 8, 4096), bf),
            pltpu.VMEM((N_JOB, 128, 3072), bf),
            pltpu.VMEM((64, 384), bf),
            pltpu.VMEM((N_JOB, 64, 384), bf),
            pltpu.VMEM((4096, 384), bf),
            pltpu.VMEM((3072, 768), bf),
            pltpu.VMEM((64, 4096), f32),
            pltpu.VMEM((8 * V_ROWS, 3072), bf),
            pltpu.VMEM((64, 3072), f32),
            pltpu.VMEM((16, 3, 128, HD), bf),
            pltpu.VMEM((16, 5, 8, HD), bf),
            pltpu.VMEM((W_FIRST, w_out.shape[1]), bf),
            DMA((7,)),
            *gather_sems(1),
            *gather_sems(V_CHUNKS),
            *gather_sems(1),
            *gather_sems(W_CHUNKS),
            DMA((32, V_CHUNKS)),
            DMA((32, V_CHUNKS)),
            DMA((32,)),
            DMA((32,)),
        ],
        compiler_params=pltpu.CompilerParams(
            collective_id=5, has_side_effects=True, vmem_limit_bytes=58 << 20
        ),
        name="project_all",
    )(holder, raw, video, refine_w, w_qkv, w_out, *small)


def attend_kernel(
    counts, splits, vid, txt, w_out, rv, rt, w_all,
    q, k, tx, vext, text_out, ov, ot, loads, vsend, vrecv, tsend, trecv, buf, wsend, wrecv, wlocal,
):
    y, c, z, x = place()
    seq = z * NX + x
    mine = y * NC + c
    job = (z + NZ - 2 * y) % NZ
    head = (x % 2) * 8 + 2 * y + x // 2
    incoming = [
        pltpu.make_async_copy(vid.at[0], q, loads.at[0]),
        pltpu.make_async_copy(vid.at[1], k, loads.at[1]),
        pltpu.make_async_copy(vid.at[2], vext.at[pl.ds(0, 4096), pl.ds(0, HD)], loads.at[2]),
        pltpu.make_async_copy(txt.at[2], vext.at[pl.ds(4096, 256), pl.ds(0, HD)], loads.at[3]),
        pltpu.make_async_copy(txt, tx, loads.at[4]),
    ]
    for one in incoming:
        one.start()

    def greet(n, carry):
        for b in range(NX):
            from_job = n * NC + x // 2
            from_seq = ((mine + 2 * n) % NZ) * NX + b

            @pl.when(jnp.logical_or(from_job != mine, from_seq != seq))
            def _():
                signal(from_job, from_seq)

        return carry

    lax.fori_loop(0, NY, greet, 0)
    for device in near():
        signal(*device)
    inside = jnp.logical_and(job == mine, x // 2 == c).astype(jnp.int32)
    pl.semaphore_wait(pltpu.get_barrier_semaphore(), 19 - inside)
    weights = JobGather(
        w_out.at[pl.ds(W_FIRST, W_REST)], w_all, wsend, wrecv, wlocal, W_REST, R_CHUNKS, buf
    )
    weights.load()
    for ahead in range(R_CHUNKS):
        weights.send_own(ahead)
    weights.loaded()

    count = counts[job]
    vext[:, HD:] = jnp.ones((4352, HD), jnp.bfloat16)
    for one in incoming:
        one.wait()
    factor = (HD**-0.5) * 1.4426950408889634
    contract = (((1,), (1,)), ((), ()))

    def block(part):
        sv = lax.dot_general(part, k[...], contract, preferred_element_type=jnp.float32)
        st = lax.dot_general(part, tx[1], contract, preferred_element_type=jnp.float32)
        st = jnp.where(lax.broadcasted_iota(jnp.int32, st.shape, 1) < count, st, -1e30)
        top = jnp.maximum(
            jnp.max(sv, axis=-1, keepdims=True), jnp.max(st, axis=-1, keepdims=True)
        )
        pv = jnp.exp2((sv - top) * factor).astype(jnp.bfloat16)
        pt = jnp.exp2((st - top) * factor).astype(jnp.bfloat16)
        both = jnp.dot(pv, vext[0:4096], preferred_element_type=jnp.float32)
        both += jnp.dot(pt, vext[4096:4352], preferred_element_type=jnp.float32)
        return (both[:, 0:HD] / both[:, HD:]).astype(jnp.bfloat16)

    text_out[...] = block(tx[0])
    across = lax.broadcasted_iota(jnp.int32, (16, 256), 1)
    down = lax.broadcasted_iota(jnp.int32, (16, 256), 0)
    base = jnp.int32(0)
    picks = []
    for zs in range(NZ):
        quad = [splits[job, NX * zs + i] for i in range(NX)]
        at = base + c * (quad[0] + quad[1])
        for b in range(2):
            length = quad[b] + c * (quad[2 + b] - quad[b])
            hit = (across == at + down) & (down < length) & (across < count)
            picks.append(jnp.where(hit, 1.0, 0.0).astype(jnp.bfloat16))
            at = at + length
        base = base + quad[0] + quad[1] + quad[2] + quad[3]
    pick = jnp.concatenate(picks, axis=0)
    for part in range(3):
        rows = text_out[...] if part == 0 else tx[part + 2]
        moved = jnp.dot(pick, rows, preferred_element_type=jnp.float32).astype(jnp.bfloat16)
        ot[:, part] = moved.reshape(16, 16, HD)

    def copies(n, b):
        zd = (z + far_first(n)) % NZ
        part = 2 * zd + b
        to = zd * NX + 2 * c + b
        away = jnp.logical_or(to != seq, job != mine)
        remote = (
            pltpu.make_async_remote_copy(
                ov.at[part], rv.at[head], vsend.at[part], vrecv.at[head], (job, to), MESH
            ),
            pltpu.make_async_remote_copy(
                ot.at[part], rt.at[head], tsend.at[part], trecv.at[head], (job, to), MESH
            ),
        )
        local = (
            pltpu.make_async_copy(ov.at[part], rv.at[head], vrecv.at[head]),
            pltpu.make_async_copy(ot.at[part], rt.at[head], trecv.at[head]),
        )
        return away, remote, local

    def start(n):
        for b in range(2):
            away, remote, local = copies(n, b)

            @pl.when(away)
            def _():
                for one in remote:
                    one.start()

            @pl.when(jnp.logical_not(away))
            def _():
                for one in local:
                    one.start()

    weights.middle(0)

    def step(n, carry):
        rows = []
        for i in range(2):
            zd = (z + far_first(2 * n + i)) % NZ
            rows.append(q[pl.ds(pl.multiple_of(zd * 512 + c * 256, 256), 256), :])
        done = block(jnp.concatenate(rows, axis=0)).reshape(4, 128, HD)
        for i in range(2):
            zd = (z + far_first(2 * n + i)) % NZ
            ov[pl.ds(2 * zd, 2)] = done[2 * i : 2 * i + 2]

        @pl.when(n > 0)
        def _():
            start(2 * n - 2)
            start(2 * n - 1)

        @pl.when(n == 0)
        def _():
            weights.middle(1)
            weights.middle(2)

        @pl.when(n == 1)
        def _():
            weights.middle(3)
            weights.last(0)
            weights.last(1)

        @pl.when(n == 2)
        def _():
            weights.last(2)
            weights.last(3)

        return carry

    lax.fori_loop(0, NZ // 2, step, 0)
    start(NZ - 2)
    start(NZ - 1)

    def finish(n, carry):
        pltpu.make_async_copy(ov.at[n], rv.at[n], vrecv.at[n]).wait()
        pltpu.make_async_copy(ot.at[n], rt.at[n], trecv.at[n]).wait()
        return carry

    lax.fori_loop(0, 16, finish, 0)

    def sent(n, carry):
        for b in range(2):
            away, remote, _ = copies(n, b)

            @pl.when(away)
            def _():
                for one in remote:
                    one.wait_send()

        return carry

    lax.fori_loop(0, NZ, sent, 0)
    lax.fori_loop(0, R_CHUNKS, lambda k, carry: (weights.side(k), carry)[1], 0)
    weights.finish()


def attend(counts, splits, vid, txt, w_out):
    bf = jnp.bfloat16
    half = (W_REST, w_out.shape[1])
    return pl.pallas_call(
        attend_kernel,
        out_shape=[
            jax.ShapeDtypeStruct((16, 128, HD), bf),
            jax.ShapeDtypeStruct((16, 3, 16, HD), bf),
            jax.ShapeDtypeStruct((N_JOB, *half), bf),
        ],
        in_specs=[pl.BlockSpec(memory_space=pltpu.SMEM)] * 2 + [ANY] * 3,
        out_specs=[ANY] * 3,
        scratch_shapes=[
            pltpu.VMEM((4096, HD), bf),
            pltpu.VMEM((4096, HD), bf),
            pltpu.VMEM((5, 256, HD), bf),
            pltpu.VMEM((4352, 2 * HD), bf),
            pltpu.VMEM((256, HD), bf),
            pltpu.VMEM((16, 128, HD), bf),
            pltpu.VMEM((16, 3, 16, HD), bf),
            DMA((5,)),
            DMA((16,)),
            DMA((16,)),
            DMA((16,)),
            DMA((16,)),
            pltpu.VMEM(half, bf),
            *gather_sems(R_CHUNKS),
        ],
        compiler_params=pltpu.CompilerParams(
            collective_id=6, has_side_effects=True, vmem_limit_bytes=56 << 20
        ),
        name="attend",
    )(counts, splits, vid, txt, w_out)


def final_kernel(counts, splits, rv, rt, w_first, w_rest, video, gate, out, text_out):
    job, shard = lax.axis_index("job"), lax.axis_index("seq")
    f32, bf = jnp.float32, jnp.bfloat16
    total = None
    for g in range(N_JOB):
        rows = jnp.concatenate(
            [
                jnp.concatenate([rv[g], rv[8 + g]], axis=1),
                jnp.concatenate([rt[g, 0], rt[8 + g, 0]], axis=1),
            ],
            axis=0,
        )
        weight = jnp.concatenate([w_first[g], w_rest[g]], axis=0)
        part = jnp.dot(rows, weight, preferred_element_type=f32).astype(bf).astype(f32)
        total = part if total is None else total + part
    change = gate[pl.ds(job, 1), :] * total
    out[...] = (video[...].astype(f32) + change[:128]).astype(bf)
    kept = []
    for i in range(N_SPLIT // HD):
        group = pl.program_id(0) * (N_SPLIT // HD) + i
        g, third = group // 3, group % 3
        kept.append(rt[jnp.where(third == 2, 8 + g, g), jnp.where(third == 1, 2, 1)])
    text = (jnp.concatenate(kept, axis=1).astype(f32) + change[128:]).astype(bf)
    first = lax.fori_loop(0, shard, lambda i, sum_: sum_ + splits[job, i], jnp.int32(0))
    ids = lax.broadcasted_iota(jnp.int32, text.shape, 0)
    ok = (ids < splits[job, shard]) & (first + ids < counts[job])
    text_out[...] = jnp.where(ok, text, jnp.zeros_like(text))


N_SPLIT = 768


def final(counts, splits, rv, rt, w_first, w_rest, video, gate):
    bf = jnp.bfloat16
    smem = pl.BlockSpec(memory_space=pltpu.SMEM)
    width = video.shape[1]

    def whole(a):
        return pl.BlockSpec(a.shape, lambda n: (0,) * a.ndim)

    def cut(a):
        return pl.BlockSpec((*a.shape[:-1], N_SPLIT), lambda n: (0,) * (a.ndim - 1) + (n,))

    return pl.pallas_call(
        final_kernel,
        grid=(width // N_SPLIT,),
        out_shape=[
            jax.ShapeDtypeStruct((128, width), bf),
            jax.ShapeDtypeStruct((16, width), bf),
        ],
        in_specs=[smem, smem, whole(rv), whole(rt), cut(w_first), cut(w_rest), cut(video), cut(gate)],
        out_specs=[
            pl.BlockSpec((128, N_SPLIT), lambda n: (0, n)),
            pl.BlockSpec((16, N_SPLIT), lambda n: (0, n)),
        ],
        compiler_params=pltpu.CompilerParams(vmem_limit_bytes=60 << 20),
        name="final",
    )(counts, splits, rv, rt, w_first, w_rest, video, gate)


def body(
    video,
    text_cache,
    text_count,
    holder,
    text_splits,
    mod_shift,
    mod_scale,
    mod_gate,
    text_gain,
    refine_w,
    refine_bias,
    w_qkv,
    q_gain,
    k_gain,
    w_out,
):
    own_video = video[0]
    w_out = w_out.reshape(2 * HD, -1)
    rvid, rtxt, w_first = project_all(
        holder,
        text_cache[0],
        own_video,
        refine_w,
        jnp.transpose(w_qkv, (2, 1, 0, 3)),
        w_out,
        text_gain[None],
        refine_bias,
        mod_scale,
        mod_shift,
        q_gain,
        k_gain,
    )

    rv, rt, w_rest = attend(text_count, text_splits, rvid, rtxt, w_out)
    out, text_out = final(text_count, text_splits, rv, rt, w_first, w_rest, own_video, mod_gate)
    return out[None], text_out[None]


def solution(mesh):
    placed = (
        P("job", "seq", None),
        P("job", "seq", None),
        P(),
        P(),
        P(),
        P(),
        P(),
        P(),
        P(),
        P(None, "job"),
        P("job"),
        P(None, "job", None, None),
        P("job", None),
        P("job", None),
        P("job", None, None),
    )
    return jax.shard_map(
        body,
        mesh=mesh,
        in_specs=placed,
        out_specs=(P("job", "seq", None), P("job", "seq", None)),
        check_vma=False,
    )
```

```python
import functools

import jax
import jax.numpy as jnp
from jax import lax
from jax.experimental import pallas as pl
from jax.experimental.pallas import tpu as pltpu
from jax.sharding import PartitionSpec as P

HD = 128
NY, NC, NZ, NX = 4, 2, 8, 4
N_JOB = NY * NC
N_SEQ = NZ * NX
MESH = pl.DeviceIdType.MESH
epsilon = 1e-06
ANY = pl.BlockSpec(memory_space=pl.ANY)
DMA = pltpu.SemaphoreType.DMA


def rms_scale(values, gains):
    mean_square = jnp.mean(values * values, axis=-1, keepdims=True)
    return values * lax.rsqrt(mean_square + epsilon) * gains


def place():
    job = lax.axis_index("job")
    seq = lax.axis_index("seq")
    return job // NC, job % NC, seq // NX, seq % NX


def signal(job, seq):
    pl.semaphore_signal(
        pltpu.get_barrier_semaphore(), inc=1, device_id=(job, seq), device_id_type=MESH
    )


def near():
    y, c, z, x = place()
    seq = z * NX + x
    up = (((y + 1) % NY) * NC + c, seq)
    down = (((y + NY - 1) % NY) * NC + c, seq)
    other = (y * NC + 1 - c, seq)
    return up, down, other


def span(k, step):
    if isinstance(k, int):
        return pl.ds(k * step, step)
    return pl.ds(pl.multiple_of(k * step, step), step)


class JobGather:
    def __init__(self, src, dst, send, recv, local, rows, chunks, buf=None):
        self.src, self.dst, self.buf = src, dst, buf
        self.send, self.recv, self.local = send, recv, local
        self.step, self.chunks = rows // chunks, chunks

    def piece(self, k):
        return span(k, self.step)

    def copy(self, source, block, role, k, device):
        return pltpu.make_async_remote_copy(
            src_ref=source.at[self.piece(k)],
            dst_ref=self.dst.at[block, self.piece(k)],
            send_sem=self.send.at[role, k],
            recv_sem=self.recv.at[role, k],
            device_id=device,
            device_id_type=MESH,
        )

    def block(self, role):
        y, c, _, _ = place()
        return {
            0: ((y + NY - 1) % NY) * NC + c,
            1: ((y + 1) % NY) * NC + c,
            2: ((y + 2) % NY) * NC + c,
            3: y * NC + 1 - c,
            4: ((y + NY - 1) % NY) * NC + 1 - c,
            5: ((y + 1) % NY) * NC + 1 - c,
            6: ((y + 2) % NY) * NC + 1 - c,
        }[role]

    def own(self):
        y, c, _, _ = place()
        return y * NC + c

    def load(self):
        into = self.dst.at[self.own()] if self.buf is None else self.buf
        pltpu.make_async_copy(self.src, into, self.local.at[0]).start()

    def loaded(self):
        into = self.dst.at[self.own()] if self.buf is None else self.buf
        pltpu.make_async_copy(self.src, into, self.local.at[0]).wait()
        if self.buf is not None:
            pltpu.make_async_copy(self.buf, self.dst.at[self.own()], self.local.at[1]).start()

    def send_own(self, k):
        up, down, other = near()
        own = self.own()
        self.copy(self.src, own, 0, k, up).start()
        self.copy(self.src, own, 1, k, down).start()
        self.copy(self.src, own, 3, k, other).start()

    def arrived(self, role, k):
        block = self.block(role)
        self.copy(self.dst.at[block], block, role, k, near()[2]).wait_recv()

    def handon(self, role, k):
        block = self.block(role)
        self.copy(self.dst.at[block], block, role + 4, k, near()[2]).start()

    def middle(self, k):
        y, c, _, _ = place()
        up, down, other = near()
        self.arrived(0, k)

        @pl.when(c == 0)
        def _():
            self.copy(self.dst.at[self.block(0)], self.block(0), 2, k, up).start()

        self.handon(0, k)
        self.arrived(1, k)

        @pl.when(c == 1)
        def _():
            self.copy(self.dst.at[self.block(1)], self.block(1), 2, k, down).start()

        self.handon(1, k)

    def last(self, k):
        self.arrived(2, k)
        self.handon(2, k)

    def side(self, k):
        for role in (3, 4, 5, 6):
            self.arrived(role, k)

    def finish(self):
        own = self.own()
        other = near()[2]

        def go(k, carry):
            for role in range(7):
                self.copy(self.src, own, role, k, other).wait_send()
            return carry

        lax.fori_loop(0, self.chunks, go, 0)
        if self.buf is not None:
            pltpu.make_async_copy(self.buf, self.dst.at[own], self.local.at[1]).wait()


def gather_sems(chunks):
    return [DMA((7, chunks)), DMA((7, chunks)), DMA((2,))]


def far_first(n):
    return 4 + ((n + 1) // 2) * (1 - 2 * (n % 2))


W_CHUNKS = 8
W_FIRST = 192
W_REST = 2 * HD - W_FIRST
R_CHUNKS = 4
V_CHUNKS = 4
V_ROWS = 128 // V_CHUNKS


def project_kernel(
    holder, raw, video, refine_w, w_qkv, w_out, gain, bias, scale, shift, q_gain, k_gain,
    rvid, rtxt, w_all,
    raw_all, video_all, refined, refined_all, wr, wq, normed, modded, text_rows, svid, stxt, buf,
    loads, rsend, rrecv, rlocal, fsend, frecv, flocal, isend, irecv, ilocal,
    wsend, wrecv, wlocal, vsend, vrecv, tsend, trecv,
):
    y, c, z, x = place()
    seq = z * NX + x
    f32, bf = jnp.float32, jnp.bfloat16
    other = near()[2]
    here = (x // 2 == c).astype(jnp.int32)
    peer_job = y * NC + x // 2
    text = JobGather(raw, raw_all, rsend, rrecv, rlocal, 8, 1)
    frames = JobGather(video, video_all, fsend, frecv, flocal, 128, V_CHUNKS)
    inner = JobGather(refined, refined_all, isend, irecv, ilocal, 64, 1)
    weights = JobGather(
        w_out.at[pl.ds(0, W_FIRST)], w_all, wsend, wrecv, wlocal, W_FIRST, W_CHUNKS, buf
    )
    text.load()
    frames.load()
    load_r = pltpu.make_async_copy(refine_w, wr, loads.at[0])
    load_q = [
        pltpu.make_async_copy(
            w_qkv.at[part, hl], wq.at[:, pl.ds((hl * 3 + part) * HD, HD)], loads.at[1 + 2 * part + hl]
        )
        for part in range(3)
        for hl in range(2)
    ]
    load_r.start()
    for one in load_q:
        one.start()

    def greet(n, carry):
        for hl in range(2):
            to = n * NX + 2 * c + hl

            @pl.when(jnp.logical_or(to != seq, here == 0))
            def _():
                signal(peer_job, to)

        return carry

    lax.fori_loop(0, NZ, greet, 0)
    for device in near():
        signal(*device)
    pl.semaphore_wait(pltpu.get_barrier_semaphore(), 19 - here)

    text.send_own(0)
    for k in range(2):
        frames.send_own(k)

    def refine():
        for j in range(N_JOB):
            rows = raw_all[holder[j]].astype(f32)
            normed[pl.ds(8 * j, 8)] = rms_scale(rows, gain[...])
        lifted = jnp.dot(normed[...].astype(bf), wr[...], preferred_element_type=f32)
        refined[...] = (lifted + bias[...].reshape(1, -1)).astype(bf)

    inner_own = pltpu.make_async_copy(refined, refined_all.at[inner.own()], ilocal.at[0])

    def vrows(shard, k):
        first = pl.multiple_of(shard * 128 + k * V_ROWS, V_ROWS)
        return rvid.at[:, pl.ds(first, V_ROWS), :]

    def trows(shard):
        return rtxt.at[:, pl.ds(pl.multiple_of(shard * 8, 8), 8), :]

    slot = 2 * z + x % 2

    def target(n, hl):
        zd = (z + far_first(n)) % NZ
        j = (zd + NZ - 2 * y) % NZ
        to = zd * NX + 2 * c + hl
        return 2 * j + hl, to, jnp.logical_or(to != seq, here == 0)

    def vcopy(n, hl, k):
        pair, to, away = target(n, hl)
        source = svid.at[pair, :, span(k, V_ROWS), :]
        remote = pltpu.make_async_remote_copy(
            source, vrows(seq, k), vsend.at[2 * n + hl, k], vrecv.at[slot, k],
            (peer_job, to), MESH,
        )
        return away, remote, pltpu.make_async_copy(source, vrows(seq, k), vrecv.at[slot, k])

    def tcopy(n, hl):
        pair, to, away = target(n, hl)
        remote = pltpu.make_async_remote_copy(
            stxt.at[pair], trows(seq), tsend.at[2 * n + hl], trecv.at[slot], (peer_job, to), MESH
        )
        return away, remote, pltpu.make_async_copy(stxt.at[pair], trows(seq), trecv.at[slot])

    def launch(make):
        def go(n, carry):
            for hl in range(2):
                away, remote, local = make(n, hl)

                @pl.when(away)
                def _():
                    remote.start()

                @pl.when(jnp.logical_not(away))
                def _():
                    local.start()

            return carry

        lax.fori_loop(0, NZ, go, 0)

    def drained(make):
        def go(n, carry):
            for hl in range(2):
                away, remote, _ = make(n, hl)

                @pl.when(away)
                def _():
                    remote.wait_send()

            return carry

        lax.fori_loop(0, NZ, go, 0)

    def vhand(shard, index, k):
        return pltpu.make_async_remote_copy(
            vrows(shard, k), vrows(shard, k), vsend.at[index, k], vrecv.at[index, k], other, MESH
        )

    def thand(shard, index):
        return pltpu.make_async_remote_copy(
            trows(shard), trows(shard), tsend.at[index], trecv.at[index], other, MESH
        )

    def sources(n):
        zs = (z + NZ - far_first(n)) % NZ
        return [(zs * NX + 2 * c + b, 2 * zs + b) for b in range(2)]

    def take(k):
        def go(n, carry):
            for shard, index in sources(n):
                vhand(shard, index, k).wait_recv()
                vhand(shard, index + 16, k).start()
            return carry

        lax.fori_loop(0, NZ, go, 0)

    def normalise(rows, j):
        centre = jnp.mean(rows, axis=-1, keepdims=True)
        moved = rows - centre
        spread_sq = jnp.mean(moved * moved, axis=-1, keepdims=True)
        out = moved * lax.rsqrt(spread_sq + epsilon)
        return (out * (1.0 + scale[pl.ds(j, 1), :]) + shift[pl.ds(j, 1), :]).astype(bf)

    def project(rows):
        got = jnp.dot(rows, wq[...], preferred_element_type=f32)
        out = []
        for hl in range(2):
            for part in range(3):
                piece = got[:, (hl * 3 + part) * HD : (hl * 3 + part + 1) * HD]
                if part == 0:
                    piece = rms_scale(piece, q_gain[pl.ds(hl, 1), :])
                if part == 1:
                    piece = rms_scale(piece, k_gain[pl.ds(hl, 1), :])
                out.append(piece.astype(bf))
        return out

    frames.loaded()
    frames.middle(0)
    frames.send_own(2)
    text.middle(0)
    text.loaded()

    def round_(k, carry):
        @pl.when(k + 1 < V_CHUNKS)
        def _():
            frames.middle(k + 1)

        @pl.when(k > 0)
        def _():
            launch(lambda n, hl: vcopy(n, hl, k - 1))

        @pl.when(k == 0)
        def _():
            frames.send_own(3)
            text.last(0)
            for one in load_q:
                one.wait()

        @pl.when(k == 2)
        def _():
            inner_own.start()
            inner.send_own(0)
            lax.fori_loop(0, W_CHUNKS, lambda n, _: (weights.send_own(n), _)[1], 0)

        @pl.when(k == 3)
        def _():
            inner.middle(0)
            inner.last(0)

        frames.last(k)
        frames.side(k)

        rows_k = span(k, V_ROWS)
        for j in range(N_JOB):
            modded[pl.ds(V_ROWS * j, V_ROWS)] = normalise(video_all[j, rows_k, :].astype(f32), j)
        for i, piece in enumerate(project(modded[...])):
            for j in range(N_JOB):
                svid[2 * j + i // 3, i % 3, rows_k, :] = piece[V_ROWS * j : V_ROWS * (j + 1)]

        @pl.when(k == 1)
        def _():
            text.side(0)
            load_r.wait()
            refine()

        return carry

    weights.load()
    lax.fori_loop(0, V_CHUNKS, round_, 0)

    def forward(first, end):
        lax.fori_loop(first, end, lambda n, _: (weights.middle(n), _)[1], 0)

    def last(first, end):
        lax.fori_loop(first, end, lambda n, _: (weights.last(n), _)[1], 0)

    weights.loaded()
    inner.side(0)
    inner_own.wait()
    for g in range(N_JOB):
        text_rows[:, 384 * g : 384 * (g + 1)] = refined_all[g].astype(f32)
    for j in range(N_JOB):
        normed[pl.ds(8 * j, 8), 0:3072] = normalise(text_rows[pl.ds(8 * j, 8)], j).astype(f32)
    launch(lambda n, hl: vcopy(n, hl, V_CHUNKS - 1))
    forward(0, 3)
    for i, piece in enumerate(project(normed[:, 0:3072].astype(bf))):
        for j in range(N_JOB):
            stxt[2 * j + i // 3, i % 3] = piece[8 * j : 8 * (j + 1)]
    for j in range(N_JOB):
        for group in range(4):
            at = min(group, 2) * HD
            stxt[2 * j + group // 2, 3 + group % 2] = refined[8 * j : 8 * (j + 1), at : at + HD]
    forward(3, 5)
    launch(tcopy)
    take(0)
    forward(5, 6)
    take(1)
    forward(6, 8)
    last(0, 4)
    take(2)
    last(4, 8)
    take(3)

    def text_rest(n, carry):
        for shard, index in sources(n):
            thand(shard, index).wait_recv()
            thand(shard, index + 16).start()
        return carry

    lax.fori_loop(0, NZ, text_rest, 0)

    def finish(n, carry):
        for b in range(2):
            shard = n * NX + 2 * (1 - c) + b
            index = 2 * n + b + 16
            for k in range(V_CHUNKS):
                vhand(shard, index, k).wait_recv()
                vhand(shard, index, k).wait_send()
            thand(shard, index).wait_recv()
            thand(shard, index).wait_send()
        return carry

    lax.fori_loop(0, NZ, finish, 0)
    for k in range(V_CHUNKS):
        drained(lambda n, hl: vcopy(n, hl, k))
    drained(tcopy)
    lax.fori_loop(0, W_CHUNKS, lambda k, carry: (weights.side(k), carry)[1], 0)
    for one in (text, frames, inner, weights):
        one.finish()


def project_all(holder, raw, video, refine_w, w_qkv, w_out, *small):
    f32, bf = jnp.float32, jnp.bfloat16
    vm = pl.BlockSpec(memory_space=pltpu.VMEM)
    return pl.pallas_call(
        project_kernel,
        out_shape=[
            jax.ShapeDtypeStruct((3, N_SEQ * 128, HD), bf),
            jax.ShapeDtypeStruct((5, N_SEQ * 8, HD), bf),
            jax.ShapeDtypeStruct((N_JOB, W_FIRST, w_out.shape[1]), bf),
        ],
        in_specs=[pl.BlockSpec(memory_space=pltpu.SMEM)] + [ANY] * 5 + [vm] * 6,
        out_specs=[ANY] * 3,
        scratch_shapes=[
            pltpu.VMEM((N_JOB, 8, 4096), bf),
            pltpu.VMEM((N_JOB, 128, 3072), bf),
            pltpu.VMEM((64, 384), bf),
            pltpu.VMEM((N_JOB, 64, 384), bf),
            pltpu.VMEM((4096, 384), bf),
            pltpu.VMEM((3072, 768), bf),
            pltpu.VMEM((64, 4096), f32),
            pltpu.VMEM((8 * V_ROWS, 3072), bf),
            pltpu.VMEM((64, 3072), f32),
            pltpu.VMEM((16, 3, 128, HD), bf),
            pltpu.VMEM((16, 5, 8, HD), bf),
            pltpu.VMEM((W_FIRST, w_out.shape[1]), bf),
            DMA((7,)),
            *gather_sems(1),
            *gather_sems(V_CHUNKS),
            *gather_sems(1),
            *gather_sems(W_CHUNKS),
            DMA((32, V_CHUNKS)),
            DMA((32, V_CHUNKS)),
            DMA((32,)),
            DMA((32,)),
        ],
        compiler_params=pltpu.CompilerParams(
            collective_id=5, has_side_effects=True, vmem_limit_bytes=58 << 20
        ),
        name="project_all",
    )(holder, raw, video, refine_w, w_qkv, w_out, *small)


def attend_kernel(
    counts, splits, vid, txt, w_out, rv, rt, w_all,
    q, k, tx, vext, text_out, ov, ot, loads, vsend, vrecv, tsend, trecv, buf, wsend, wrecv, wlocal,
):
    y, c, z, x = place()
    seq = z * NX + x
    mine = y * NC + c
    job = (z + NZ - 2 * y) % NZ
    head = (x % 2) * 8 + 2 * y + x // 2
    incoming = [
        pltpu.make_async_copy(vid.at[0], q, loads.at[0]),
        pltpu.make_async_copy(vid.at[1], k, loads.at[1]),
        pltpu.make_async_copy(vid.at[2], vext.at[pl.ds(0, 4096), pl.ds(0, HD)], loads.at[2]),
        pltpu.make_async_copy(txt.at[2], vext.at[pl.ds(4096, 256), pl.ds(0, HD)], loads.at[3]),
        pltpu.make_async_copy(txt, tx, loads.at[4]),
    ]
    for one in incoming:
        one.start()

    def greet(n, carry):
        for b in range(NX):
            from_job = n * NC + x // 2
            from_seq = ((mine + 2 * n) % NZ) * NX + b

            @pl.when(jnp.logical_or(from_job != mine, from_seq != seq))
            def _():
                signal(from_job, from_seq)

        return carry

    lax.fori_loop(0, NY, greet, 0)
    for device in near():
        signal(*device)
    inside = jnp.logical_and(job == mine, x // 2 == c).astype(jnp.int32)
    pl.semaphore_wait(pltpu.get_barrier_semaphore(), 19 - inside)
    weights = JobGather(
        w_out.at[pl.ds(W_FIRST, W_REST)], w_all, wsend, wrecv, wlocal, W_REST, R_CHUNKS, buf
    )
    weights.load()
    for ahead in range(R_CHUNKS):
        weights.send_own(ahead)
    weights.loaded()

    count = counts[job]
    vext[:, HD:] = jnp.ones((4352, HD), jnp.bfloat16)
    for one in incoming:
        one.wait()
    factor = (HD**-0.5) * 1.4426950408889634
    contract = (((1,), (1,)), ((), ()))

    def block(part):
        sv = lax.dot_general(part, k[...], contract, preferred_element_type=jnp.float32)
        st = lax.dot_general(part, tx[1], contract, preferred_element_type=jnp.float32)
        st = jnp.where(lax.broadcasted_iota(jnp.int32, st.shape, 1) < count, st, -1e30)
        top = jnp.maximum(
            jnp.max(sv, axis=-1, keepdims=True), jnp.max(st, axis=-1, keepdims=True)
        )
        pv = jnp.exp2((sv - top) * factor).astype(jnp.bfloat16)
        pt = jnp.exp2((st - top) * factor).astype(jnp.bfloat16)
        both = jnp.dot(pv, vext[0:4096], preferred_element_type=jnp.float32)
        both += jnp.dot(pt, vext[4096:4352], preferred_element_type=jnp.float32)
        return (both[:, 0:HD] / both[:, HD:]).astype(jnp.bfloat16)

    text_out[...] = block(tx[0])
    across = lax.broadcasted_iota(jnp.int32, (16, 256), 1)
    down = lax.broadcasted_iota(jnp.int32, (16, 256), 0)
    base = jnp.int32(0)
    picks = []
    for zs in range(NZ):
        quad = [splits[job, NX * zs + i] for i in range(NX)]
        at = base + c * (quad[0] + quad[1])
        for b in range(2):
            length = quad[b] + c * (quad[2 + b] - quad[b])
            hit = (across == at + down) & (down < length) & (across < count)
            picks.append(jnp.where(hit, 1.0, 0.0).astype(jnp.bfloat16))
            at = at + length
        base = base + quad[0] + quad[1] + quad[2] + quad[3]
    pick = jnp.concatenate(picks, axis=0)
    for part in range(3):
        rows = text_out[...] if part == 0 else tx[part + 2]
        moved = jnp.dot(pick, rows, preferred_element_type=jnp.float32).astype(jnp.bfloat16)
        ot[:, part] = moved.reshape(16, 16, HD)

    def copies(n, b):
        zd = (z + far_first(n)) % NZ
        part = 2 * zd + b
        to = zd * NX + 2 * c + b
        away = jnp.logical_or(to != seq, job != mine)
        remote = (
            pltpu.make_async_remote_copy(
                ov.at[part], rv.at[head], vsend.at[part], vrecv.at[head], (job, to), MESH
            ),
            pltpu.make_async_remote_copy(
                ot.at[part], rt.at[head], tsend.at[part], trecv.at[head], (job, to), MESH
            ),
        )
        local = (
            pltpu.make_async_copy(ov.at[part], rv.at[head], vrecv.at[head]),
            pltpu.make_async_copy(ot.at[part], rt.at[head], trecv.at[head]),
        )
        return away, remote, local

    def start(n):
        for b in range(2):
            away, remote, local = copies(n, b)

            @pl.when(away)
            def _():
                for one in remote:
                    one.start()

            @pl.when(jnp.logical_not(away))
            def _():
                for one in local:
                    one.start()

    weights.middle(0)

    def step(n, carry):
        rows = []
        for i in range(2):
            zd = (z + far_first(2 * n + i)) % NZ
            rows.append(q[pl.ds(pl.multiple_of(zd * 512 + c * 256, 256), 256), :])
        done = block(jnp.concatenate(rows, axis=0)).reshape(4, 128, HD)
        for i in range(2):
            zd = (z + far_first(2 * n + i)) % NZ
            ov[pl.ds(2 * zd, 2)] = done[2 * i : 2 * i + 2]

        @pl.when(n > 0)
        def _():
            start(2 * n - 2)
            start(2 * n - 1)

        @pl.when(n == 0)
        def _():
            weights.middle(1)
            weights.middle(2)

        @pl.when(n == 1)
        def _():
            weights.middle(3)
            weights.last(0)
            weights.last(1)

        @pl.when(n == 2)
        def _():
            weights.last(2)
            weights.last(3)

        return carry

    lax.fori_loop(0, NZ // 2, step, 0)
    start(NZ - 2)
    start(NZ - 1)

    def finish(n, carry):
        pltpu.make_async_copy(ov.at[n], rv.at[n], vrecv.at[n]).wait()
        pltpu.make_async_copy(ot.at[n], rt.at[n], trecv.at[n]).wait()
        return carry

    lax.fori_loop(0, 16, finish, 0)

    def sent(n, carry):
        for b in range(2):
            away, remote, _ = copies(n, b)

            @pl.when(away)
            def _():
                for one in remote:
                    one.wait_send()

        return carry

    lax.fori_loop(0, NZ, sent, 0)
    lax.fori_loop(0, R_CHUNKS, lambda k, carry: (weights.side(k), carry)[1], 0)
    weights.finish()


def attend(counts, splits, vid, txt, w_out):
    bf = jnp.bfloat16
    half = (W_REST, w_out.shape[1])
    return pl.pallas_call(
        attend_kernel,
        out_shape=[
            jax.ShapeDtypeStruct((16, 128, HD), bf),
            jax.ShapeDtypeStruct((16, 3, 16, HD), bf),
            jax.ShapeDtypeStruct((N_JOB, *half), bf),
        ],
        in_specs=[pl.BlockSpec(memory_space=pltpu.SMEM)] * 2 + [ANY] * 3,
        out_specs=[ANY] * 3,
        scratch_shapes=[
            pltpu.VMEM((4096, HD), bf),
            pltpu.VMEM((4096, HD), bf),
            pltpu.VMEM((5, 256, HD), bf),
            pltpu.VMEM((4352, 2 * HD), bf),
            pltpu.VMEM((256, HD), bf),
            pltpu.VMEM((16, 128, HD), bf),
            pltpu.VMEM((16, 3, 16, HD), bf),
            DMA((5,)),
            DMA((16,)),
            DMA((16,)),
            DMA((16,)),
            DMA((16,)),
            pltpu.VMEM(half, bf),
            *gather_sems(R_CHUNKS),
        ],
        compiler_params=pltpu.CompilerParams(
            collective_id=6, has_side_effects=True, vmem_limit_bytes=56 << 20
        ),
        name="attend",
    )(counts, splits, vid, txt, w_out)


def final_kernel(counts, splits, rv, rt, w_first, w_rest, video, gate, out, text_out):
    job, shard = lax.axis_index("job"), lax.axis_index("seq")
    f32, bf = jnp.float32, jnp.bfloat16
    total = None
    for g in range(N_JOB):
        rows = jnp.concatenate(
            [
                jnp.concatenate([rv[g], rv[8 + g]], axis=1),
                jnp.concatenate([rt[g, 0], rt[8 + g, 0]], axis=1),
            ],
            axis=0,
        )
        weight = jnp.concatenate([w_first[g], w_rest[g]], axis=0)
        part = jnp.dot(rows, weight, preferred_element_type=f32).astype(bf).astype(f32)
        total = part if total is None else total + part
    change = gate[pl.ds(job, 1), :] * total
    out[...] = (video[...].astype(f32) + change[:128]).astype(bf)
    kept = []
    for i in range(N_SPLIT // HD):
        group = pl.program_id(0) * (N_SPLIT // HD) + i
        g, third = group // 3, group % 3
        kept.append(rt[jnp.where(third == 2, 8 + g, g), jnp.where(third == 1, 2, 1)])
    text = (jnp.concatenate(kept, axis=1).astype(f32) + change[128:]).astype(bf)
    first = lax.fori_loop(0, shard, lambda i, sum_: sum_ + splits[job, i], jnp.int32(0))
    ids = lax.broadcasted_iota(jnp.int32, text.shape, 0)
    ok = (ids < splits[job, shard]) & (first + ids < counts[job])
    text_out[...] = jnp.where(ok, text, jnp.zeros_like(text))


N_SPLIT = 768


def final(counts, splits, rv, rt, w_first, w_rest, video, gate):
    bf = jnp.bfloat16
    smem = pl.BlockSpec(memory_space=pltpu.SMEM)
    width = video.shape[1]

    def whole(a):
        return pl.BlockSpec(a.shape, lambda n: (0,) * a.ndim)

    def cut(a):
        return pl.BlockSpec((*a.shape[:-1], N_SPLIT), lambda n: (0,) * (a.ndim - 1) + (n,))

    return pl.pallas_call(
        final_kernel,
        grid=(width // N_SPLIT,),
        out_shape=[
            jax.ShapeDtypeStruct((128, width), bf),
            jax.ShapeDtypeStruct((16, width), bf),
        ],
        in_specs=[smem, smem, whole(rv), whole(rt), cut(w_first), cut(w_rest), cut(video), cut(gate)],
        out_specs=[
            pl.BlockSpec((128, N_SPLIT), lambda n: (0, n)),
            pl.BlockSpec((16, N_SPLIT), lambda n: (0, n)),
        ],
        compiler_params=pltpu.CompilerParams(vmem_limit_bytes=60 << 20),
        name="final",
    )(counts, splits, rv, rt, w_first, w_rest, video, gate)


def body(
    video,
    text_cache,
    text_count,
    holder,
    text_splits,
    mod_shift,
    mod_scale,
    mod_gate,
    text_gain,
    refine_w,
    refine_bias,
    w_qkv,
    q_gain,
    k_gain,
    w_out,
):
    own_video = video[0]
    w_out = w_out.reshape(2 * HD, -1)
    rvid, rtxt, w_first = project_all(
        holder,
        text_cache[0],
        own_video,
        refine_w,
        jnp.transpose(w_qkv, (2, 1, 0, 3)),
        w_out,
        text_gain[None],
        refine_bias,
        mod_scale,
        mod_shift,
        q_gain,
        k_gain,
    )

    rv, rt, w_rest = attend(text_count, text_splits, rvid, rtxt, w_out)
    out, text_out = final(text_count, text_splits, rv, rt, w_first, w_rest, own_video, mod_gate)
    return out[None], text_out[None]


def solution(mesh):
    placed = (
        P("job", "seq", None),
        P("job", "seq", None),
        P(),
        P(),
        P(),
        P(),
        P(),
        P(),
        P(),
        P(None, "job"),
        P("job"),
        P(None, "job", None, None),
        P("job", None),
        P("job", None),
        P("job", None, None),
    )
    return jax.shard_map(
        body,
        mesh=mesh,
        in_specs=placed,
        out_specs=(P("job", "seq", None), P("job", "seq", None)),
        check_vma=False,
    )
```

```python
import functools

import jax
import jax.numpy as jnp
from jax import lax
from jax.experimental import pallas as pl
from jax.experimental.pallas import tpu as pltpu
from jax.sharding import PartitionSpec as P

HD = 128
NY, NC, NZ, NX = 4, 2, 8, 4
N_JOB = NY * NC
N_SEQ = NZ * NX
MESH = pl.DeviceIdType.MESH
epsilon = 1e-06
ANY = pl.BlockSpec(memory_space=pl.ANY)
DMA = pltpu.SemaphoreType.DMA


def rms_scale(values, gains):
    mean_square = jnp.mean(values * values, axis=-1, keepdims=True)
    return values * lax.rsqrt(mean_square + epsilon) * gains


def place():
    job = lax.axis_index("job")
    seq = lax.axis_index("seq")
    return job // NC, job % NC, seq // NX, seq % NX


def signal(job, seq):
    pl.semaphore_signal(
        pltpu.get_barrier_semaphore(), inc=1, device_id=(job, seq), device_id_type=MESH
    )


def near():
    y, c, z, x = place()
    seq = z * NX + x
    up = (((y + 1) % NY) * NC + c, seq)
    down = (((y + NY - 1) % NY) * NC + c, seq)
    other = (y * NC + 1 - c, seq)
    return up, down, other


def span(k, step):
    if isinstance(k, int):
        return pl.ds(k * step, step)
    return pl.ds(pl.multiple_of(k * step, step), step)


class JobGather:
    def __init__(self, src, dst, send, recv, local, rows, chunks, buf=None):
        self.src, self.dst, self.buf = src, dst, buf
        self.send, self.recv, self.local = send, recv, local
        self.step, self.chunks = rows // chunks, chunks

    def piece(self, k):
        return span(k, self.step)

    def copy(self, source, block, role, k, device):
        return pltpu.make_async_remote_copy(
            src_ref=source.at[self.piece(k)],
            dst_ref=self.dst.at[block, self.piece(k)],
            send_sem=self.send.at[role, k],
            recv_sem=self.recv.at[role, k],
            device_id=device,
            device_id_type=MESH,
        )

    def block(self, role):
        y, c, _, _ = place()
        return {
            0: ((y + NY - 1) % NY) * NC + c,
            1: ((y + 1) % NY) * NC + c,
            2: ((y + 2) % NY) * NC + c,
            3: y * NC + 1 - c,
            4: ((y + NY - 1) % NY) * NC + 1 - c,
            5: ((y + 1) % NY) * NC + 1 - c,
            6: ((y + 2) % NY) * NC + 1 - c,
        }[role]

    def own(self):
        y, c, _, _ = place()
        return y * NC + c

    def load(self):
        into = self.dst.at[self.own()] if self.buf is None else self.buf
        pltpu.make_async_copy(self.src, into, self.local.at[0]).start()

    def loaded(self):
        into = self.dst.at[self.own()] if self.buf is None else self.buf
        pltpu.make_async_copy(self.src, into, self.local.at[0]).wait()
        if self.buf is not None:
            pltpu.make_async_copy(self.buf, self.dst.at[self.own()], self.local.at[1]).start()

    def send_own(self, k):
        up, down, other = near()
        own = self.own()
        self.copy(self.src, own, 0, k, up).start()
        self.copy(self.src, own, 1, k, down).start()
        self.copy(self.src, own, 3, k, other).start()

    def arrived(self, role, k):
        block = self.block(role)
        self.copy(self.dst.at[block], block, role, k, near()[2]).wait_recv()

    def handon(self, role, k):
        block = self.block(role)
        self.copy(self.dst.at[block], block, role + 4, k, near()[2]).start()

    def middle(self, k):
        y, c, _, _ = place()
        up, down, other = near()
        self.arrived(0, k)

        @pl.when(c == 0)
        def _():
            self.copy(self.dst.at[self.block(0)], self.block(0), 2, k, up).start()

        self.handon(0, k)
        self.arrived(1, k)

        @pl.when(c == 1)
        def _():
            self.copy(self.dst.at[self.block(1)], self.block(1), 2, k, down).start()

        self.handon(1, k)

    def last(self, k):
        self.arrived(2, k)
        self.handon(2, k)

    def side(self, k):
        for role in (3, 4, 5, 6):
            self.arrived(role, k)

    def finish(self):
        own = self.own()
        other = near()[2]

        def go(k, carry):
            for role in range(7):
                self.copy(self.src, own, role, k, other).wait_send()
            return carry

        lax.fori_loop(0, self.chunks, go, 0)
        if self.buf is not None:
            pltpu.make_async_copy(self.buf, self.dst.at[own], self.local.at[1]).wait()


def gather_sems(chunks):
    return [DMA((7, chunks)), DMA((7, chunks)), DMA((2,))]


def far_first(n):
    return 4 + ((n + 1) // 2) * (1 - 2 * (n % 2))


W_CHUNKS = 8
AHEAD = 4
W_FIRST = 128
W_REST = 2 * HD - W_FIRST
R_CHUNKS = 4
V_CHUNKS = 4
V_ROWS = 128 // V_CHUNKS


def project_kernel(
    holder, raw, video, refine_w, w_qkv, w_out, gain, bias, scale, shift, q_gain, k_gain,
    rvid, rtxt, w_all,
    raw_all, video_all, refined, refined_all, wr, wq, normed, modded, text_rows, svid, stxt, buf,
    loads, rsend, rrecv, rlocal, fsend, frecv, flocal, isend, irecv, ilocal,
    wsend, wrecv, wlocal, vsend, vrecv, tsend, trecv,
):
    y, c, z, x = place()
    seq = z * NX + x
    f32, bf = jnp.float32, jnp.bfloat16
    other = near()[2]
    here = (x // 2 == c).astype(jnp.int32)
    peer_job = y * NC + x // 2
    text = JobGather(raw, raw_all, rsend, rrecv, rlocal, 8, 1)
    frames = JobGather(video, video_all, fsend, frecv, flocal, 128, V_CHUNKS)
    inner = JobGather(refined, refined_all, isend, irecv, ilocal, 64, 1)
    weights = JobGather(
        w_out.at[pl.ds(0, W_FIRST)], w_all, wsend, wrecv, wlocal, W_FIRST, W_CHUNKS, buf
    )
    text.load()
    frames.load()
    load_r = pltpu.make_async_copy(refine_w, wr, loads.at[0])
    load_q = [
        pltpu.make_async_copy(
            w_qkv.at[part, hl], wq.at[:, pl.ds((hl * 3 + part) * HD, HD)], loads.at[1 + 2 * part + hl]
        )
        for part in range(3)
        for hl in range(2)
    ]
    load_r.start()
    for one in load_q:
        one.start()

    def greet(n, carry):
        for hl in range(2):
            to = n * NX + 2 * c + hl

            @pl.when(jnp.logical_or(to != seq, here == 0))
            def _():
                signal(peer_job, to)

        return carry

    lax.fori_loop(0, NZ, greet, 0)
    for device in near():
        signal(*device)
    pl.semaphore_wait(pltpu.get_barrier_semaphore(), 19 - here)

    text.send_own(0)
    for k in range(2):
        frames.send_own(k)

    def refine():
        for j in range(N_JOB):
            rows = raw_all[holder[j]].astype(f32)
            normed[pl.ds(8 * j, 8)] = rms_scale(rows, gain[...])
        lifted = jnp.dot(normed[...].astype(bf), wr[...], preferred_element_type=f32)
        refined[...] = (lifted + bias[...].reshape(1, -1)).astype(bf)

    inner_own = pltpu.make_async_copy(refined, refined_all.at[inner.own()], ilocal.at[0])

    def vrows(shard, k):
        first = pl.multiple_of(shard * 128 + k * V_ROWS, V_ROWS)
        return rvid.at[:, pl.ds(first, V_ROWS), :]

    def trows(shard):
        return rtxt.at[:, pl.ds(pl.multiple_of(shard * 8, 8), 8), :]

    slot = 2 * z + x % 2

    def target(n, hl):
        zd = (z + far_first(n)) % NZ
        j = (zd + NZ - 2 * y) % NZ
        to = zd * NX + 2 * c + hl
        return 2 * j + hl, to, jnp.logical_or(to != seq, here == 0)

    def vcopy(n, hl, k):
        pair, to, away = target(n, hl)
        source = svid.at[pair, :, span(k, V_ROWS), :]
        remote = pltpu.make_async_remote_copy(
            source, vrows(seq, k), vsend.at[2 * n + hl, k], vrecv.at[slot, k],
            (peer_job, to), MESH,
        )
        return away, remote, pltpu.make_async_copy(source, vrows(seq, k), vrecv.at[slot, k])

    def tcopy(n, hl):
        pair, to, away = target(n, hl)
        remote = pltpu.make_async_remote_copy(
            stxt.at[pair], trows(seq), tsend.at[2 * n + hl], trecv.at[slot], (peer_job, to), MESH
        )
        return away, remote, pltpu.make_async_copy(stxt.at[pair], trows(seq), trecv.at[slot])

    def launch(make):
        def go(n, carry):
            for hl in range(2):
                away, remote, local = make(n, hl)

                @pl.when(away)
                def _():
                    remote.start()

                @pl.when(jnp.logical_not(away))
                def _():
                    local.start()

            return carry

        lax.fori_loop(0, NZ, go, 0)

    def drained(make):
        def go(n, carry):
            for hl in range(2):
                away, remote, _ = make(n, hl)

                @pl.when(away)
                def _():
                    remote.wait_send()

            return carry

        lax.fori_loop(0, NZ, go, 0)

    def vhand(shard, index, k):
        return pltpu.make_async_remote_copy(
            vrows(shard, k), vrows(shard, k), vsend.at[index, k], vrecv.at[index, k], other, MESH
        )

    def thand(shard, index):
        return pltpu.make_async_remote_copy(
            trows(shard), trows(shard), tsend.at[index], trecv.at[index], other, MESH
        )

    def sources(n):
        zs = (z + NZ - far_first(n)) % NZ
        return [(zs * NX + 2 * c + b, 2 * zs + b) for b in range(2)]

    def take(k):
        def go(n, carry):
            for shard, index in sources(n):
                vhand(shard, index, k).wait_recv()
                vhand(shard, index + 16, k).start()
            return carry

        lax.fori_loop(0, NZ, go, 0)

    def normalise(rows, j):
        centre = jnp.mean(rows, axis=-1, keepdims=True)
        moved = rows - centre
        spread_sq = jnp.mean(moved * moved, axis=-1, keepdims=True)
        out = moved * lax.rsqrt(spread_sq + epsilon)
        return (out * (1.0 + scale[pl.ds(j, 1), :]) + shift[pl.ds(j, 1), :]).astype(bf)

    def project(rows):
        got = jnp.dot(rows, wq[...], preferred_element_type=f32)
        out = []
        for hl in range(2):
            for part in range(3):
                piece = got[:, (hl * 3 + part) * HD : (hl * 3 + part + 1) * HD]
                if part == 0:
                    piece = rms_scale(piece, q_gain[pl.ds(hl, 1), :])
                if part == 1:
                    piece = rms_scale(piece, k_gain[pl.ds(hl, 1), :])
                out.append(piece.astype(bf))
        return out

    frames.loaded()
    frames.middle(0)
    frames.send_own(2)
    text.middle(0)
    text.loaded()

    def round_(k, carry):
        @pl.when(k + 1 < V_CHUNKS)
        def _():
            frames.middle(k + 1)

        @pl.when(k > 0)
        def _():
            launch(lambda n, hl: vcopy(n, hl, k - 1))

        @pl.when(k == 0)
        def _():
            frames.send_own(3)
            text.last(0)
            for one in load_q:
                one.wait()

        @pl.when(k == 2)
        def _():
            inner_own.start()
            inner.send_own(0)
            for ahead in range(AHEAD):
                weights.send_own(ahead)

        @pl.when(k == 3)
        def _():
            inner.middle(0)
            inner.last(0)

        frames.last(k)
        frames.side(k)

        rows_k = span(k, V_ROWS)
        for j in range(N_JOB):
            modded[pl.ds(V_ROWS * j, V_ROWS)] = normalise(video_all[j, rows_k, :].astype(f32), j)
        for i, piece in enumerate(project(modded[...])):
            for j in range(N_JOB):
                svid[2 * j + i // 3, i % 3, rows_k, :] = piece[V_ROWS * j : V_ROWS * (j + 1)]

        @pl.when(k == 1)
        def _():
            text.side(0)
            load_r.wait()
            refine()

        return carry

    weights.load()
    lax.fori_loop(0, V_CHUNKS, round_, 0)

    def forward(n):
        weights.middle(n)
        if n + AHEAD < W_CHUNKS:
            weights.send_own(n + AHEAD)

    weights.loaded()
    forward(0)
    launch(lambda n, hl: vcopy(n, hl, V_CHUNKS - 1))
    inner.side(0)
    inner_own.wait()
    for g in range(N_JOB):
        text_rows[:, 384 * g : 384 * (g + 1)] = refined_all[g].astype(f32)
    for j in range(N_JOB):
        normed[pl.ds(8 * j, 8), 0:3072] = normalise(text_rows[pl.ds(8 * j, 8)], j).astype(f32)
    for i, piece in enumerate(project(normed[:, 0:3072].astype(bf))):
        for j in range(N_JOB):
            stxt[2 * j + i // 3, i % 3] = piece[8 * j : 8 * (j + 1)]
    for j in range(N_JOB):
        for group in range(4):
            at = min(group, 2) * HD
            stxt[2 * j + group // 2, 3 + group % 2] = refined[8 * j : 8 * (j + 1), at : at + HD]
    forward(1)
    take(0)
    launch(tcopy)
    forward(2)
    weights.last(0)
    forward(3)
    weights.last(1)
    take(1)
    forward(4)
    weights.last(2)
    forward(5)
    weights.last(3)
    take(2)
    forward(6)
    weights.last(4)
    forward(7)
    weights.last(5)
    weights.last(6)
    take(3)
    weights.last(7)

    def text_rest(n, carry):
        for shard, index in sources(n):
            thand(shard, index).wait_recv()
            thand(shard, index + 16).start()
        return carry

    lax.fori_loop(0, NZ, text_rest, 0)

    def finish(n, carry):
        for b in range(2):
            shard = n * NX + 2 * (1 - c) + b
            index = 2 * n + b + 16
            for k in range(V_CHUNKS):
                vhand(shard, index, k).wait_recv()
                vhand(shard, index, k).wait_send()
            thand(shard, index).wait_recv()
            thand(shard, index).wait_send()
        return carry

    lax.fori_loop(0, NZ, finish, 0)
    for k in range(V_CHUNKS):
        drained(lambda n, hl: vcopy(n, hl, k))
    drained(tcopy)
    lax.fori_loop(0, W_CHUNKS, lambda k, carry: (weights.side(k), carry)[1], 0)
    for one in (text, frames, inner, weights):
        one.finish()


def project_all(holder, raw, video, refine_w, w_qkv, w_out, *small):
    f32, bf = jnp.float32, jnp.bfloat16
    vm = pl.BlockSpec(memory_space=pltpu.VMEM)
    return pl.pallas_call(
        project_kernel,
        out_shape=[
            jax.ShapeDtypeStruct((3, N_SEQ * 128, HD), bf),
            jax.ShapeDtypeStruct((5, N_SEQ * 8, HD), bf),
            jax.ShapeDtypeStruct((N_JOB, W_FIRST, w_out.shape[1]), bf),
        ],
        in_specs=[pl.BlockSpec(memory_space=pltpu.SMEM)] + [ANY] * 5 + [vm] * 6,
        out_specs=[ANY] * 3,
        scratch_shapes=[
            pltpu.VMEM((N_JOB, 8, 4096), bf),
            pltpu.VMEM((N_JOB, 128, 3072), bf),
            pltpu.VMEM((64, 384), bf),
            pltpu.VMEM((N_JOB, 64, 384), bf),
            pltpu.VMEM((4096, 384), bf),
            pltpu.VMEM((3072, 768), bf),
            pltpu.VMEM((64, 4096), f32),
            pltpu.VMEM((8 * V_ROWS, 3072), bf),
            pltpu.VMEM((64, 3072), f32),
            pltpu.VMEM((16, 3, 128, HD), bf),
            pltpu.VMEM((16, 5, 8, HD), bf),
            pltpu.VMEM((W_FIRST, w_out.shape[1]), bf),
            DMA((7,)),
            *gather_sems(1),
            *gather_sems(V_CHUNKS),
            *gather_sems(1),
            *gather_sems(W_CHUNKS),
            DMA((32, V_CHUNKS)),
            DMA((32, V_CHUNKS)),
            DMA((32,)),
            DMA((32,)),
        ],
        compiler_params=pltpu.CompilerParams(
            collective_id=5, has_side_effects=True, vmem_limit_bytes=58 << 20
        ),
        name="project_all",
    )(holder, raw, video, refine_w, w_qkv, w_out, *small)


def attend_kernel(
    counts, splits, vid, txt, w_out, rv, rt, w_all,
    q, k, tx, vext, text_out, ov, ot, loads, vsend, vrecv, tsend, trecv, buf, wsend, wrecv, wlocal,
):
    y, c, z, x = place()
    seq = z * NX + x
    mine = y * NC + c
    job = (z + NZ - 2 * y) % NZ
    head = (x % 2) * 8 + 2 * y + x // 2
    incoming = [
        pltpu.make_async_copy(vid.at[0], q, loads.at[0]),
        pltpu.make_async_copy(vid.at[1], k, loads.at[1]),
        pltpu.make_async_copy(vid.at[2], vext.at[pl.ds(0, 4096), pl.ds(0, HD)], loads.at[2]),
        pltpu.make_async_copy(txt.at[2], vext.at[pl.ds(4096, 256), pl.ds(0, HD)], loads.at[3]),
        pltpu.make_async_copy(txt, tx, loads.at[4]),
    ]
    for one in incoming:
        one.start()

    def greet(n, carry):
        for b in range(NX):
            from_job = n * NC + x // 2
            from_seq = ((mine + 2 * n) % NZ) * NX + b

            @pl.when(jnp.logical_or(from_job != mine, from_seq != seq))
            def _():
                signal(from_job, from_seq)

        return carry

    lax.fori_loop(0, NY, greet, 0)
    for device in near():
        signal(*device)
    inside = jnp.logical_and(job == mine, x // 2 == c).astype(jnp.int32)
    pl.semaphore_wait(pltpu.get_barrier_semaphore(), 19 - inside)
    weights = JobGather(
        w_out.at[pl.ds(W_FIRST, W_REST)], w_all, wsend, wrecv, wlocal, W_REST, R_CHUNKS, buf
    )
    weights.load()
    for ahead in range(R_CHUNKS):
        weights.send_own(ahead)
    weights.loaded()

    count = counts[job]
    vext[:, HD:] = jnp.ones((4352, HD), jnp.bfloat16)
    for one in incoming:
        one.wait()
    factor = (HD**-0.5) * 1.4426950408889634
    contract = (((1,), (1,)), ((), ()))

    def block(part):
        sv = lax.dot_general(part, k[...], contract, preferred_element_type=jnp.float32)
        st = lax.dot_general(part, tx[1], contract, preferred_element_type=jnp.float32)
        st = jnp.where(lax.broadcasted_iota(jnp.int32, st.shape, 1) < count, st, -1e30)
        top = jnp.maximum(
            jnp.max(sv, axis=-1, keepdims=True), jnp.max(st, axis=-1, keepdims=True)
        )
        pv = jnp.exp2((sv - top) * factor).astype(jnp.bfloat16)
        pt = jnp.exp2((st - top) * factor).astype(jnp.bfloat16)
        both = jnp.dot(pv, vext[0:4096], preferred_element_type=jnp.float32)
        both += jnp.dot(pt, vext[4096:4352], preferred_element_type=jnp.float32)
        return (both[:, 0:HD] / both[:, HD:]).astype(jnp.bfloat16)

    text_out[...] = block(tx[0])
    across = lax.broadcasted_iota(jnp.int32, (16, 256), 1)
    down = lax.broadcasted_iota(jnp.int32, (16, 256), 0)
    base = jnp.int32(0)
    picks = []
    for zs in range(NZ):
        quad = [splits[job, NX * zs + i] for i in range(NX)]
        at = base + c * (quad[0] + quad[1])
        for b in range(2):
            length = quad[b] + c * (quad[2 + b] - quad[b])
            hit = (across == at + down) & (down < length) & (across < count)
            picks.append(jnp.where(hit, 1.0, 0.0).astype(jnp.bfloat16))
            at = at + length
        base = base + quad[0] + quad[1] + quad[2] + quad[3]
    pick = jnp.concatenate(picks, axis=0)
    for part in range(3):
        rows = text_out[...] if part == 0 else tx[part + 2]
        moved = jnp.dot(pick, rows, preferred_element_type=jnp.float32).astype(jnp.bfloat16)
        ot[:, part] = moved.reshape(16, 16, HD)

    def copies(n, b):
        zd = (z + far_first(n)) % NZ
        part = 2 * zd + b
        to = zd * NX + 2 * c + b
        away = jnp.logical_or(to != seq, job != mine)
        remote = (
            pltpu.make_async_remote_copy(
                ov.at[part], rv.at[head], vsend.at[part], vrecv.at[head], (job, to), MESH
            ),
            pltpu.make_async_remote_copy(
                ot.at[part], rt.at[head], tsend.at[part], trecv.at[head], (job, to), MESH
            ),
        )
        local = (
            pltpu.make_async_copy(ov.at[part], rv.at[head], vrecv.at[head]),
            pltpu.make_async_copy(ot.at[part], rt.at[head], trecv.at[head]),
        )
        return away, remote, local

    def start(n):
        for b in range(2):
            away, remote, local = copies(n, b)

            @pl.when(away)
            def _():
                for one in remote:
                    one.start()

            @pl.when(jnp.logical_not(away))
            def _():
                for one in local:
                    one.start()

    weights.middle(0)

    def step(n, carry):
        rows = []
        for i in range(2):
            zd = (z + far_first(2 * n + i)) % NZ
            rows.append(q[pl.ds(pl.multiple_of(zd * 512 + c * 256, 256), 256), :])
        done = block(jnp.concatenate(rows, axis=0)).reshape(4, 128, HD)
        for i in range(2):
            zd = (z + far_first(2 * n + i)) % NZ
            ov[pl.ds(2 * zd, 2)] = done[2 * i : 2 * i + 2]

        @pl.when(n > 0)
        def _():
            start(2 * n - 2)
            start(2 * n - 1)

        @pl.when(n == 0)
        def _():
            weights.middle(1)

        @pl.when(n == 1)
        def _():
            weights.middle(2)
            weights.middle(3)

        @pl.when(n == 2)
        def _():
            weights.last(0)
            weights.last(1)

        @pl.when(n == 3)
        def _():
            weights.last(2)
            weights.last(3)

        return carry

    lax.fori_loop(0, NZ // 2, step, 0)
    start(NZ - 2)
    start(NZ - 1)

    def finish(n, carry):
        pltpu.make_async_copy(ov.at[n], rv.at[n], vrecv.at[n]).wait()
        pltpu.make_async_copy(ot.at[n], rt.at[n], trecv.at[n]).wait()
        return carry

    lax.fori_loop(0, 16, finish, 0)

    def sent(n, carry):
        for b in range(2):
            away, remote, _ = copies(n, b)

            @pl.when(away)
            def _():
                for one in remote:
                    one.wait_send()

        return carry

    lax.fori_loop(0, NZ, sent, 0)
    lax.fori_loop(0, R_CHUNKS, lambda k, carry: (weights.side(k), carry)[1], 0)
    weights.finish()


def attend(counts, splits, vid, txt, w_out):
    bf = jnp.bfloat16
    half = (W_REST, w_out.shape[1])
    return pl.pallas_call(
        attend_kernel,
        out_shape=[
            jax.ShapeDtypeStruct((16, 128, HD), bf),
            jax.ShapeDtypeStruct((16, 3, 16, HD), bf),
            jax.ShapeDtypeStruct((N_JOB, *half), bf),
        ],
        in_specs=[pl.BlockSpec(memory_space=pltpu.SMEM)] * 2 + [ANY] * 3,
        out_specs=[ANY] * 3,
        scratch_shapes=[
            pltpu.VMEM((4096, HD), bf),
            pltpu.VMEM((4096, HD), bf),
            pltpu.VMEM((5, 256, HD), bf),
            pltpu.VMEM((4352, 2 * HD), bf),
            pltpu.VMEM((256, HD), bf),
            pltpu.VMEM((16, 128, HD), bf),
            pltpu.VMEM((16, 3, 16, HD), bf),
            DMA((5,)),
            DMA((16,)),
            DMA((16,)),
            DMA((16,)),
            DMA((16,)),
            pltpu.VMEM(half, bf),
            *gather_sems(R_CHUNKS),
        ],
        compiler_params=pltpu.CompilerParams(
            collective_id=6, has_side_effects=True, vmem_limit_bytes=56 << 20
        ),
        name="attend",
    )(counts, splits, vid, txt, w_out)


def final_kernel(counts, splits, rv, rt, w_first, w_rest, video, gate, out, text_out):
    job, shard = lax.axis_index("job"), lax.axis_index("seq")
    f32, bf = jnp.float32, jnp.bfloat16
    total = None
    for g in range(N_JOB):
        rows = jnp.concatenate(
            [
                jnp.concatenate([rv[g], rv[8 + g]], axis=1),
                jnp.concatenate([rt[g, 0], rt[8 + g, 0]], axis=1),
            ],
            axis=0,
        )
        weight = jnp.concatenate([w_first[g], w_rest[g]], axis=0)
        part = jnp.dot(rows, weight, preferred_element_type=f32).astype(bf).astype(f32)
        total = part if total is None else total + part
    change = gate[pl.ds(job, 1), :] * total
    out[...] = (video[...].astype(f32) + change[:128]).astype(bf)
    kept = []
    for i in range(N_SPLIT // HD):
        group = pl.program_id(0) * (N_SPLIT // HD) + i
        g, third = group // 3, group % 3
        kept.append(rt[jnp.where(third == 2, 8 + g, g), jnp.where(third == 1, 2, 1)])
    text = (jnp.concatenate(kept, axis=1).astype(f32) + change[128:]).astype(bf)
    first = lax.fori_loop(0, shard, lambda i, sum_: sum_ + splits[job, i], jnp.int32(0))
    ids = lax.broadcasted_iota(jnp.int32, text.shape, 0)
    ok = (ids < splits[job, shard]) & (first + ids < counts[job])
    text_out[...] = jnp.where(ok, text, jnp.zeros_like(text))


N_SPLIT = 768


def final(counts, splits, rv, rt, w_first, w_rest, video, gate):
    bf = jnp.bfloat16
    smem = pl.BlockSpec(memory_space=pltpu.SMEM)
    width = video.shape[1]

    def whole(a):
        return pl.BlockSpec(a.shape, lambda n: (0,) * a.ndim)

    def cut(a):
        return pl.BlockSpec((*a.shape[:-1], N_SPLIT), lambda n: (0,) * (a.ndim - 1) + (n,))

    return pl.pallas_call(
        final_kernel,
        grid=(width // N_SPLIT,),
        out_shape=[
            jax.ShapeDtypeStruct((128, width), bf),
            jax.ShapeDtypeStruct((16, width), bf),
        ],
        in_specs=[smem, smem, whole(rv), whole(rt), cut(w_first), cut(w_rest), cut(video), cut(gate)],
        out_specs=[
            pl.BlockSpec((128, N_SPLIT), lambda n: (0, n)),
            pl.BlockSpec((16, N_SPLIT), lambda n: (0, n)),
        ],
        compiler_params=pltpu.CompilerParams(vmem_limit_bytes=60 << 20),
        name="final",
    )(counts, splits, rv, rt, w_first, w_rest, video, gate)


def body(
    video,
    text_cache,
    text_count,
    holder,
    text_splits,
    mod_shift,
    mod_scale,
    mod_gate,
    text_gain,
    refine_w,
    refine_bias,
    w_qkv,
    q_gain,
    k_gain,
    w_out,
):
    own_video = video[0]
    w_out = w_out.reshape(2 * HD, -1)
    rvid, rtxt, w_first = project_all(
        holder,
        text_cache[0],
        own_video,
        refine_w,
        jnp.transpose(w_qkv, (2, 1, 0, 3)),
        w_out,
        text_gain[None],
        refine_bias,
        mod_scale,
        mod_shift,
        q_gain,
        k_gain,
    )

    rv, rt, w_rest = attend(text_count, text_splits, rvid, rtxt, w_out)
    out, text_out = final(text_count, text_splits, rv, rt, w_first, w_rest, own_video, mod_gate)
    return out[None], text_out[None]


def solution(mesh):
    placed = (
        P("job", "seq", None),
        P("job", "seq", None),
        P(),
        P(),
        P(),
        P(),
        P(),
        P(),
        P(),
        P(None, "job"),
        P("job"),
        P(None, "job", None, None),
        P("job", None),
        P("job", None),
        P("job", None, None),
    )
    return jax.shard_map(
        body,
        mesh=mesh,
        in_specs=placed,
        out_specs=(P("job", "seq", None), P("job", "seq", None)),
        check_vma=False,
    )
```
